32 devices in a mesh: groups: 2 (over y), strip: 4 (over z), sub: 2 (over x), rep: 2 (over core).
Axes of the slice: x: 2, y: 2, z: 4, core: 2. Of those that a mesh axis runs over, the one named last changes fastest.
Arguments:
- source: bfloat16 [32, 16, 128, 128], P(('groups', 'strip'), 'sub', 'rep'), parts along dimension 0, may hold values from -6 to 6
- target: bfloat16 [32, 16, 128, 128], P(('groups', 'strip'), 'sub', 'rep'), parts along dimension 0, may hold values from -6 to 6
- target_ids: int32 [32, 16, 25], P(('groups', 'strip'), 'sub'), parts along dimension 0, may hold values from 0 to 255, as said below
- out_grad: bfloat16 [32, 16, 25, 128], P(('groups', 'strip'), 'sub'), parts along dimension 0, may hold values from -6 to 6
- w_in: bfloat16 [128, 256], replicated, may hold values from -0.5 to 0.5
- b_in: float32 [256], replicated, may hold values from -4 to 4
- w_out: bfloat16 [256, 128], replicated, may hold values from -0.375 to 0.375
Outputs:
- source_grad: bfloat16 [32, 16, 128, 128], P(('groups', 'strip'), 'sub', 'rep'), parts along dimension 0
- target_grad: bfloat16 [32, 16, 128, 128], P(('groups', 'strip'), 'sub', 'rep'), parts along dimension 0
The draws below stay inside these ranges and needn't reach their ends.
There are 2 independent parts, one for each index of `groups`. The reference program is written for one: setup_inputs(seed, part) draws one part's arguments, and reference() takes and returns one part's arrays. A program takes and returns all parts, laid end to end along the dimension named above; an argument that names none is the same for every part. Nothing has to cross between parts.
Inputs may be any that keep to these rules, and one draw needn't show every extreme that they name: `target_ids`: the targets of source block (i, j) lie within 3 block rows and 3 block columns of it and inside the section; they come in no particular order and may repeat.
All inputs are finite; a program needn't handle non-finite values.
Results may differ from the reference program's by a relative error of at most 0.007.
Values may be sent and summed in bfloat16 or wider, within the bound.
No kernel may reach another device: no remote copies, remote signals or barrier semaphores. Data moves between devices by JAX's collectives and lax.ppermute only.
A program may use at most 64 MiB of HBM per device.

```python
import math
import jax
import jax.numpy as jnp
from jax import lax

C = 128
P_SIZE = 128
HID = 256
K = 25
H = 3
NBR = 16
NBC = 16


def draw_target_ids(key, part):
    row_key = jax.random.fold_in(key, 11)
    col_key = jax.random.fold_in(key, 12)
    row_move = jax.random.randint(row_key, (NBR, NBC, K), -H, H + 1)
    col_move = jax.random.randint(col_key, (NBR, NBC, K), -H, H + 1)
    row_at = jnp.arange(NBR, dtype=jnp.int32)[:, None, None]
    col_at = jnp.arange(NBC, dtype=jnp.int32)[None, :, None]
    target_row = jnp.clip(row_at + row_move, 0, NBR - 1)
    target_col = jnp.clip(col_at + col_move, 0, NBC - 1)
    return (target_row * NBC + target_col).astype(jnp.int32)


def level_of(rng, dims, cuts, smallest, top_value):
    def one(dim, shards_of):
        draws = jax.random.uniform(jax.random.fold_in(jax.random.fold_in(rng, 6), dim), (shards_of,), jnp.float32, smallest / len(cuts), top_value / len(cuts))
        return jnp.repeat(jnp.exp(draws), dims[dim] // shards_of).reshape((-1,) + (1,) * (len(dims) - dim - 1))

    gain = one(*cuts[0])
    for cut in cuts[1:]:
        gain = gain * one(*cut)
    return gain


def centred(key, extent, deviation, reach, pieces=(), kind=jnp.bfloat16):
    level = level_of(key, extent, pieces, -0.22, 0.18) if pieces else 1.0
    array = jax.random.normal(key, extent, jnp.float32) * deviation * level
    return jnp.minimum(jnp.maximum(array, -reach), reach).astype(kind)


def setup_inputs(seed: int = 0, part: int = 0) -> dict:
    splits = jax.random.split(jax.random.key(seed), 8)
    part_keys = jax.random.split(jax.random.fold_in(splits[7], part), 8)
    source = centred(part_keys[0], (NBR, NBC, P_SIZE, C), 1.0, 6.0, ((0, 4), (1, 2), (2, 2)))
    target = centred(part_keys[1], (NBR, NBC, P_SIZE, C), 1.0, 6.0, ((0, 4), (1, 2), (2, 2)))
    target_ids = draw_target_ids(jax.random.fold_in(jax.random.fold_in(splits[7], part), 71), part)
    out_grad = centred(part_keys[3], (NBR, NBC, K, P_SIZE), 1.0, 6.0, ((0, 4), (1, 2)))
    w_in = centred(splits[4], (P_SIZE, HID), P_SIZE ** -0.5, 0.5)
    b_in = centred(splits[5], (HID,), 1.0, 4.0, (), jnp.float32)
    w_out = centred(splits[6], (HID, P_SIZE), HID ** -0.5, 0.375)
    return {"source": source, "target": target, "target_ids": target_ids, "out_grad": out_grad, "w_in": w_in, "b_in": b_in, "w_out": w_out}


def gelu_tanh(values):
    return jax.nn.gelu(values, approximate=True)

def reference(source, target, target_ids, out_grad, w_in, b_in, w_out):
    inv_root = 1.0 / math.sqrt(C)
    flat_target = target.reshape(NBR * NBC, P_SIZE, C)

    def row_costs(items):
        src_row, id_row = items
        chosen = flat_target[id_row.astype(jnp.int32)]
        total = jnp.einsum('jpc,jkpc->jkp', src_row.astype(jnp.float32), chosen.astype(jnp.float32))
        return (total * inv_root).astype(jnp.bfloat16)
    costs = lax.map(row_costs, (source, target_ids))
    cost_rows = costs.reshape(-1, P_SIZE)
    hidden_pre = jnp.dot(cost_rows, w_in, preferred_element_type=jnp.float32) + b_in.astype(jnp.float32)
    grad_hidden = lax.dot_general(out_grad.reshape(-1, P_SIZE), w_out, (((1,), (1,)), ((), ())), preferred_element_type=jnp.float32)
    _, pullback = jax.vjp(gelu_tanh, hidden_pre)
    grad_pre = pullback(grad_hidden)[0].astype(jnp.bfloat16)
    grad_cost = lax.dot_general(grad_pre, w_in, (((1,), (1,)), ((), ())), preferred_element_type=jnp.float32)
    grad_cost = grad_cost.astype(jnp.bfloat16).reshape(NBR, NBC, K, P_SIZE)
    same_id = target_ids[..., :, None] == target_ids[..., None, :]
    merged = jnp.einsum('ijkl,ijlp->ijkp', same_id.astype(jnp.float32), grad_cost.astype(jnp.float32)).astype(jnp.bfloat16)
    earlier = jnp.arange(K)[None, :] < jnp.arange(K)[:, None]
    first = jnp.logical_not(jnp.any(same_id & earlier, axis=-1))
    weights = merged.astype(jnp.float32) * first[..., None].astype(jnp.float32)

    def row_grads(accum, items):
        src_row, id_row, wgt_row = items
        chosen = flat_target[id_row.astype(jnp.int32)].astype(jnp.float32)
        src_grad = (jnp.einsum('jkp,jkpc->jpc', wgt_row, chosen) * inv_root).astype(jnp.bfloat16)
        contrib = wgt_row[..., None] * src_row.astype(jnp.float32)[:, None]
        accum = accum.at[id_row.reshape(-1).astype(jnp.int32)].add(contrib.reshape(-1, P_SIZE, C))
        return (accum, src_grad)
    accum_start = jnp.zeros((NBR * NBC, P_SIZE, C), jnp.float32)
    accum, source_grad = lax.scan(row_grads, accum_start, (source, target_ids, weights))
    target_grad = (accum * inv_root).astype(jnp.bfloat16).reshape(NBR, NBC, P_SIZE, C)
    return (source_grad, target_grad)
```

```python
from functools import partial
import math

import jax
import jax.numpy as jnp
from jax import lax
from jax.experimental import pallas as pl
from jax.experimental.pallas import tpu as pltpu
from jax.sharding import PartitionSpec as P

H = 3
LANES = 128
NT = (((1,), (1,)), ((), ()))
TN = (((0,), (0,)), ((), ()))
F32 = jnp.float32
BF16 = jnp.bfloat16


def mate(i, q, n):
    j = i + 1 if (i + q) % 2 == 0 else i - 1
    return j if 0 <= j < n else None


def turns(n):
    return [q for q in (0, 1) if any(mate(i, q, n) is not None for i in range(n))]


def swap(x, qz, qx):
    strips, subs = lax.axis_size("strip"), lax.axis_size("sub")
    pairs = []
    for s in range(strips):
        for u in range(subs):
            t = s if qz is None else mate(s, qz, strips)
            v = u if qx is None else mate(u, qx, subs)
            if t is not None and v is not None:
                pairs.append((s * subs + u, t * subs + v))
    return lax.ppermute(x, ("strip", "sub"), pairs)


def plan(rows, cols):
    zs, xs = turns(lax.axis_size("strip")), turns(lax.axis_size("sub"))
    pieces = [(q, None) for q in zs]
    pieces += [(q, r) for q in zs for r in xs]
    pieces += [(None, r) for r in xs]
    base, at = {(None, None): 0}, rows * cols
    for qz, qx in pieces:
        base[qz, qx] = at
        at += (rows if qz is None else H) * (cols if qx is None else H)
    return pieces, base, at


def facing(q, extent, index):
    return jnp.where((index + q) % 2 == 0, extent - H, 0)


def places(target_ids, base, rows, cols):
    total_cols = cols * lax.axis_size("sub")
    strip_at, sub_at = lax.axis_index("strip"), lax.axis_index("sub")

    def split(d, extent, index):
        side = jnp.where(d < 0, -1, jnp.where(d >= extent, 1, 0))
        inner = jnp.where(side < 0, d + H, jnp.where(side > 0, d - extent, d))
        ahead = jnp.where(index % 2 == 0, 1, -1)
        turn = jnp.where(side == 0, -1, jnp.where(side == ahead, 0, 1))
        return turn, inner

    tz, dr = split(target_ids // total_cols - strip_at * rows, rows, strip_at)
    tx, dc = split(target_ids % total_cols - sub_at * cols, cols, sub_at)
    where_to = jnp.full(target_ids.shape, -1, jnp.int32)
    for (qz, qx), start in base.items():
        here = (tz == (-1 if qz is None else qz)) & (tx == (-1 if qx is None else qx))
        width = cols if qx is None else H
        where_to = jnp.where(here, start + dr * width + dc, where_to)
    return where_to


def widen(dst, at, src_ref, px):
    count = src_ref.shape[0] // px

    def body(i, _):
        dst[pl.ds((at + i) * px, px), :] = src_ref[pl.ds(i * px, px), :].astype(F32)
        return 0

    lax.fori_loop(0, count, body, 0)


def one_hot(x_ref, b, slots, tile):
    group, j = divmod(b, LANES // slots)
    lane = lax.broadcasted_iota(jnp.int32, (1, LANES), 1) // slots
    row = jnp.where(lane == j, x_ref[group : group + 1, :], -1)
    e = lax.broadcasted_iota(jnp.int32, (LANES, LANES), 0) + tile * LANES
    return (e == row).astype(F32).astype(BF16)


def corr_kernel(px, n, ext, starts, slots, *refs):
    k = len(starts)
    src_ref, tgt_refs, x_ref = refs[0], refs[1 : 1 + k], refs[1 + k]
    costs_ref, tgt_t, src_t, s32, t32, corr = refs[2 + k :]
    ext_pad = tgt_t.shape[1]
    channels = src_ref.shape[1]
    inv_root = 1.0 / math.sqrt(channels)
    widen(s32, 0, src_ref, px)
    for start, ref in zip(starts, tgt_refs):
        widen(t32, start, ref, px)

    def clear(i, _):
        t32[pl.ds(i * px, px), :] = jnp.zeros((px, channels), F32)
        return 0

    lax.fori_loop(ext, ext_pad, clear, 0)

    def per_pixel(p, _):
        sp = s32[pl.ds(p, n, stride=px), :].astype(BF16)
        tp = t32[pl.ds(p, ext_pad, stride=px), :].astype(BF16)
        src_t[p] = sp
        tgt_t[p] = tp
        c = lax.dot_general(sp, tp, NT, preferred_element_type=F32) * inv_root
        for t in range(ext_pad // LANES):
            corr[t, pl.ds(p, n, stride=px), :] = c[:, t * LANES : (t + 1) * LANES]
        return 0

    lax.fori_loop(0, px, per_pixel, 0, unroll=4)
    per = LANES // slots
    for g in range(n // per):
        acc = jnp.zeros((px, LANES), F32)
        for j in range(per):
            b = g * per + j
            for t in range(ext_pad // LANES):
                acc += jnp.dot(
                    corr[t, b * px : (b + 1) * px, :].astype(BF16),
                    one_hot(x_ref, b, slots, t),
                    preferred_element_type=F32,
                )
        costs_ref[:, g * LANES : (g + 1) * LANES] = acc.astype(BF16)


def hidden_kernel(og_ref, w_out_ref, gh_ref):
    gh_ref[...] = lax.dot_general(
        w_out_ref[...], og_ref[...], NT, preferred_element_type=F32
    )


def gelu_slope(x):
    c = math.sqrt(2.0 / math.pi)
    x2 = x * x
    th = jnp.tanh(c * (x + 0.044715 * (x2 * x)))
    inner = c * (1.0 + (3.0 * 0.044715) * x2)
    return 0.5 * (1.0 + th) + (0.5 * x) * ((1.0 - th) * (1.0 + th)) * inner


def decoder_kernel(rep_ref, mine_ref, other_ref, gh_ref, wt_ref, b_ref, w_ref, gc_ref, whole):
    px = mine_ref.shape[0]
    rep = rep_ref[0]
    whole[pl.ds(pl.multiple_of(rep * px, px), px), :] = mine_ref[...]
    whole[pl.ds(pl.multiple_of((1 - rep) * px, px), px), :] = other_ref[...]
    w_half = w_ref[pl.ds(pl.multiple_of(rep * px, px), px), :]
    width = 2 * LANES
    for g in range(mine_ref.shape[1] // width):
        cut = slice(g * width, (g + 1) * width)
        pre = jnp.dot(wt_ref[...], whole[:, cut], preferred_element_type=F32) + b_ref[...]
        grad = (gh_ref[:, cut] * gelu_slope(pre)).astype(BF16)
        gc_ref[:, cut] = jnp.dot(w_half, grad, preferred_element_type=F32).astype(BF16)


def grads_kernel(px, n, starts, counts, slots, gc_ref, x_ref, tgt_t, src_t, *refs):
    k = len(starts)
    sg_ref, own_ref, part_refs = refs[0], refs[1], refs[2 : 1 + k]
    pw, s32, part = refs[1 + k :]
    ext_pad = tgt_t.shape[1]
    inv_root = 1.0 / math.sqrt(tgt_t.shape[2])
    tiles = ext_pad // LANES
    per = LANES // slots
    for b in range(n):
        g = b // per
        gc = gc_ref[:, g * LANES : (g + 1) * LANES]
        for t in range(tiles):
            pw[t, b * px : (b + 1) * px, :] = lax.dot_general(
                gc, one_hot(x_ref, b, slots, t), NT, preferred_element_type=F32
            )

    def per_pixel(p, _):
        tp, sp = tgt_t[p], src_t[p]
        sg = jnp.zeros((n, tp.shape[1]), F32)
        for t in range(tiles):
            w = pw[t, pl.ds(p, n, stride=px), :].astype(BF16)
            sg += jnp.dot(
                w, tp[t * LANES : (t + 1) * LANES, :], preferred_element_type=F32
            )
            part[pl.ds(t * LANES * px + p, LANES, stride=px), :] = lax.dot_general(
                w, sp, TN, preferred_element_type=F32
            )
        s32[pl.ds(p, n, stride=px), :] = sg * inv_root
        return 0

    lax.fori_loop(0, px, per_pixel, 0, unroll=4)

    def narrow(dst, src, at, count):
        def body(i, _):
            dst[pl.ds(i * px, px), :] = src[pl.ds((at + i) * px, px), :].astype(dst.dtype)
            return 0

        lax.fori_loop(0, count, body, 0)

    narrow(sg_ref, s32, 0, n)
    for start, count, ref in zip(starts, counts, (own_ref, *part_refs)):
        narrow(ref, part, start, count)


def total_kernel(px, rows, cols, pieces, off_ref, own_ref, *refs):
    parts, tg_ref, acc = refs[: len(pieces)], refs[-2], refs[-1]
    inv_root = 1.0 / math.sqrt(own_ref.shape[1])
    n = rows * cols

    def load(i, _):
        acc[pl.ds(i * px, px), :] = own_ref[pl.ds(i * px, px), :]
        return 0

    lax.fori_loop(0, n, load, 0)
    for (qz, qx), ref in zip(pieces, parts):
        r0 = 0 if qz is None else off_ref[qz]
        c0 = 0 if qx is None else off_ref[2 + qx]
        high = rows if qz is None else H
        wide = cols if qx is None else H

        def add(r, _, r0=r0, c0=c0, wide=wide, ref=ref):
            for c in range(wide):
                at = pl.ds(pl.multiple_of(((r0 + r) * cols + c0 + c) * px, px), px)
                piece = ref[pl.ds(pl.multiple_of((r * wide + c) * px, px), px), :]
                acc[at, :] += piece.astype(F32)
            return 0

        lax.fori_loop(0, high, add, 0)

    def store(i, _):
        tg_ref[pl.ds(i * px, px), :] = (acc[pl.ds(i * px, px), :] * inv_root).astype(BF16)
        return 0

    lax.fori_loop(0, n, store, 0)


VM = pl.BlockSpec(memory_space=pltpu.VMEM)
SM = pl.BlockSpec(memory_space=pltpu.SMEM)


def call(kernel, outs, scratch, args, scalars=0, flops=10**8, moved=4 * 10**6):
    return pl.pallas_call(
        kernel,
        out_shape=[jax.ShapeDtypeStruct(s, d) for s, d in outs],
        in_specs=[SM] * scalars + [VM] * (len(args) - scalars),
        out_specs=[VM] * len(outs),
        scratch_shapes=[pltpu.VMEM(s, d) for s, d in scratch],
        compiler_params=pltpu.CompilerParams(vmem_limit_bytes=60 * 2**20),
        cost_estimate=pl.CostEstimate(flops=flops, bytes_accessed=moved, transcendentals=0),
    )(*args)


def shards(source, target, target_ids, out_grad, w_in, b_in, w_out):
    rows, cols, px, channels = source.shape
    picks = target_ids.shape[2]
    n = rows * cols
    slots = 1 << (picks - 1).bit_length()
    per = LANES // slots
    groups = n // per
    pieces, base, ext = plan(rows, cols)
    ext_pad = -(-ext // LANES) * LANES
    strip_at, sub_at = lax.axis_index("strip"), lax.axis_index("sub")
    rep = lax.axis_index("rep")

    def boundary(x, qz, qx):
        if qz is not None:
            x = lax.dynamic_slice_in_dim(x, facing(qz, rows, strip_at), H, 0)
        if qx is not None:
            x = lax.dynamic_slice_in_dim(x, facing(qx, cols, sub_at), H, 1)
        return x

    halo = [swap(boundary(target, qz, qx), qz, qx) for qz, qx in pieces]
    flat = [h.reshape(-1, channels) for h in halo]
    starts = [0] + [base[q] for q in pieces]
    counts = [n] + [f.shape[0] // px for f in flat]

    place = places(target_ids.reshape(n, picks), base, rows, cols)
    x_ids = jnp.pad(place, ((0, 0), (0, slots - picks)), constant_values=-1).reshape(groups, LANES)
    og = jnp.pad(
        out_grad.reshape(n, picks, out_grad.shape[3]), ((0, 0), (0, slots - picks), (0, 0))
    ).reshape(n * slots, out_grad.shape[3])
    (grad_hidden,) = call(
        hidden_kernel, [((w_out.shape[0], n * slots), F32)], [], (og, w_out)
    )

    src = source.reshape(n * px, channels)
    tgt = target.reshape(n * px, channels)
    costs, tgt_t, src_t = call(
        partial(corr_kernel, px, n, ext, starts, slots),
        [((px, n * slots), BF16), ((px, ext_pad, channels), BF16), ((px, n, channels), BF16)],
        [
            ((n * px, channels), F32),
            ((ext_pad * px, channels), F32),
            ((ext_pad // LANES, n * px, LANES), F32),
        ],
        (src, tgt, *flat, x_ids),
    )
    reps = lax.axis_size("rep")
    other = lax.ppermute(costs, "rep", [(i, reps - 1 - i) for i in range(reps)])
    (gc,) = call(
        decoder_kernel,
        [((px, n * slots), BF16)],
        [((2 * px, n * slots), BF16)],
        (rep.astype(jnp.int32)[None], costs, other, grad_hidden, w_in.T, b_in[:, None], w_in),
        scalars=1,
    )
    sg, own, *parts = call(
        partial(grads_kernel, px, n, starts, counts, slots),
        [((n * px, channels), BF16), ((n * px, channels), F32)]
        + [((c * px, channels), BF16) for c in counts[1:]],
        [
            ((ext_pad // LANES, n * px, LANES), F32),
            ((n * px, channels), F32),
            ((ext_pad * px, channels), F32),
        ],
        (gc, x_ids, tgt_t, src_t),
    )
    back = [swap(part, qz, qx) for part, (qz, qx) in zip(parts, pieces)]
    offs = jnp.stack(
        [facing(q, rows, strip_at) for q in (0, 1)] + [facing(q, cols, sub_at) for q in (0, 1)]
    ).astype(jnp.int32)
    (tg,) = call(
        partial(total_kernel, px, rows, cols, pieces),
        [((n * px, channels), BF16)],
        [((n * px, channels), F32)],
        (offs, own, *back),
        scalars=1,
    )
    return sg.reshape(source.shape), tg.reshape(source.shape)


def solution(mesh):
    cells = P(("groups", "strip"), "sub", "rep", None)
    placed = (
        cells,
        cells,
        P(("groups", "strip"), "sub", None),
        P(("groups", "strip"), "sub", None, None),
        P(),
        P(),
        P(),
    )
    return jax.shard_map(
        shards, mesh=mesh, in_specs=placed, out_specs=(cells, cells), check_vma=False
    )
```

```python
from functools import partial
import math

import jax
import jax.numpy as jnp
from jax import lax
from jax.experimental import pallas as pl
from jax.experimental.pallas import tpu as pltpu
from jax.sharding import PartitionSpec as P

H = 3
LANES = 128
NT = (((1,), (1,)), ((), ()))
TN = (((0,), (0,)), ((), ()))
F32 = jnp.float32
BF16 = jnp.bfloat16


def mate(i, q, n):
    j = i + 1 if (i + q) % 2 == 0 else i - 1
    return j if 0 <= j < n else None


def turns(n):
    return [q for q in (0, 1) if any(mate(i, q, n) is not None for i in range(n))]


def swap(x, qz, qx):
    strips, subs = lax.axis_size("strip"), lax.axis_size("sub")
    pairs = []
    for s in range(strips):
        for u in range(subs):
            t = s if qz is None else mate(s, qz, strips)
            v = u if qx is None else mate(u, qx, subs)
            if t is not None and v is not None:
                pairs.append((s * subs + u, t * subs + v))
    return lax.ppermute(x, ("strip", "sub"), pairs)


def plan(rows, cols):
    zs, xs = turns(lax.axis_size("strip")), turns(lax.axis_size("sub"))
    pieces = [(q, r) for q in zs for r in xs]
    pieces += [(q, None) for q in zs]
    pieces += [(None, r) for r in xs]
    base, at = {(None, None): 0}, rows * cols
    for qz, qx in pieces:
        base[qz, qx] = at
        at += (rows if qz is None else H) * (cols if qx is None else H)
    return pieces, base, at


def facing(q, extent, index):
    return jnp.where((index + q) % 2 == 0, extent - H, 0)


def places(target_ids, base, rows, cols):
    total_cols = cols * lax.axis_size("sub")
    strip_at, sub_at = lax.axis_index("strip"), lax.axis_index("sub")

    def split(d, extent, index):
        side = jnp.where(d < 0, -1, jnp.where(d >= extent, 1, 0))
        inner = jnp.where(side < 0, d + H, jnp.where(side > 0, d - extent, d))
        ahead = jnp.where(index % 2 == 0, 1, -1)
        turn = jnp.where(side == 0, -1, jnp.where(side == ahead, 0, 1))
        return turn, inner

    row, col = target_ids // total_cols, target_ids % total_cols
    tz, dr = split(row - strip_at * rows, rows, strip_at)
    tx, dc = split(col - sub_at * cols, cols, sub_at)
    where_to = jnp.full(target_ids.shape, -1, jnp.int32)
    for (qz, qx), start in base.items():
        here = (tz == (-1 if qz is None else qz)) & (tx == (-1 if qx is None else qx))
        width = cols if qx is None else H
        where_to = jnp.where(here, start + dr * width + dc, where_to)
    return where_to, (row % rows) * cols + col % cols


def loop(count, body, most=4):
    step = max(d for d in range(1, most + 1) if count % d == 0) if count else 1

    def run(i, _):
        body(i)
        return 0

    lax.fori_loop(0, count, run, 0, unroll=step)


def widen(dst, at, src_ref, px, pitch):
    def body(i):
        rows = src_ref[pl.ds(pl.multiple_of(i * px, px), px), :]
        dst[pl.ds((at + i) * pitch, px), :] = rows.astype(F32)

    loop(src_ref.shape[0] // px, body)


def clear(dst, at, end, px, pitch):
    def body(i):
        dst[pl.ds((at + i) * pitch, px), :] = jnp.zeros((px, dst.shape[1]), F32)

    loop(end - at, body)


def hot(row, tile=0):
    e = lax.broadcasted_iota(jnp.int32, (LANES, LANES), 0) + tile * LANES
    return (e == row).astype(F32).astype(BF16)


def pick_hot(e_ref, b, slots, tile):
    group, j = divmod(b, LANES // slots)
    lane = lax.broadcasted_iota(jnp.int32, (1, LANES), 1) // slots
    return hot(jnp.where(lane == j, e_ref[group : group + 1, :], -1), tile)


def prep_kernel(px, n, slots, src_ref, tgt_ref, og_ref, w_out_ref, src_t, tgt_t, gh_ref, s32, t32, og):
    pitch = px + 1
    widen(s32, 0, src_ref, px, pitch)
    widen(t32, 0, tgt_ref, px, pitch)

    def turn(p):
        src_t[p] = s32[pl.ds(p, n, stride=pitch), :].astype(BF16)
        tgt_t[p] = t32[pl.ds(p, n, stride=pitch), :].astype(BF16)

    loop(px, turn)
    picks = og_ref.shape[1]
    og[...] = jnp.zeros_like(og)

    for b in range(n):
        og[b, :picks, :] = og_ref[b].astype(F32)
    for g in range(n * slots // LANES):
        per = LANES // slots
        block = og[g * per : (g + 1) * per].reshape(LANES, og.shape[2]).astype(BF16)
        gh_ref[:, g * LANES : (g + 1) * LANES] = lax.dot_general(
            w_out_ref[...], block, NT, preferred_element_type=F32
        )


def corr_kernel(px, n, ext, starts, slots, *refs):
    k = len(starts)
    own_t, src_t, e_ref, tgt_refs = refs[0], refs[1], refs[2], refs[3 : 3 + k]
    costs_ref, tgt_t, t32, corr = refs[3 + k :]
    ext_pad = tgt_t.shape[1]
    pitch = px + 1
    inv_root = 1.0 / math.sqrt(tgt_t.shape[2])
    for start, ref in zip(starts, tgt_refs):
        widen(t32, start - n, ref, px, pitch)
    clear(t32, ext - n, ext_pad - n, px, pitch)

    def per_pixel(p):
        tp = t32[pl.ds(p, ext_pad - n, stride=pitch), :].astype(BF16)
        tp = jnp.concatenate([own_t[p], tp], axis=0)
        tgt_t[p] = tp
        c = lax.dot_general(src_t[p], tp, NT, preferred_element_type=F32) * inv_root
        for t in range(ext_pad // LANES):
            corr[t, pl.ds(p, n, stride=pitch), :] = c[:, t * LANES : (t + 1) * LANES]

    loop(px, per_pixel, 8)
    per = LANES // slots
    for g in range(n // per):
        acc = jnp.zeros((px, LANES), F32)
        for j in range(per):
            b = g * per + j
            for t in range(ext_pad // LANES):
                acc += jnp.dot(
                    corr[t, b * pitch : b * pitch + px, :].astype(BF16),
                    pick_hot(e_ref, b, slots, t),
                    preferred_element_type=F32,
                )
        costs_ref[:, g * LANES : (g + 1) * LANES] = acc.astype(BF16)


def gelu_slope(x):
    c = math.sqrt(2.0 / math.pi)
    x2 = x * x
    th = jnp.tanh(c * (x + 0.044715 * (x2 * x)))
    inner = c * (1.0 + (3.0 * 0.044715) * x2)
    return 0.5 * (1.0 + th) + (0.5 * x) * ((1.0 - th) * (1.0 + th)) * inner


def decoder_kernel(info_ref, mine_ref, other_ref, gh_ref, wt_ref, b_ref, w_ref, gc_ref, whole):
    px = mine_ref.shape[0]
    rep = info_ref[0]
    whole[pl.ds(pl.multiple_of(rep * px, px), px), :] = mine_ref[...]
    whole[pl.ds(pl.multiple_of((1 - rep) * px, px), px), :] = other_ref[...]
    w_half = w_ref[pl.ds(pl.multiple_of(rep * px, px), px), :]
    width = 2 * LANES
    for g in range(mine_ref.shape[1] // width):
        cut = slice(g * width, (g + 1) * width)
        pre = jnp.dot(wt_ref[...], whole[:, cut], preferred_element_type=F32) + b_ref[...]
        grad = (gh_ref[:, cut] * gelu_slope(pre)).astype(BF16)
        gc_ref[:, cut] = jnp.dot(w_half, grad, preferred_element_type=F32).astype(BF16)


def send_kernel(px, rows, cols, slots, pieces, starts, counts, info_ref, gc_ref, e_ref, m_ref, *out_refs):
    per = LANES // slots
    wide = cols // per
    lane = lax.broadcasted_iota(jnp.int32, (1, LANES), 1) // slots
    for (qz, qx), start, count, ref in zip(pieces, starts, counts, out_refs):
        r0 = 0 if qz is None else info_ref[1 + qz]
        c0 = 0 if qx is None else info_ref[3 + qx]
        half, shift = c0 // per, c0 % per
        i = 0
        for r in range(rows if qz is None else H):
            for h in range(wide if qx is None else 1):
                g = (r0 + r) * wide + half + h
                e, m = e_ref[pl.ds(g, 1), :], m_ref[pl.ds(g, 1), :]
                here = (e >= start) & (e < start + count)
                to = jnp.where(here, (lane - shift) * slots + m, -1)
                gc = gc_ref[:, pl.ds(pl.multiple_of(g * LANES, LANES), LANES)]
                ref[:, i * LANES : (i + 1) * LANES] = lax.dot_general(
                    gc, hot(to), NT, preferred_element_type=F32
                ).astype(BF16)
                i += 1


def own_kernel(px, n, slots, gc_ref, e_ref, tgt_t, src_t, sg_ref, own_ref, pw, s32):
    ext_pad = tgt_t.shape[1]
    pitch = px + 1
    inv_root = 1.0 / math.sqrt(tgt_t.shape[2])
    tiles = ext_pad // LANES
    per = LANES // slots
    for b in range(n):
        g = b // per
        gc = gc_ref[:, g * LANES : (g + 1) * LANES]
        for t in range(tiles):
            pw[t, b * pitch : b * pitch + px, :] = lax.dot_general(
                gc, pick_hot(e_ref, b, slots, t), NT, preferred_element_type=F32
            )

    def per_pixel(p):
        tp = tgt_t[p]
        sg = jnp.zeros((n, tp.shape[1]), F32)
        for t in range(tiles):
            w = pw[t, pl.ds(p, n, stride=pitch), :].astype(BF16)
            sg += jnp.dot(w, tp[t * LANES : (t + 1) * LANES, :], preferred_element_type=F32)
            if t == 0:
                own_ref[p] = lax.dot_general(
                    w[:, :n], src_t[p], TN, preferred_element_type=F32
                )
        s32[pl.ds(p, n, stride=pitch), :] = sg * inv_root

    loop(px, per_pixel, 8)

    def narrow(i):
        sg_ref[pl.ds(pl.multiple_of(i * px, px), px), :] = s32[pl.ds(i * pitch, px), :].astype(BF16)

    loop(n, narrow)


def halo_kernel(px, starts, *refs):
    k = len(starts)
    src_refs, out, s32 = refs[:k], refs[k], refs[k + 1]
    pitch = px + 1
    for start, ref in zip(starts, src_refs):
        widen(s32, start, ref, px, pitch)
    last = starts[-1] + src_refs[-1].shape[0] // px
    clear(s32, last, out.shape[1], px, pitch)

    def turn(p):
        out[p] = s32[pl.ds(p, out.shape[1], stride=pitch), :].astype(BF16)

    loop(px, turn)


def total_kernel(px, n, slots, widths, own_ref, halo_t, *refs):
    k = len(widths)
    msg_refs, tg_ref, pw, t32 = refs[:k], refs[k], refs[k + 1], refs[k + 2]
    pitch = px + 1
    inv_root = 1.0 / math.sqrt(own_ref.shape[2])
    at = 0
    for width, ref in zip(widths, msg_refs):
        for g in range(ref.shape[1] // LANES):
            block = ref[:, g * LANES : (g + 1) * LANES].astype(F32)
            for j in range(width):
                turned = block if j == 0 else pltpu.roll(block, LANES - j * slots, 1)
                pw[at * pitch : at * pitch + px, :] = turned
                at += 1
    clear(pw, at, halo_t.shape[1], px, pitch)

    def per_pixel(p):
        w = pw[pl.ds(p, halo_t.shape[1], stride=pitch), :]
        tg = own_ref[p] + lax.dot_general(
            w[:, :n].astype(BF16), halo_t[p], TN, preferred_element_type=F32
        )
        t32[pl.ds(p, n, stride=pitch), :] = tg * inv_root

    loop(px, per_pixel, 8)

    def narrow(i):
        tg_ref[pl.ds(pl.multiple_of(i * px, px), px), :] = t32[pl.ds(i * pitch, px), :].astype(BF16)

    loop(n, narrow)


VM = pl.BlockSpec(memory_space=pltpu.VMEM)
SM = pl.BlockSpec(memory_space=pltpu.SMEM)


def call(name, kernel, outs, scratch, args, scalars=0, us=2.0):
    return pl.pallas_call(
        kernel,
        name=name,
        out_shape=[jax.ShapeDtypeStruct(s, d) for s, d in outs],
        in_specs=[SM] * scalars + [VM] * (len(args) - scalars),
        out_specs=[VM] * len(outs),
        scratch_shapes=[pltpu.VMEM(s, d) for s, d in scratch],
        compiler_params=pltpu.CompilerParams(vmem_limit_bytes=28 * 2**20),
        cost_estimate=pl.CostEstimate(
            flops=0, bytes_accessed=int(us * 3 * 10**6), transcendentals=0
        ),
    )(*args)


def shards(source, target, target_ids, out_grad, w_in, b_in, w_out):
    rows, cols, px, channels = source.shape
    picks = target_ids.shape[2]
    n = rows * cols
    pitch = px + 1
    slots = 1 << (picks - 1).bit_length()
    per = LANES // slots
    groups = n // per
    assert n <= slots and cols % per == 0 and H <= per and groups * per == n
    pieces, base, ext = plan(rows, cols)
    ext_pad = -(-ext // LANES) * LANES
    strip_at, sub_at = lax.axis_index("strip"), lax.axis_index("sub")
    rep = lax.axis_index("rep")

    def boundary(x, qz, qx):
        if qz is not None:
            x = lax.dynamic_slice_in_dim(x, facing(qz, rows, strip_at), H, 0)
        if qx is not None:
            x = lax.dynamic_slice_in_dim(x, facing(qx, cols, sub_at), H, 1)
        return x

    def halo_of(x):
        got = [swap(boundary(x, qz, qx), qz, qx) for qz, qx in pieces]
        return [h.reshape(-1, channels) for h in got]

    tgt_halo = halo_of(target)
    src_halo = halo_of(source)
    starts = [base[q] for q in pieces]
    counts = [h.shape[0] // px for h in tgt_halo]

    def slotted(x):
        return jnp.pad(x, ((0, 0), (0, slots - picks)), constant_values=-1).reshape(groups, LANES)

    e_at, m_at = places(target_ids.reshape(n, picks), base, rows, cols)
    e_ids, m_ids = slotted(e_at), slotted(m_at)
    info = jnp.stack(
        [rep]
        + [facing(q, rows, strip_at) for q in (0, 1)]
        + [facing(q, cols, sub_at) for q in (0, 1)]
    ).astype(jnp.int32)

    src_t, own_t, grad_hidden = call(
        "prep",
        partial(prep_kernel, px, n, slots),
        [((px, n, channels), BF16), ((px, n, channels), BF16), ((w_out.shape[0], n * slots), F32)],
        [((n * pitch, channels), F32)] * 2 + [((n, slots, out_grad.shape[3]), F32)],
        (
            source.reshape(n * px, channels),
            target.reshape(n * px, channels),
            out_grad.reshape(n, picks, out_grad.shape[3]),
            w_out,
        ),
        us=4,
    )
    costs, tgt_t = call(
        "corr",
        partial(corr_kernel, px, n, ext, starts, slots),
        [((px, n * slots), BF16), ((px, ext_pad, channels), BF16)],
        [
            (((ext_pad - n) * pitch, channels), F32),
            ((ext_pad // LANES, n * pitch, LANES), F32),
        ],
        (own_t, src_t, e_ids, *tgt_halo),
        us=3,
    )
    reps = lax.axis_size("rep")
    other = lax.ppermute(costs, "rep", [(i, reps - 1 - i) for i in range(reps)])
    (gc,) = call(
        "decoder",
        decoder_kernel,
        [((px, n * slots), BF16)],
        [((2 * px, n * slots), BF16)],
        (info, costs, other, grad_hidden, w_in.T, b_in[:, None], w_in),
        scalars=1,
        us=3,
    )
    lanes = [
        (rows if qz is None else H) * (cols // per if qx is None else 1) * LANES
        for qz, qx in pieces
    ]
    sent = call(
        "send",
        partial(send_kernel, px, rows, cols, slots, pieces, starts, counts),
        [((px, w), BF16) for w in lanes],
        [],
        (info, gc, e_ids, m_ids),
        scalars=1,
        us=1,
    )
    got = [swap(x, qz, qx) for x, (qz, qx) in zip(sent, pieces)]
    sg, own = call(
        "own",
        partial(own_kernel, px, n, slots),
        [((n * px, channels), BF16), ((px, n, channels), F32)],
        [((ext_pad // LANES, n * pitch, LANES), F32), ((n * pitch, channels), F32)],
        (gc, e_ids, tgt_t, src_t),
        us=4,
    )
    halo_pad = -(-(ext - n) // 16) * 16
    (halo_t,) = call(
        "halo",
        partial(halo_kernel, px, [s - n for s in starts]),
        [((px, halo_pad, channels), BF16)],
        [((halo_pad * pitch, channels), F32)],
        tuple(src_halo),
        us=1,
    )
    (tg,) = call(
        "total",
        partial(total_kernel, px, n, slots, [per if qx is None else H for _, qx in pieces]),
        [((n * px, channels), BF16)],
        [((halo_pad * pitch, LANES), F32), ((n * pitch, channels), F32)],
        (own, halo_t, *got),
        us=3,
    )
    return sg.reshape(source.shape), tg.reshape(source.shape)


def solution(mesh):
    cells = P(("groups", "strip"), "sub", "rep", None)
    placed = (
        cells,
        cells,
        P(("groups", "strip"), "sub", None),
        P(("groups", "strip"), "sub", None, None),
        P(),
        P(),
        P(),
    )
    return jax.shard_map(
        shards, mesh=mesh, in_specs=placed, out_specs=(cells, cells), check_vma=False
    )
```

```python
from functools import partial
import math

import jax
import jax.numpy as jnp
from jax import lax
from jax.experimental import pallas as pl
from jax.experimental.pallas import tpu as pltpu
from jax.sharding import PartitionSpec as P

H = 3
LANES = 128
NT = (((1,), (1,)), ((), ()))
TN = (((0,), (0,)), ((), ()))
F32 = jnp.float32
BF16 = jnp.bfloat16


def mate(i, q, n):
    j = i + 1 if (i + q) % 2 == 0 else i - 1
    return j if 0 <= j < n else None


def turns(n):
    return [q for q in (0, 1) if any(mate(i, q, n) is not None for i in range(n))]


def swap(x, qz, qx):
    strips, subs = lax.axis_size("strip"), lax.axis_size("sub")
    pairs = []
    for s in range(strips):
        for u in range(subs):
            t = s if qz is None else mate(s, qz, strips)
            v = u if qx is None else mate(u, qx, subs)
            if t is not None and v is not None:
                pairs.append((s * subs + u, t * subs + v))
    return lax.ppermute(x, ("strip", "sub"), pairs)


def plan(rows, cols):
    zs, xs = turns(lax.axis_size("strip")), turns(lax.axis_size("sub"))
    pieces = [(q, r) for q in zs for r in xs]
    pieces += [(q, None) for q in zs]
    pieces += [(None, r) for r in xs]
    base, at = {(None, None): 0}, rows * cols
    for qz, qx in pieces:
        base[qz, qx] = at
        at += (rows if qz is None else H) * (cols if qx is None else H)
    return pieces, base, at


def facing(q, extent, index):
    return jnp.where((index + q) % 2 == 0, extent - H, 0)


def scale_of(n):
    assert n & (n - 1) == 0
    return n.bit_length() - 1


def places(ids, base, rows, cols):
    total_cols = cols * lax.axis_size("sub")
    strip_at, sub_at = lax.axis_index("strip"), lax.axis_index("sub")

    def split(d, extent, index):
        side = jnp.where(d < 0, -1, jnp.where(d >= extent, 1, 0))
        inner = jnp.where(side < 0, d + H, jnp.where(side > 0, d - extent, d))
        ahead = jnp.where(index % 2 == 0, 1, -1)
        turn = jnp.where(side == 0, -1, jnp.where(side == ahead, 0, 1))
        return turn, inner

    row = lax.shift_right_arithmetic(ids, jnp.int32(scale_of(total_cols)))
    col = ids & (total_cols - 1)
    tz, dr = split(row - strip_at * rows, rows, strip_at)
    tx, dc = split(col - sub_at * cols, cols, sub_at)
    where_to = jnp.full(ids.shape, -1, jnp.int32)
    for (qz, qx), start in base.items():
        here = (tz == (-1 if qz is None else qz)) & (tx == (-1 if qx is None else qx))
        width = cols if qx is None else H
        where_to = jnp.where(here, start + dr * width + dc, where_to)
    assert scale_of(rows) + scale_of(cols) >= 0
    return where_to, (row & (rows - 1)) * cols + (col & (cols - 1))


def cut_kernel(pieces, rows, cols, x_ref, *refs):
    out_refs, sems = refs[:-1], refs[-1]
    strip_at, sub_at = lax.axis_index("strip"), lax.axis_index("sub")
    copies = []
    for i, ((qz, qx), ref) in enumerate(zip(pieces, out_refs)):
        r = pl.ds(0, rows) if qz is None else pl.ds(facing(qz, rows, strip_at), H)
        c = pl.ds(0, cols) if qx is None else pl.ds(facing(qx, cols, sub_at), H)
        copies.append(pltpu.make_async_copy(x_ref.at[r, c], ref, sems.at[i]))
    for copy in copies:
        copy.start()
    for copy in copies:
        copy.wait()


def loop(count, body, most=4):
    step = max(d for d in range(1, most + 1) if count % d == 0) if count else 1

    def run(i, _):
        body(i)
        return 0

    lax.fori_loop(0, count, run, 0, unroll=step)


def widen(dst, at, src_ref, px, pitch):
    def body(i):
        rows = src_ref[pl.ds(pl.multiple_of(i * px, px), px), :]
        dst[pl.ds((at + i) * pitch, px), :] = rows.astype(F32)

    loop(src_ref.shape[0] // px, body)


def clear(dst, at, end, px, pitch):
    def body(i):
        dst[pl.ds((at + i) * pitch, px), :] = jnp.zeros((px, dst.shape[1]), F32)

    loop(end - at, body)


def hot(row, tile=0):
    e = lax.broadcasted_iota(jnp.int32, (LANES, LANES), 0) + tile * LANES
    return (e == row).astype(F32).astype(BF16)


def pick_hot(e_ref, b, slots, tile):
    group, j = divmod(b, LANES // slots)
    lane = lax.broadcasted_iota(jnp.int32, (1, LANES), 1) // slots
    return hot(jnp.where(lane == j, e_ref[group : group + 1, :], -1), tile)


def slotted(x, out_ref, table, slots):
    n, picks = x.shape
    per = LANES // slots
    table[...] = jnp.full(table.shape, -1, jnp.int32)
    table[:, :picks] = x
    lane = lax.broadcasted_iota(jnp.int32, (n // per, LANES), 1) // slots
    acc = jnp.full((n // per, LANES), -1, jnp.int32)
    for j in range(per):
        rows = table[pl.ds(j, n // per, stride=per), :]
        acc = jnp.where(lane == j, rows if j == 0 else pltpu.roll(rows, j * slots, 1), acc)
    out_ref[...] = acc


def prep_kernel(base, rows, cols, slots, src_ref, tgt_ref, og_ref, ids_ref, w_in_ref, b_ref, w_out_ref, *refs):
    src_t, tgt_t, gh_ref, wt_ref, bt_ref, e_ref, m_ref, s32, t32, og, table = refs
    px, n, _ = src_t.shape
    pitch = px + 1
    e_at, m_at = places(ids_ref[...], base, rows, cols)
    slotted(e_at, e_ref, table, slots)
    slotted(m_at, m_ref, table, slots)
    wt_ref[...] = w_in_ref[...].T
    bt_ref[...] = jnp.broadcast_to(b_ref[...], (LANES, b_ref.shape[1])).T
    widen(s32, 0, src_ref, px, pitch)
    widen(t32, 0, tgt_ref, px, pitch)

    def turn(p):
        src_t[p] = s32[pl.ds(p, n, stride=pitch), :].astype(BF16)
        tgt_t[p] = t32[pl.ds(p, n, stride=pitch), :].astype(BF16)

    loop(px, turn)
    picks = og_ref.shape[1]
    og[...] = jnp.zeros_like(og)

    for b in range(n):
        og[b, :picks, :] = og_ref[b].astype(F32)
    for g in range(n * slots // LANES):
        per = LANES // slots
        block = og[g * per : (g + 1) * per].reshape(LANES, og.shape[2]).astype(BF16)
        gh_ref[:, g * LANES : (g + 1) * LANES] = lax.dot_general(
            w_out_ref[...], block, NT, preferred_element_type=F32
        )


def corr_kernel(px, n, ext, starts, slots, *refs):
    k = len(starts)
    own_t, src_t, e_ref, tgt_refs = refs[0], refs[1], refs[2], refs[3 : 3 + k]
    costs_ref, tgt_t, t32, corr = refs[3 + k :]
    ext_pad = tgt_t.shape[1]
    pitch = px + 1
    inv_root = 1.0 / math.sqrt(tgt_t.shape[2])
    for start, ref in zip(starts, tgt_refs):
        widen(t32, start - n, ref, px, pitch)
    clear(t32, ext - n, ext_pad - n, px, pitch)

    def per_pixel(p):
        tp = t32[pl.ds(p, ext_pad - n, stride=pitch), :].astype(BF16)
        tp = jnp.concatenate([own_t[p], tp], axis=0)
        tgt_t[p] = tp
        c = lax.dot_general(src_t[p], tp, NT, preferred_element_type=F32) * inv_root
        for t in range(ext_pad // LANES):
            corr[t, pl.ds(p, n, stride=pitch), :] = c[:, t * LANES : (t + 1) * LANES]

    loop(px, per_pixel, 8)
    per = LANES // slots
    for g in range(n // per):
        acc = jnp.zeros((px, LANES), F32)
        for j in range(per):
            b = g * per + j
            for t in range(ext_pad // LANES):
                acc += jnp.dot(
                    corr[t, b * pitch : b * pitch + px, :].astype(BF16),
                    pick_hot(e_ref, b, slots, t),
                    preferred_element_type=F32,
                )
        costs_ref[:, g * LANES : (g + 1) * LANES] = acc.astype(BF16)


def gelu_slope(x):
    c = math.sqrt(2.0 / math.pi)
    x2 = x * x
    th = jnp.tanh(c * (x + 0.044715 * (x2 * x)))
    inner = c * (1.0 + (3.0 * 0.044715) * x2)
    return 0.5 * (1.0 + th) + (0.5 * x) * ((1.0 - th) * (1.0 + th)) * inner


def decoder_kernel(rows, cols, slots, pieces, starts, counts, *refs):
    mine_ref, other_ref, gh_ref, wt_ref, bt_ref, w_ref, e_ref, m_ref = refs[:8]
    gc_ref, out_refs, whole = refs[8], refs[9:-1], refs[-1]
    px = mine_ref.shape[0]
    rep = lax.axis_index("rep")
    whole[pl.ds(pl.multiple_of(rep * px, px), px), :] = mine_ref[...]
    whole[pl.ds(pl.multiple_of((1 - rep) * px, px), px), :] = other_ref[...]
    w_half = w_ref[pl.ds(pl.multiple_of(rep * px, px), px), :]
    wide = 2
    bias = jnp.concatenate([bt_ref[...]] * wide, axis=1)
    width = wide * LANES
    for g in range(mine_ref.shape[1] // width):
        cut = slice(g * width, (g + 1) * width)
        pre = jnp.dot(wt_ref[...], whole[:, cut], preferred_element_type=F32) + bias
        grad = (gh_ref[:, cut] * gelu_slope(pre)).astype(BF16)
        gc_ref[:, cut] = jnp.dot(w_half, grad, preferred_element_type=F32).astype(BF16)
    send(rows, cols, slots, pieces, starts, counts, gc_ref, e_ref, m_ref, out_refs)


def send(rows, cols, slots, pieces, starts, counts, gc_ref, e_ref, m_ref, out_refs):
    per = LANES // slots
    wide = cols // per
    strip_at, sub_at = lax.axis_index("strip"), lax.axis_index("sub")
    lane = lax.broadcasted_iota(jnp.int32, (1, LANES), 1) // slots
    for (qz, qx), start, count, ref in zip(pieces, starts, counts, out_refs):
        r0 = 0 if qz is None else facing(qz, rows, strip_at)
        tail = None if qx is None else (sub_at + qx) % 2 == 0
        half = 0 if qx is None else jnp.where(tail, (cols - H) // per, 0)
        shift = 0 if qx is None else jnp.where(tail, (cols - H) % per, 0)
        i = 0
        for r in range(rows if qz is None else H):
            for h in range(wide if qx is None else 1):
                g = (r0 + r) * wide + half + h
                e, m = e_ref[pl.ds(g, 1), :], m_ref[pl.ds(g, 1), :]
                here = (e >= start) & (e < start + count)
                to = jnp.where(here, (lane - shift) * slots + m, -1)
                at = g * LANES
                at = at if isinstance(at, int) else pl.multiple_of(at, LANES)
                ref[:, i * LANES : (i + 1) * LANES] = lax.dot_general(
                    gc_ref[:, pl.ds(at, LANES)], hot(to), NT, preferred_element_type=F32
                ).astype(BF16)
                i += 1


def own_kernel(px, n, slots, gc_ref, e_ref, tgt_t, src_t, sg_ref, own_ref, pw, s32):
    ext_pad = tgt_t.shape[1]
    pitch = px + 1
    inv_root = 1.0 / math.sqrt(tgt_t.shape[2])
    tiles = ext_pad // LANES
    per = LANES // slots
    for b in range(n):
        g = b // per
        gc = gc_ref[:, g * LANES : (g + 1) * LANES]
        for t in range(tiles):
            pw[t, b * pitch : b * pitch + px, :] = lax.dot_general(
                gc, pick_hot(e_ref, b, slots, t), NT, preferred_element_type=F32
            )

    def per_pixel(p):
        tp = tgt_t[p]
        sg = jnp.zeros((n, tp.shape[1]), F32)
        for t in range(tiles):
            w = pw[t, pl.ds(p, n, stride=pitch), :].astype(BF16)
            sg += jnp.dot(w, tp[t * LANES : (t + 1) * LANES, :], preferred_element_type=F32)
            if t == 0:
                own_ref[p] = lax.dot_general(
                    w[:, :n], src_t[p], TN, preferred_element_type=F32
                )
        s32[pl.ds(p, n, stride=pitch), :] = sg * inv_root

    loop(px, per_pixel, 8)

    def narrow(i):
        sg_ref[pl.ds(pl.multiple_of(i * px, px), px), :] = s32[pl.ds(i * pitch, px), :].astype(BF16)

    loop(n, narrow)


def halo_kernel(px, starts, *refs):
    k = len(starts)
    src_refs, out, s32 = refs[:k], refs[k], refs[k + 1]
    pitch = px + 1
    for start, ref in zip(starts, src_refs):
        widen(s32, start, ref, px, pitch)
    last = starts[-1] + src_refs[-1].shape[0] // px
    clear(s32, last, out.shape[1], px, pitch)

    def turn(p):
        out[p] = s32[pl.ds(p, out.shape[1], stride=pitch), :].astype(BF16)

    loop(px, turn)


def total_kernel(px, n, slots, widths, own_ref, halo_t, *refs):
    k = len(widths)
    msg_refs, tg_ref, pw, t32 = refs[:k], refs[k], refs[k + 1], refs[k + 2]
    pitch = px + 1
    inv_root = 1.0 / math.sqrt(own_ref.shape[2])
    at = 0
    for width, ref in zip(widths, msg_refs):
        for g in range(ref.shape[1] // LANES):
            block = ref[:, g * LANES : (g + 1) * LANES].astype(F32)
            for j in range(width):
                turned = block if j == 0 else pltpu.roll(block, LANES - j * slots, 1)
                pw[at * pitch : at * pitch + px, :] = turned
                at += 1
    clear(pw, at, halo_t.shape[1], px, pitch)

    def per_pixel(p):
        w = pw[pl.ds(p, halo_t.shape[1], stride=pitch), :]
        tg = own_ref[p] + lax.dot_general(
            w[:, :n].astype(BF16), halo_t[p], TN, preferred_element_type=F32
        )
        t32[pl.ds(p, n, stride=pitch), :] = tg * inv_root

    loop(px, per_pixel, 8)

    def narrow(i):
        tg_ref[pl.ds(pl.multiple_of(i * px, px), px), :] = t32[pl.ds(i * pitch, px), :].astype(BF16)

    loop(n, narrow)


VM = pl.BlockSpec(memory_space=pltpu.VMEM)


def call(name, kernel, outs, scratch, args, us=2.0):
    return pl.pallas_call(
        kernel,
        name=name,
        out_shape=[jax.ShapeDtypeStruct(s, d) for s, d in outs],
        in_specs=[VM] * len(args),
        out_specs=[VM] * len(outs),
        scratch_shapes=[pltpu.VMEM(s, d) for s, d in scratch],
        compiler_params=pltpu.CompilerParams(vmem_limit_bytes=24 * 2**20),
        cost_estimate=pl.CostEstimate(
            flops=0, bytes_accessed=int(us * 3 * 10**6), transcendentals=0
        ),
    )(*args)


def shards(source, target, target_ids, out_grad, w_in, b_in, w_out):
    rows, cols, px, channels = source.shape
    picks = target_ids.shape[2]
    n = rows * cols
    pitch = px + 1
    slots = 1 << (picks - 1).bit_length()
    per = LANES // slots
    groups = n // per
    assert n <= slots and cols % per == 0 and H <= per and groups * per == n
    pieces, base, ext = plan(rows, cols)
    ext_pad = -(-ext // LANES) * LANES

    shapes = [
        (rows if qz is None else H, cols if qx is None else H, px, channels) for qz, qx in pieces
    ]

    def halo_of(name, x):
        slabs = pl.pallas_call(
            partial(cut_kernel, pieces, rows, cols),
            name=name,
            out_shape=[jax.ShapeDtypeStruct(s, BF16) for s in shapes],
            in_specs=[pl.BlockSpec(memory_space=pl.ANY)],
            out_specs=[VM] * len(pieces),
            scratch_shapes=[pltpu.SemaphoreType.DMA((len(pieces),))],
            compiler_params=pltpu.CompilerParams(vmem_limit_bytes=4 * 2**20),
        )(x)
        got = [swap(x, qz, qx) for x, (qz, qx) in zip(slabs, pieces)]
        return [h.reshape(-1, channels) for h in got]

    tgt_halo = halo_of("cut_target", target)
    src_halo = halo_of("cut_source", source)
    starts = [base[q] for q in pieces]
    counts = [h.shape[0] // px for h in tgt_halo]
    hidden = w_in.shape[1]
    src_t, own_t, grad_hidden, w_t, b_t, e_ids, m_ids = call(
        "prep",
        partial(prep_kernel, base, rows, cols, slots),
        [
            ((px, n, channels), BF16),
            ((px, n, channels), BF16),
            ((hidden, n * slots), F32),
            ((hidden, 2 * px), BF16),
            ((hidden, LANES), F32),
            ((groups, LANES), jnp.int32),
            ((groups, LANES), jnp.int32),
        ],
        [((n * pitch, channels), F32)] * 2
        + [((n, slots, out_grad.shape[3]), F32), ((n, LANES), jnp.int32)],
        (
            source.reshape(n * px, channels),
            target.reshape(n * px, channels),
            out_grad.reshape(n, picks, out_grad.shape[3]),
            target_ids.reshape(n, picks),
            w_in,
            b_in.reshape(1, hidden),
            w_out,
        ),
        us=4,
    )
    costs, tgt_t = call(
        "corr",
        partial(corr_kernel, px, n, ext, starts, slots),
        [((px, n * slots), BF16), ((px, ext_pad, channels), BF16)],
        [
            (((ext_pad - n) * pitch, channels), F32),
            ((ext_pad // LANES, n * pitch, LANES), F32),
        ],
        (own_t, src_t, e_ids, *tgt_halo),
        us=3,
    )
    reps = lax.axis_size("rep")
    other = lax.ppermute(costs, "rep", [(i, reps - 1 - i) for i in range(reps)])
    lanes = [
        (rows if qz is None else H) * (cols // per if qx is None else 1) * LANES
        for qz, qx in pieces
    ]
    gc, *sent = call(
        "decoder",
        partial(decoder_kernel, rows, cols, slots, pieces, starts, counts),
        [((px, n * slots), BF16)] + [((px, w), BF16) for w in lanes],
        [((2 * px, n * slots), BF16)],
        (costs, other, grad_hidden, w_t, b_t, w_in, e_ids, m_ids),
        us=3,
    )
    got = [swap(x, qz, qx) for x, (qz, qx) in zip(sent, pieces)]
    sg, own = call(
        "own",
        partial(own_kernel, px, n, slots),
        [((n * px, channels), BF16), ((px, n, channels), F32)],
        [((ext_pad // LANES, n * pitch, LANES), F32), ((n * pitch, channels), F32)],
        (gc, e_ids, tgt_t, src_t),
        us=4,
    )
    halo_pad = -(-(ext - n) // 16) * 16
    (halo_t,) = call(
        "halo",
        partial(halo_kernel, px, [s - n for s in starts]),
        [((px, halo_pad, channels), BF16)],
        [((halo_pad * pitch, channels), F32)],
        tuple(src_halo),
        us=1,
    )
    (tg,) = call(
        "total",
        partial(total_kernel, px, n, slots, [per if qx is None else H for _, qx in pieces]),
        [((n * px, channels), BF16)],
        [((halo_pad * pitch, LANES), F32), ((n * pitch, channels), F32)],
        (own, halo_t, *got),
        us=3,
    )
    return sg.reshape(source.shape), tg.reshape(source.shape)


def solution(mesh):
    cells = P(("groups", "strip"), "sub", "rep", None)
    placed = (
        cells,
        cells,
        P(("groups", "strip"), "sub", None),
        P(("groups", "strip"), "sub", None, None),
        P(),
        P(),
        P(),
    )
    return jax.shard_map(
        shards, mesh=mesh, in_specs=placed, out_specs=(cells, cells), check_vma=False
    )
```

```python
from functools import partial
import math

import jax
import jax.numpy as jnp
from jax import lax
from jax.experimental import pallas as pl
from jax.experimental.pallas import tpu as pltpu
from jax.sharding import PartitionSpec as P

H = 3
LANES = 128
NT = (((1,), (1,)), ((), ()))
TN = (((0,), (0,)), ((), ()))
F32 = jnp.float32
BF16 = jnp.bfloat16


def mate(i, q, n):
    j = i + 1 if (i + q) % 2 == 0 else i - 1
    return j if 0 <= j < n else None


def turns(n):
    return [q for q in (0, 1) if any(mate(i, q, n) is not None for i in range(n))]


def swap(x, qz, qx):
    strips, subs = lax.axis_size("strip"), lax.axis_size("sub")
    pairs = []
    for s in range(strips):
        for u in range(subs):
            t = s if qz is None else mate(s, qz, strips)
            v = u if qx is None else mate(u, qx, subs)
            if t is not None and v is not None:
                pairs.append((s * subs + u, t * subs + v))
    return lax.ppermute(x, ("strip", "sub"), pairs)


def plan(rows, cols):
    zs, xs = turns(lax.axis_size("strip")), turns(lax.axis_size("sub"))
    pieces = [(q, r) for q in zs for r in xs]
    pieces += [(q, None) for q in zs]
    pieces += [(None, r) for r in xs]
    base, at = {(None, None): 0}, rows * cols
    for qz, qx in pieces:
        base[qz, qx] = at
        at += (rows if qz is None else H) * (cols if qx is None else H)
    return pieces, base, at


def facing(q, extent, index):
    return jnp.where((index + q) % 2 == 0, extent - H, 0)


def scale_of(n):
    assert n & (n - 1) == 0
    return n.bit_length() - 1


def places(ids, base, rows, cols):
    total_cols = cols * lax.axis_size("sub")
    strip_at, sub_at = lax.axis_index("strip"), lax.axis_index("sub")

    def split(d, extent, index):
        side = jnp.where(d < 0, -1, jnp.where(d >= extent, 1, 0))
        inner = jnp.where(side < 0, d + H, jnp.where(side > 0, d - extent, d))
        ahead = jnp.where(index % 2 == 0, 1, -1)
        turn = jnp.where(side == 0, -1, jnp.where(side == ahead, 0, 1))
        return turn, inner

    row = lax.shift_right_arithmetic(ids, jnp.int32(scale_of(total_cols)))
    col = ids & (total_cols - 1)
    tz, dr = split(row - strip_at * rows, rows, strip_at)
    tx, dc = split(col - sub_at * cols, cols, sub_at)
    where_to = jnp.full(ids.shape, -1, jnp.int32)
    for (qz, qx), start in base.items():
        here = (tz == (-1 if qz is None else qz)) & (tx == (-1 if qx is None else qx))
        width = cols if qx is None else H
        where_to = jnp.where(here, start + dr * width + dc, where_to)
    assert scale_of(rows) + scale_of(cols) >= 0
    return where_to, (row & (rows - 1)) * cols + (col & (cols - 1))


def cuts(pieces, rows, cols, x_ref, out_refs, sems, at):
    strip_at, sub_at = lax.axis_index("strip"), lax.axis_index("sub")
    copies = []
    for i, ((qz, qx), ref) in enumerate(zip(pieces, out_refs)):
        r = pl.ds(0, rows) if qz is None else pl.ds(facing(qz, rows, strip_at), H)
        c = pl.ds(0, cols) if qx is None else pl.ds(facing(qx, cols, sub_at), H)
        copies.append(pltpu.make_async_copy(x_ref.at[r, c], ref, sems.at[at + i]))
    return copies


def loop(count, body, most=4):
    step = max(d for d in range(1, most + 1) if count % d == 0) if count else 1

    def run(i, _):
        body(i)
        return 0

    lax.fori_loop(0, count, run, 0, unroll=step)


def widen(dst, at, src_ref, px, pitch):
    def body(i):
        rows = src_ref[pl.ds(pl.multiple_of(i * px, px), px), :]
        dst[pl.ds((at + i) * pitch, px), :] = rows.astype(F32)

    loop(src_ref.shape[0] // px, body)


def clear(dst, at, end, px, pitch):
    def body(i):
        dst[pl.ds((at + i) * pitch, px), :] = jnp.zeros((px, dst.shape[1]), F32)

    loop(end - at, body)


def hot(row, tile=0):
    e = lax.broadcasted_iota(jnp.int32, (LANES, LANES), 0) + tile * LANES
    return (e == row).astype(F32).astype(BF16)


def pick_hot(e_ref, b, slots, tile):
    group, j = divmod(b, LANES // slots)
    lane = lax.broadcasted_iota(jnp.int32, (1, LANES), 1) // slots
    return hot(jnp.where(lane == j, e_ref[group : group + 1, :], -1), tile)


def slotted(x, out_ref, table, slots):
    n, picks = x.shape
    per = LANES // slots
    table[...] = jnp.full(table.shape, -1, jnp.int32)
    table[:, :picks] = x
    lane = lax.broadcasted_iota(jnp.int32, (n // per, LANES), 1) // slots
    acc = jnp.full((n // per, LANES), -1, jnp.int32)
    for j in range(per):
        rows = table[pl.ds(j, n // per, stride=per), :]
        acc = jnp.where(lane == j, rows if j == 0 else pltpu.roll(rows, j * slots, 1), acc)
    out_ref[...] = acc


def head_kernel(base, pieces, rows, cols, slots, *refs):
    k = len(pieces)
    far, rest = refs[:7], refs[7:]
    tgt_slabs, src_slabs, outs, rest = rest[:k], rest[k : 2 * k], rest[2 * k : 2 * k + 8], rest[2 * k + 8 :]
    src_t, tgt_t, gh_ref, wt_ref, wh_ref, bt_ref, e_ref, m_ref = outs
    (s32, t32, og, table), near, sems = rest[:4], rest[4:-1], rest[-1]
    src_ref, tgt_ref, og_ref, ids_ref, w_in_ref, b_ref, w_out_ref = near
    fetches = [pltpu.make_async_copy(f, v, sems.at[i]) for i, (f, v) in enumerate(zip(far, near))]
    slabs = cuts(pieces, rows, cols, far[1], tgt_slabs, sems, 7)
    slabs += cuts(pieces, rows, cols, far[0], src_slabs, sems, 7 + k)
    for copy in fetches[2:] + fetches[:2] + slabs:
        copy.start()
    px, n, _ = src_t.shape
    pitch = px + 1
    for fetch in fetches[2:]:
        fetch.wait()
    e_at, m_at = places(ids_ref[...], base, rows, cols)
    slotted(e_at, e_ref, table, slots)
    slotted(m_at, m_ref, table, slots)
    wt_ref[...] = w_in_ref[...].T
    rep = lax.axis_index("rep")
    wh_ref[...] = w_in_ref[pl.ds(pl.multiple_of(rep * px, px), px), :]
    bt_ref[...] = jnp.broadcast_to(b_ref[...], (LANES, b_ref.shape[1])).T
    picks = og_ref.shape[1]
    og[...] = jnp.zeros_like(og)
    for r in range(rows):
        for pick in range(picks):
            at = r * cols * (slots + 1) + pick
            og[pl.ds(at, cols, stride=slots + 1), :] = og_ref[r, pick].astype(F32)
    per = LANES // slots
    for g in range(n // per):
        block = jnp.concatenate(
            [og[b * (slots + 1) : b * (slots + 1) + slots, :] for b in range(g * per, (g + 1) * per)]
        ).astype(BF16)
        gh_ref[:, g * LANES : (g + 1) * LANES] = lax.dot_general(
            w_out_ref[...], block, NT, preferred_element_type=F32
        )
    for fetch in fetches[:2]:
        fetch.wait()
    for dst, src in ((s32, src_ref), (t32, tgt_ref)):

        def body(i, dst=dst, src=src):
            rows_of = src[i // cols, lax.rem(i, cols)]
            dst[pl.ds(i * pitch, px), :] = rows_of.astype(F32)

        loop(n, body)

    def turn(p):
        src_t[p] = s32[pl.ds(p, n, stride=pitch), :].astype(BF16)
        tgt_t[p] = t32[pl.ds(p, n, stride=pitch), :].astype(BF16)

    loop(px, turn)
    for copy in slabs:
        copy.wait()


def corr_kernel(px, n, ext, starts, slots, *refs):
    k = len(starts)
    own_t, src_t, e_ref, tgt_refs = refs[0], refs[1], refs[2], refs[3 : 3 + k]
    costs_ref, tgt_t, t32, corr = refs[3 + k :]
    ext_pad = tgt_t.shape[1]
    pitch = px + 1
    inv_root = 1.0 / math.sqrt(tgt_t.shape[2])
    for start, ref in zip(starts, tgt_refs):
        widen(t32, start - n, ref, px, pitch)
    clear(t32, ext - n, ext_pad - n, px, pitch)

    def per_pixel(p):
        tp = t32[pl.ds(p, ext_pad - n, stride=pitch), :].astype(BF16)
        tp = jnp.concatenate([own_t[p], tp], axis=0)
        tgt_t[p] = tp
        c = lax.dot_general(src_t[p], tp, NT, preferred_element_type=F32) * inv_root
        for t in range(ext_pad // LANES):
            corr[t, pl.ds(p, n, stride=pitch), :] = c[:, t * LANES : (t + 1) * LANES]

    loop(px, per_pixel, 8)
    per = LANES // slots
    for g in range(n // per):
        acc = jnp.zeros((px, LANES), F32)
        for j in range(per):
            b = g * per + j
            for t in range(ext_pad // LANES):
                acc += jnp.dot(
                    corr[t, b * pitch : b * pitch + px, :].astype(BF16),
                    pick_hot(e_ref, b, slots, t),
                    preferred_element_type=F32,
                )
        costs_ref[:, g * LANES : (g + 1) * LANES] = acc.astype(BF16)


def gelu_slope(x):
    c = math.sqrt(2.0 / math.pi)
    x2 = x * x
    th = jnp.tanh(c * (x + 0.044715 * (x2 * x)))
    inner = c * (1.0 + (3.0 * 0.044715) * x2)
    return 0.5 * (1.0 + th) + (0.5 * x) * ((1.0 - th) * (1.0 + th)) * inner


def decoder_kernel(rows, cols, slots, pieces, starts, counts, *refs):
    mine_ref, other_ref, gh_ref, wt_ref, bt_ref, w_ref, e_ref, m_ref = refs[:8]
    gc_ref, out_refs, whole = refs[8], refs[9:-1], refs[-1]
    px = mine_ref.shape[0]
    rep = lax.axis_index("rep")
    whole[pl.ds(pl.multiple_of(rep * px, px), px), :] = mine_ref[...]
    whole[pl.ds(pl.multiple_of((1 - rep) * px, px), px), :] = other_ref[...]
    w_half = w_ref[...]
    wide = 2
    bias = jnp.concatenate([bt_ref[...]] * wide, axis=1)
    width = wide * LANES
    for g in range(mine_ref.shape[1] // width):
        cut = slice(g * width, (g + 1) * width)
        pre = jnp.dot(wt_ref[...], whole[:, cut], preferred_element_type=F32) + bias
        grad = (gh_ref[:, cut] * gelu_slope(pre)).astype(BF16)
        gc_ref[:, cut] = jnp.dot(w_half, grad, preferred_element_type=F32).astype(BF16)
    send(rows, cols, slots, pieces, starts, counts, gc_ref, e_ref, m_ref, out_refs)


def send(rows, cols, slots, pieces, starts, counts, gc_ref, e_ref, m_ref, out_refs):
    per = LANES // slots
    wide = cols // per
    strip_at, sub_at = lax.axis_index("strip"), lax.axis_index("sub")
    lane = lax.broadcasted_iota(jnp.int32, (1, LANES), 1) // slots
    for (qz, qx), start, count, ref in zip(pieces, starts, counts, out_refs):
        r0 = 0 if qz is None else facing(qz, rows, strip_at)
        tail = None if qx is None else (sub_at + qx) % 2 == 0
        half = 0 if qx is None else jnp.where(tail, (cols - H) // per, 0)
        shift = 0 if qx is None else jnp.where(tail, (cols - H) % per, 0)
        i = 0
        for r in range(rows if qz is None else H):
            for h in range(wide if qx is None else 1):
                g = (r0 + r) * wide + half + h
                e, m = e_ref[pl.ds(g, 1), :], m_ref[pl.ds(g, 1), :]
                here = (e >= start) & (e < start + count)
                to = jnp.where(here, (lane - shift) * slots + m, -1)
                at = g * LANES
                at = at if isinstance(at, int) else pl.multiple_of(at, LANES)
                ref[:, i * LANES : (i + 1) * LANES] = lax.dot_general(
                    gc_ref[:, pl.ds(at, LANES)], hot(to), NT, preferred_element_type=F32
                ).astype(BF16)
                i += 1


def own_kernel(px, n, slots, gc_ref, e_ref, tgt_t, src_t, sg_ref, own_ref, pw, s32):
    ext_pad = tgt_t.shape[1]
    pitch = px + 1
    inv_root = 1.0 / math.sqrt(tgt_t.shape[2])
    tiles = ext_pad // LANES
    per = LANES // slots
    for b in range(n):
        g = b // per
        gc = gc_ref[:, g * LANES : (g + 1) * LANES]
        for t in range(tiles):
            pw[t, b * pitch : b * pitch + px, :] = lax.dot_general(
                gc, pick_hot(e_ref, b, slots, t), NT, preferred_element_type=F32
            )

    def per_pixel(p):
        tp = tgt_t[p]
        sg = jnp.zeros((n, tp.shape[1]), F32)
        for t in range(tiles):
            w = pw[t, pl.ds(p, n, stride=pitch), :].astype(BF16)
            sg += jnp.dot(w, tp[t * LANES : (t + 1) * LANES, :], preferred_element_type=F32)
            if t == 0:
                own_ref[p] = lax.dot_general(
                    w[:, :n], src_t[p], TN, preferred_element_type=F32
                )
        s32[pl.ds(p, n, stride=pitch), :] = sg * inv_root

    loop(px, per_pixel, 8)

    def narrow(i):
        sg_ref[pl.ds(pl.multiple_of(i * px, px), px), :] = s32[pl.ds(i * pitch, px), :].astype(BF16)

    loop(n, narrow)


def halo_kernel(px, starts, *refs):
    k = len(starts)
    src_refs, out, s32 = refs[:k], refs[k], refs[k + 1]
    pitch = px + 1
    for start, ref in zip(starts, src_refs):
        widen(s32, start, ref, px, pitch)
    last = starts[-1] + src_refs[-1].shape[0] // px
    clear(s32, last, out.shape[1], px, pitch)

    def turn(p):
        out[p] = s32[pl.ds(p, out.shape[1], stride=pitch), :].astype(BF16)

    loop(px, turn)


def total_kernel(px, n, slots, widths, own_ref, halo_t, *refs):
    k = len(widths)
    msg_refs, tg_ref, pw, t32 = refs[:k], refs[k], refs[k + 1], refs[k + 2]
    pitch = px + 1
    inv_root = 1.0 / math.sqrt(own_ref.shape[2])
    at = 0
    for width, ref in zip(widths, msg_refs):
        for g in range(ref.shape[1] // LANES):
            block = ref[:, g * LANES : (g + 1) * LANES].astype(F32)
            for j in range(width):
                turned = block if j == 0 else pltpu.roll(block, LANES - j * slots, 1)
                pw[at * pitch : at * pitch + px, :] = turned
                at += 1
    clear(pw, at, halo_t.shape[1], px, pitch)

    def per_pixel(p):
        w = pw[pl.ds(p, halo_t.shape[1], stride=pitch), :]
        tg = own_ref[p] + lax.dot_general(
            w[:, :n].astype(BF16), halo_t[p], TN, preferred_element_type=F32
        )
        t32[pl.ds(p, n, stride=pitch), :] = tg * inv_root

    loop(px, per_pixel, 8)

    def narrow(i):
        tg_ref[pl.ds(pl.multiple_of(i * px, px), px), :] = t32[pl.ds(i * pitch, px), :].astype(BF16)

    loop(n, narrow)


VM = pl.BlockSpec(memory_space=pltpu.VMEM)
HB = pl.BlockSpec(memory_space=pltpu.HBM)


def call(kernel, outs, scratch, args, us=2.0, far=0, sems=0, limit=24):
    return pl.pallas_call(
        kernel,
        out_shape=[jax.ShapeDtypeStruct(s, d) for s, d in outs],
        in_specs=[HB] * far + [VM] * (len(args) - far),
        out_specs=[VM] * len(outs),
        scratch_shapes=[pltpu.VMEM(s, d) for s, d in scratch]
        + ([pltpu.VMEM(x.shape, x.dtype) for x in args[:far]] if far else [])
        + ([pltpu.SemaphoreType.DMA((sems,))] if far else []),
        compiler_params=pltpu.CompilerParams(vmem_limit_bytes=limit * 2**20),
        cost_estimate=pl.CostEstimate(
            flops=0, bytes_accessed=int(us * 3 * 10**6), transcendentals=0
        ),
    )(*args)


def shards(source, target, target_ids, out_grad, w_in, b_in, w_out):
    rows, cols, px, channels = source.shape
    picks = target_ids.shape[2]
    n = rows * cols
    pitch = px + 1
    slots = 1 << (picks - 1).bit_length()
    per = LANES // slots
    groups = n // per
    assert n <= slots and cols % per == 0 and H <= per and groups * per == n
    pieces, base, ext = plan(rows, cols)
    ext_pad = -(-ext // LANES) * LANES

    shapes = [
        (rows if qz is None else H, cols if qx is None else H, px, channels) for qz, qx in pieces
    ]

    hidden = w_in.shape[1]
    outs = [(s, BF16) for s in shapes] * 2 + [
        ((px, n, channels), BF16),
        ((px, n, channels), BF16),
        ((hidden, n * slots), F32),
        ((hidden, 2 * px), BF16),
        ((px, hidden), BF16),
        ((hidden, LANES), F32),
        ((groups, LANES), jnp.int32),
        ((groups, LANES), jnp.int32),
    ]
    args = (
        source,
        target,
        jnp.swapaxes(out_grad, 1, 2),
        target_ids.reshape(n, picks),
        w_in,
        b_in.reshape(1, hidden),
        w_out,
    )
    args = tuple(pltpu.with_memory_space_constraint(a, pltpu.HBM) for a in args)
    made = call(
        partial(head_kernel, base, pieces, rows, cols, slots),
        outs,
        [((n * pitch, channels), F32)] * 2
        + [((n * (slots + 1), out_grad.shape[3]), F32), ((n, LANES), jnp.int32)],
        args,
        far=len(args),
        sems=len(args) + 2 * len(pieces),
        limit=24,
    )
    k = len(pieces)
    src_t, own_t, grad_hidden, w_t, w_half, b_t, e_ids, m_ids = made[2 * k :]

    def halo_of(slabs):
        got = []
        for x, (qz, qx) in zip(slabs, pieces):
            got.append(swap(x, qz, qx).reshape(-1, channels))
        return got

    tgt_halo = halo_of(made[:k])
    src_halo = halo_of(made[k : 2 * k])
    starts = [base[q] for q in pieces]
    counts = [h.shape[0] // px for h in tgt_halo]
    costs, tgt_t = call(
        partial(corr_kernel, px, n, ext, starts, slots),
        [((px, n * slots), BF16), ((px, ext_pad, channels), BF16)],
        [
            (((ext_pad - n) * pitch, channels), F32),
            ((ext_pad // LANES, n * pitch, LANES), F32),
        ],
        (own_t, src_t, e_ids, *tgt_halo),
        us=3,
    )
    reps = lax.axis_size("rep")
    other = lax.ppermute(costs, "rep", [(i, reps - 1 - i) for i in range(reps)])
    lanes = [
        (rows if qz is None else H) * (cols // per if qx is None else 1) * LANES
        for qz, qx in pieces
    ]
    gc, *sent = call(
        partial(decoder_kernel, rows, cols, slots, pieces, starts, counts),
        [((px, n * slots), BF16)] + [((px, w), BF16) for w in lanes],
        [((2 * px, n * slots), BF16)],
        (costs, other, grad_hidden, w_t, b_t, w_half, e_ids, m_ids),
        us=3,
    )
    got = []
    for x, (qz, qx) in zip(sent, pieces):
        got.append(swap(x, qz, qx))
    sg, own = call(
        partial(own_kernel, px, n, slots),
        [((n * px, channels), BF16), ((px, n, channels), F32)],
        [((ext_pad // LANES, n * pitch, LANES), F32), ((n * pitch, channels), F32)],
        (gc, e_ids, tgt_t, src_t),
        us=4,
    )
    halo_pad = -(-(ext - n) // 16) * 16
    (halo_t,) = call(
        partial(halo_kernel, px, [s - n for s in starts]),
        [((px, halo_pad, channels), BF16)],
        [((halo_pad * pitch, channels), F32)],
        tuple(src_halo),
        us=1,
    )
    (tg,) = call(
        partial(total_kernel, px, n, slots, [per if qx is None else H for _, qx in pieces]),
        [((n * px, channels), BF16)],
        [((halo_pad * pitch, LANES), F32), ((n * pitch, channels), F32)],
        (own, halo_t, *got),
        us=3,
    )
    return sg.reshape(source.shape), tg.reshape(source.shape)


def solution(mesh):
    cells = P(("groups", "strip"), "sub", "rep", None)
    placed = (
        cells,
        cells,
        P(("groups", "strip"), "sub", None),
        P(("groups", "strip"), "sub", None, None),
        P(),
        P(),
        P(),
    )

    return jax.shard_map(
        shards, mesh=mesh, in_specs=placed, out_specs=(cells, cells), check_vma=False
    )
```

```python
from functools import partial
import math

import jax
import jax.numpy as jnp
from jax import lax
from jax.experimental import pallas as pl
from jax.experimental.pallas import tpu as pltpu
from jax.sharding import PartitionSpec as P

H = 3
LANES = 128
NT = (((1,), (1,)), ((), ()))
TN = (((0,), (0,)), ((), ()))
F32 = jnp.float32
BF16 = jnp.bfloat16


def mate(i, q, n):
    j = i + 1 if (i + q) % 2 == 0 else i - 1
    return j if 0 <= j < n else None


def turns(n):
    return [q for q in (0, 1) if any(mate(i, q, n) is not None for i in range(n))]


def swap(x, qz, qx):
    strips, subs = lax.axis_size("strip"), lax.axis_size("sub")
    pairs = []
    for s in range(strips):
        for u in range(subs):
            t = s if qz is None else mate(s, qz, strips)
            v = u if qx is None else mate(u, qx, subs)
            if t is not None and v is not None:
                pairs.append((s * subs + u, t * subs + v))
    return lax.ppermute(x, ("strip", "sub"), pairs)


def plan(rows, cols):
    zs, xs = turns(lax.axis_size("strip")), turns(lax.axis_size("sub"))
    pieces = [(q, None) for q in zs]
    pieces += [(None, r) for r in xs]
    pieces += [(q, r) for q in zs for r in xs]
    base, at = {(None, None): 0}, rows * cols
    for qz, qx in pieces:
        base[qz, qx] = at
        at += (rows if qz is None else H) * (cols if qx is None else H)
    return pieces, base, at


def facing(q, extent, index):
    return jnp.where((index + q) % 2 == 0, extent - H, 0)


def scale_of(n):
    assert n & (n - 1) == 0
    return n.bit_length() - 1


def places(ids, base, rows, cols):
    total_cols = cols * lax.axis_size("sub")
    strip_at, sub_at = lax.axis_index("strip"), lax.axis_index("sub")

    def split(d, extent, index):
        side = jnp.where(d < 0, -1, jnp.where(d >= extent, 1, 0))
        inner = jnp.where(side < 0, d + H, jnp.where(side > 0, d - extent, d))
        ahead = jnp.where(index % 2 == 0, 1, -1)
        turn = jnp.where(side == 0, -1, jnp.where(side == ahead, 0, 1))
        return turn, inner

    row = lax.shift_right_arithmetic(ids, jnp.int32(scale_of(total_cols)))
    col = ids & (total_cols - 1)
    tz, dr = split(row - strip_at * rows, rows, strip_at)
    tx, dc = split(col - sub_at * cols, cols, sub_at)
    where_to = jnp.full(ids.shape, -1, jnp.int32)
    for (qz, qx), start in base.items():
        here = (tz == (-1 if qz is None else qz)) & (tx == (-1 if qx is None else qx))
        width = cols if qx is None else H
        where_to = jnp.where(here, start + dr * width + dc, where_to)
    assert scale_of(rows) + scale_of(cols) >= 0
    return where_to, (row & (rows - 1)) * cols + (col & (cols - 1))


def cuts(pieces, rows, cols, x_ref, out_refs, sems, at):
    strip_at, sub_at = lax.axis_index("strip"), lax.axis_index("sub")
    copies = []
    for i, ((qz, qx), ref) in enumerate(zip(pieces, out_refs)):
        r = pl.ds(0, rows) if qz is None else pl.ds(facing(qz, rows, strip_at), H)
        c = pl.ds(0, cols) if qx is None else pl.ds(facing(qx, cols, sub_at), H)
        copies.append(pltpu.make_async_copy(x_ref.at[r, c], ref, sems.at[at + i]))
    return copies


def loop(count, body, most=4):
    step = max(d for d in range(1, most + 1) if count % d == 0) if count else 1

    def run(i, _):
        body(i)
        return 0

    lax.fori_loop(0, count, run, 0, unroll=step)


def widen(dst, at, src_ref, px, pitch):
    def body(i):
        rows = src_ref[pl.ds(pl.multiple_of(i * px, px), px), :]
        dst[pl.ds((at + i) * pitch, px), :] = rows.astype(F32)

    loop(src_ref.shape[0] // px, body)


def clear(dst, at, end, px, pitch):
    def body(i):
        dst[pl.ds((at + i) * pitch, px), :] = jnp.zeros((px, dst.shape[1]), F32)

    loop(end - at, body)


def hot(row, tile=0):
    e = lax.broadcasted_iota(jnp.int32, (LANES, LANES), 0) + tile * LANES
    return (e == row).astype(F32).astype(BF16)


def pick_hot(e_ref, b, slots, tile):
    group, j = divmod(b, LANES // slots)
    lane = lax.broadcasted_iota(jnp.int32, (1, LANES), 1) // slots
    return hot(jnp.where(lane == j, e_ref[group : group + 1, :], -1), tile)


def cut_kernel(pieces, rows, cols, x_ref, *refs):
    copies = cuts(pieces, rows, cols, x_ref, refs[:-1], refs[-1], 0)
    for copy in copies:
        copy.start()
    for copy in copies:
        copy.wait()


def slotted(x, out_ref, table, slots):
    n, picks = x.shape
    per = LANES // slots
    table[...] = jnp.full(table.shape, -1, jnp.int32)
    table[:, :picks] = x
    lane = lax.broadcasted_iota(jnp.int32, (n // per, LANES), 1) // slots
    acc = jnp.full((n // per, LANES), -1, jnp.int32)
    for j in range(per):
        rows = table[pl.ds(j, n // per, stride=per), :]
        acc = jnp.where(lane == j, rows if j == 0 else pltpu.roll(rows, j * slots, 1), acc)
    out_ref[...] = acc


def head_kernel(base, pieces, rows, cols, slots, *refs):
    k = len(pieces)
    far, rest = refs[:7], refs[7:]
    src_slabs, outs, rest = rest[:k], rest[k : k + 8], rest[k + 8 :]
    src_t, tgt_t, gh_ref, wt_ref, wh_ref, bt_ref, e_ref, m_ref = outs
    (s32, t32, og, table), near, sems = rest[:4], rest[4:-1], rest[-1]
    src_ref, tgt_ref, og_ref, ids_ref, w_in_ref, b_ref, w_out_ref = near
    fetches = [pltpu.make_async_copy(f, v, sems.at[i]) for i, (f, v) in enumerate(zip(far, near))]
    slabs = cuts(pieces, rows, cols, far[0], src_slabs, sems, 7)
    for copy in fetches[2:] + fetches[:2] + slabs:
        copy.start()
    px, n, _ = src_t.shape
    pitch = px + 1
    for fetch in fetches[2:]:
        fetch.wait()
    e_at, m_at = places(ids_ref[...], base, rows, cols)
    slotted(e_at, e_ref, table, slots)
    slotted(m_at, m_ref, table, slots)
    wt_ref[...] = w_in_ref[...].T
    rep = lax.axis_index("rep")
    wh_ref[...] = w_in_ref[pl.ds(pl.multiple_of(rep * px, px), px), :]
    bt_ref[...] = jnp.broadcast_to(b_ref[...], (LANES, b_ref.shape[1])).T
    picks = og_ref.shape[1]
    og[...] = jnp.zeros_like(og)
    for r in range(rows):
        for pick in range(picks):
            at = r * cols * (slots + 1) + pick
            og[pl.ds(at, cols, stride=slots + 1), :] = og_ref[r, pick].astype(F32)
    per = LANES // slots
    for g in range(n // per):
        block = jnp.concatenate(
            [og[b * (slots + 1) : b * (slots + 1) + slots, :] for b in range(g * per, (g + 1) * per)]
        ).astype(BF16)
        gh_ref[:, g * LANES : (g + 1) * LANES] = lax.dot_general(
            w_out_ref[...], block, NT, preferred_element_type=F32
        )
    for fetch in fetches[:2]:
        fetch.wait()
    for dst, src in ((s32, src_ref), (t32, tgt_ref)):

        def body(i, dst=dst, src=src):
            rows_of = src[i // cols, lax.rem(i, cols)]
            dst[pl.ds(i * pitch, px), :] = rows_of.astype(F32)

        loop(n, body)

    def turn(p):
        src_t[p] = s32[pl.ds(p, n, stride=pitch), :].astype(BF16)
        tgt_t[p] = t32[pl.ds(p, n, stride=pitch), :].astype(BF16)

    loop(px, turn)
    for copy in slabs:
        copy.wait()


def corr_kernel(px, n, ext, starts, slots, *refs):
    k = len(starts)
    own_t, src_t, e_ref, tgt_refs = refs[0], refs[1], refs[2], refs[3 : 3 + k]
    costs_ref, tgt_t, t32, corr = refs[3 + k :]
    ext_pad = tgt_t.shape[1]
    pitch = px + 1
    inv_root = 1.0 / math.sqrt(tgt_t.shape[2])
    for start, ref in zip(starts, tgt_refs):
        widen(t32, start - n, ref, px, pitch)
    clear(t32, ext - n, ext_pad - n, px, pitch)

    def per_pixel(p):
        tp = t32[pl.ds(p, ext_pad - n, stride=pitch), :].astype(BF16)
        tp = jnp.concatenate([own_t[p], tp], axis=0)
        tgt_t[p] = tp
        c = lax.dot_general(src_t[p], tp, NT, preferred_element_type=F32) * inv_root
        for t in range(ext_pad // LANES):
            corr[t, pl.ds(p, n, stride=pitch), :] = c[:, t * LANES : (t + 1) * LANES]

    loop(px, per_pixel, 8)
    per = LANES // slots
    for g in range(n // per):
        acc = jnp.zeros((px, LANES), F32)
        for j in range(per):
            b = g * per + j
            for t in range(ext_pad // LANES):
                acc += jnp.dot(
                    corr[t, b * pitch : b * pitch + px, :].astype(BF16),
                    pick_hot(e_ref, b, slots, t),
                    preferred_element_type=F32,
                )
        costs_ref[:, g * LANES : (g + 1) * LANES] = acc.astype(BF16)


def gelu_slope(x):
    c = math.sqrt(2.0 / math.pi)
    x2 = x * x
    th = jnp.tanh(c * (x + 0.044715 * (x2 * x)))
    inner = c * (1.0 + (3.0 * 0.044715) * x2)
    return 0.5 * (1.0 + th) + (0.5 * x) * ((1.0 - th) * (1.0 + th)) * inner


def decoder_kernel(rows, cols, slots, pieces, starts, counts, *refs):
    mine_ref, other_ref, gh_ref, wt_ref, bt_ref, w_ref, e_ref, m_ref = refs[:8]
    gc_ref, out_refs, whole = refs[8], refs[9:-1], refs[-1]
    px = mine_ref.shape[0]
    rep = lax.axis_index("rep")
    whole[pl.ds(pl.multiple_of(rep * px, px), px), :] = mine_ref[...]
    whole[pl.ds(pl.multiple_of((1 - rep) * px, px), px), :] = other_ref[...]
    w_half = w_ref[...]
    wide = 2
    bias = jnp.concatenate([bt_ref[...]] * wide, axis=1)
    width = wide * LANES
    for g in range(mine_ref.shape[1] // width):
        cut = slice(g * width, (g + 1) * width)
        pre = jnp.dot(wt_ref[...], whole[:, cut], preferred_element_type=F32) + bias
        grad = (gh_ref[:, cut] * gelu_slope(pre)).astype(BF16)
        gc_ref[:, cut] = jnp.dot(w_half, grad, preferred_element_type=F32).astype(BF16)
    send(rows, cols, slots, pieces, starts, counts, gc_ref, e_ref, m_ref, out_refs)


def send(rows, cols, slots, pieces, starts, counts, gc_ref, e_ref, m_ref, out_refs):
    per = LANES // slots
    wide = cols // per
    strip_at, sub_at = lax.axis_index("strip"), lax.axis_index("sub")
    lane = lax.broadcasted_iota(jnp.int32, (1, LANES), 1) // slots
    for (qz, qx), start, count, ref in zip(pieces, starts, counts, out_refs):
        r0 = 0 if qz is None else facing(qz, rows, strip_at)
        tail = None if qx is None else (sub_at + qx) % 2 == 0
        half = 0 if qx is None else jnp.where(tail, (cols - H) // per, 0)
        shift = 0 if qx is None else jnp.where(tail, (cols - H) % per, 0)
        i = 0
        for r in range(rows if qz is None else H):
            for h in range(wide if qx is None else 1):
                g = (r0 + r) * wide + half + h
                e, m = e_ref[pl.ds(g, 1), :], m_ref[pl.ds(g, 1), :]
                here = (e >= start) & (e < start + count)
                to = jnp.where(here, (lane - shift) * slots + m, -1)
                at = g * LANES
                at = at if isinstance(at, int) else pl.multiple_of(at, LANES)
                ref[:, i * LANES : (i + 1) * LANES] = lax.dot_general(
                    gc_ref[:, pl.ds(at, LANES)], hot(to), NT, preferred_element_type=F32
                ).astype(BF16)
                i += 1


def own_kernel(px, n, slots, gc_ref, e_ref, tgt_t, src_t, sg_ref, own_ref, pw, s32):
    ext_pad = tgt_t.shape[1]
    pitch = px + 1
    inv_root = 1.0 / math.sqrt(tgt_t.shape[2])
    tiles = ext_pad // LANES
    per = LANES // slots
    for b in range(n):
        g = b // per
        gc = gc_ref[:, g * LANES : (g + 1) * LANES]
        for t in range(tiles):
            pw[t, b * pitch : b * pitch + px, :] = lax.dot_general(
                gc, pick_hot(e_ref, b, slots, t), NT, preferred_element_type=F32
            )

    def per_pixel(p):
        tp = tgt_t[p]
        sg = jnp.zeros((n, tp.shape[1]), F32)
        for t in range(tiles):
            w = pw[t, pl.ds(p, n, stride=pitch), :].astype(BF16)
            sg += jnp.dot(w, tp[t * LANES : (t + 1) * LANES, :], preferred_element_type=F32)
            if t == 0:
                own_ref[p] = lax.dot_general(
                    w[:, :n], src_t[p], TN, preferred_element_type=F32
                )
        s32[pl.ds(p, n, stride=pitch), :] = sg * inv_root

    loop(px, per_pixel, 8)

    def narrow(i):
        sg_ref[pl.ds(pl.multiple_of(i * px, px), px), :] = s32[pl.ds(i * pitch, px), :].astype(BF16)

    loop(n, narrow)


def halo_kernel(px, starts, *refs):
    k = len(starts)
    src_refs, out, s32 = refs[:k], refs[k], refs[k + 1]
    pitch = px + 1
    for start, ref in zip(starts, src_refs):
        widen(s32, start, ref, px, pitch)
    last = starts[-1] + src_refs[-1].shape[0] // px
    clear(s32, last, out.shape[1], px, pitch)

    def turn(p):
        out[p] = s32[pl.ds(p, out.shape[1], stride=pitch), :].astype(BF16)

    loop(px, turn)


def total_kernel(px, n, slots, widths, own_ref, halo_t, *refs):
    k = len(widths)
    msg_refs, tg_ref, pw, t32 = refs[:k], refs[k], refs[k + 1], refs[k + 2]
    pitch = px + 1
    inv_root = 1.0 / math.sqrt(own_ref.shape[2])
    at = 0
    for width, ref in zip(widths, msg_refs):
        for g in range(ref.shape[1] // LANES):
            block = ref[:, g * LANES : (g + 1) * LANES].astype(F32)
            for j in range(width):
                turned = block if j == 0 else pltpu.roll(block, LANES - j * slots, 1)
                pw[at * pitch : at * pitch + px, :] = turned
                at += 1
    clear(pw, at, halo_t.shape[1], px, pitch)

    def per_pixel(p):
        w = pw[pl.ds(p, halo_t.shape[1], stride=pitch), :]
        tg = own_ref[p] + lax.dot_general(
            w[:, :n].astype(BF16), halo_t[p], TN, preferred_element_type=F32
        )
        t32[pl.ds(p, n, stride=pitch), :] = tg * inv_root

    loop(px, per_pixel, 8)

    def narrow(i):
        tg_ref[pl.ds(pl.multiple_of(i * px, px), px), :] = t32[pl.ds(i * pitch, px), :].astype(BF16)

    loop(n, narrow)


VM = pl.BlockSpec(memory_space=pltpu.VMEM)
HB = pl.BlockSpec(memory_space=pltpu.HBM)


def call(kernel, outs, scratch, args, us=2.0, far=0, sems=0, limit=24):
    return pl.pallas_call(
        kernel,
        out_shape=[jax.ShapeDtypeStruct(s, d) for s, d in outs],
        in_specs=[HB] * far + [VM] * (len(args) - far),
        out_specs=[VM] * len(outs),
        scratch_shapes=[pltpu.VMEM(s, d) for s, d in scratch]
        + ([pltpu.VMEM(x.shape, x.dtype) for x in args[:far]] if far else [])
        + ([pltpu.SemaphoreType.DMA((sems,))] if far else []),
        compiler_params=pltpu.CompilerParams(vmem_limit_bytes=limit * 2**20),
        cost_estimate=pl.CostEstimate(
            flops=0, bytes_accessed=int(us * 3 * 10**6), transcendentals=0
        ),
    )(*args)


def shards(source, target, target_ids, out_grad, w_in, b_in, w_out):
    rows, cols, px, channels = source.shape
    picks = target_ids.shape[2]
    n = rows * cols
    pitch = px + 1
    slots = 1 << (picks - 1).bit_length()
    per = LANES // slots
    groups = n // per
    assert n <= slots and cols % per == 0 and H <= per and groups * per == n
    pieces, base, ext = plan(rows, cols)
    ext_pad = -(-ext // LANES) * LANES

    shapes = [
        (rows if qz is None else H, cols if qx is None else H, px, channels) for qz, qx in pieces
    ]

    hidden = w_in.shape[1]
    outs = [(s, BF16) for s in shapes] + [
        ((px, n, channels), BF16),
        ((px, n, channels), BF16),
        ((hidden, n * slots), F32),
        ((hidden, 2 * px), BF16),
        ((px, hidden), BF16),
        ((hidden, LANES), F32),
        ((groups, LANES), jnp.int32),
        ((groups, LANES), jnp.int32),
    ]
    args = (
        source,
        target,
        jnp.swapaxes(out_grad, 1, 2),
        target_ids.reshape(n, picks),
        w_in,
        b_in.reshape(1, hidden),
        w_out,
    )
    args = tuple(pltpu.with_memory_space_constraint(a, pltpu.HBM) for a in args)
    made = call(
        partial(head_kernel, base, pieces, rows, cols, slots),
        outs,
        [((n * pitch, channels), F32)] * 2
        + [((n * (slots + 1), out_grad.shape[3]), F32), ((n, LANES), jnp.int32)],
        args,
        far=len(args),
        sems=len(args) + len(pieces),
        limit=24,
    )
    k = len(pieces)
    src_t, own_t, grad_hidden, w_t, w_half, b_t, e_ids, m_ids = made[k:]
    cut_t = pl.pallas_call(
        partial(cut_kernel, pieces, rows, cols),
        name="cut",
        out_shape=[jax.ShapeDtypeStruct(s, BF16) for s in shapes],
        in_specs=[HB],
        out_specs=[VM] * k,
        scratch_shapes=[pltpu.SemaphoreType.DMA((k,))],
        compiler_params=pltpu.CompilerParams(vmem_limit_bytes=4 * 2**20),
    )(args[1])

    def halo_of(slabs):
        got = []
        for x, (qz, qx) in zip(slabs, pieces):
            got.append(swap(x, qz, qx).reshape(-1, channels))
        return got

    tgt_halo = halo_of(cut_t)
    src_halo = halo_of(made[:k])
    starts = [base[q] for q in pieces]
    counts = [h.shape[0] // px for h in tgt_halo]
    costs, tgt_t = call(
        partial(corr_kernel, px, n, ext, starts, slots),
        [((px, n * slots), BF16), ((px, ext_pad, channels), BF16)],
        [
            (((ext_pad - n) * pitch, channels), F32),
            ((ext_pad // LANES, n * pitch, LANES), F32),
        ],
        (own_t, src_t, e_ids, *tgt_halo),
        us=3,
    )
    reps = lax.axis_size("rep")
    other = lax.ppermute(costs, "rep", [(i, reps - 1 - i) for i in range(reps)])
    lanes = [
        (rows if qz is None else H) * (cols // per if qx is None else 1) * LANES
        for qz, qx in pieces
    ]
    gc, *sent = call(
        partial(decoder_kernel, rows, cols, slots, pieces, starts, counts),
        [((px, n * slots), BF16)] + [((px, w), BF16) for w in lanes],
        [((2 * px, n * slots), BF16)],
        (costs, other, grad_hidden, w_t, b_t, w_half, e_ids, m_ids),
        us=3,
    )
    got = []
    for x, (qz, qx) in zip(sent, pieces):
        got.append(swap(x, qz, qx))
    sg, own = call(
        partial(own_kernel, px, n, slots),
        [((n * px, channels), BF16), ((px, n, channels), F32)],
        [((ext_pad // LANES, n * pitch, LANES), F32), ((n * pitch, channels), F32)],
        (gc, e_ids, tgt_t, src_t),
        us=4,
    )
    halo_pad = -(-(ext - n) // 16) * 16
    (halo_t,) = call(
        partial(halo_kernel, px, [s - n for s in starts]),
        [((px, halo_pad, channels), BF16)],
        [((halo_pad * pitch, channels), F32)],
        tuple(src_halo),
        us=1,
    )
    (tg,) = call(
        partial(total_kernel, px, n, slots, [per if qx is None else H for _, qx in pieces]),
        [((n * px, channels), BF16)],
        [((halo_pad * pitch, LANES), F32), ((n * pitch, channels), F32)],
        (own, halo_t, *got),
        us=3,
    )
    return sg.reshape(source.shape), tg.reshape(source.shape)


def solution(mesh):
    cells = P(("groups", "strip"), "sub", "rep", None)
    placed = (
        cells,
        cells,
        P(("groups", "strip"), "sub", None),
        P(("groups", "strip"), "sub", None, None),
        P(),
        P(),
        P(),
    )

    return jax.shard_map(
        shards, mesh=mesh, in_specs=placed, out_specs=(cells, cells), check_vma=False
    )
```

```python
from functools import partial
import math

import jax
import jax.numpy as jnp
from jax import lax
from jax.experimental import pallas as pl
from jax.experimental.pallas import tpu as pltpu
from jax.sharding import PartitionSpec as P

H = 3
LANES = 128
NT = (((1,), (1,)), ((), ()))
TN = (((0,), (0,)), ((), ()))
F32 = jnp.float32
BF16 = jnp.bfloat16


def mate(i, q, n):
    j = i + 1 if (i + q) % 2 == 0 else i - 1
    return j if 0 <= j < n else None


def turns(n):
    return [q for q in (0, 1) if any(mate(i, q, n) is not None for i in range(n))]


def swap(x, qz, qx):
    strips, subs = lax.axis_size("strip"), lax.axis_size("sub")
    pairs = []
    for s in range(strips):
        for u in range(subs):
            t = s if qz is None else mate(s, qz, strips)
            v = u if qx is None else mate(u, qx, subs)
            if t is not None and v is not None:
                pairs.append((s * subs + u, t * subs + v))
    return lax.ppermute(x, ("strip", "sub"), pairs)


def plan(rows, cols):
    zs, xs = turns(lax.axis_size("strip")), turns(lax.axis_size("sub"))
    pieces = [(q, None) for q in zs]
    pieces += [(None, r) for r in xs]
    pieces += [(q, r) for q in zs for r in xs]
    base, at = {(None, None): 0}, rows * cols
    for qz, qx in pieces:
        base[qz, qx] = at
        at += (rows if qz is None else H) * (cols if qx is None else H)
    return pieces, base, at


def facing(q, extent, index):
    return jnp.where((index + q) % 2 == 0, extent - H, 0)


def scale_of(n):
    assert n & (n - 1) == 0
    return n.bit_length() - 1


def places(ids, base, rows, cols):
    total_cols = cols * lax.axis_size("sub")
    strip_at, sub_at = lax.axis_index("strip"), lax.axis_index("sub")

    def split(d, extent, index):
        side = jnp.where(d < 0, -1, jnp.where(d >= extent, 1, 0))
        inner = jnp.where(side < 0, d + H, jnp.where(side > 0, d - extent, d))
        ahead = jnp.where(index % 2 == 0, 1, -1)
        turn = jnp.where(side == 0, -1, jnp.where(side == ahead, 0, 1))
        return turn, inner

    row = lax.shift_right_arithmetic(ids, jnp.int32(scale_of(total_cols)))
    col = ids & (total_cols - 1)
    tz, dr = split(row - strip_at * rows, rows, strip_at)
    tx, dc = split(col - sub_at * cols, cols, sub_at)
    where_to = jnp.full(ids.shape, -1, jnp.int32)
    for (qz, qx), start in base.items():
        here = (tz == (-1 if qz is None else qz)) & (tx == (-1 if qx is None else qx))
        width = cols if qx is None else H
        where_to = jnp.where(here, start + dr * width + dc, where_to)
    assert scale_of(rows) + scale_of(cols) >= 0
    return where_to, (row & (rows - 1)) * cols + (col & (cols - 1))


def cuts(pieces, rows, cols, x_ref, out_refs, sems, at):
    strip_at, sub_at = lax.axis_index("strip"), lax.axis_index("sub")
    copies = []
    for i, ((qz, qx), ref) in enumerate(zip(pieces, out_refs)):
        r = pl.ds(0, rows) if qz is None else pl.ds(facing(qz, rows, strip_at), H)
        c = pl.ds(0, cols) if qx is None else pl.ds(facing(qx, cols, sub_at), H)
        copies.append(pltpu.make_async_copy(x_ref.at[r, c], ref, sems.at[at + i]))
    return copies


def loop(count, body, most=4):
    step = max(d for d in range(1, most + 1) if count % d == 0) if count else 1

    def run(i, _):
        body(i)
        return 0

    lax.fori_loop(0, count, run, 0, unroll=step)


def widen(dst, at, src_ref, px, pitch):
    def body(i):
        rows = src_ref[pl.ds(pl.multiple_of(i * px, px), px), :]
        dst[pl.ds((at + i) * pitch, px), :] = rows.astype(F32)

    loop(src_ref.shape[0] // px, body)


def clear(dst, at, end, px, pitch):
    def body(i):
        dst[pl.ds((at + i) * pitch, px), :] = jnp.zeros((px, dst.shape[1]), F32)

    loop(end - at, body)


def hot(row, tile=0):
    e = lax.broadcasted_iota(jnp.int32, (LANES, LANES), 0) + tile * LANES
    return (e == row).astype(F32).astype(BF16)


def pick_hot(e_ref, b, slots, tile):
    group, j = divmod(b, LANES // slots)
    lane = lax.broadcasted_iota(jnp.int32, (1, LANES), 1) // slots
    return hot(jnp.where(lane == j, e_ref[group : group + 1, :], -1), tile)


def cut_kernel(pieces, rows, cols, x_ref, *refs):
    copies = cuts(pieces, rows, cols, x_ref, refs[:-1], refs[-1], 0)
    for copy in copies:
        copy.start()
    for copy in copies:
        copy.wait()


def slotted(x, out_ref, table, slots):
    n, picks = x.shape
    per = LANES // slots
    table[...] = jnp.full(table.shape, -1, jnp.int32)
    table[:, :picks] = x
    lane = lax.broadcasted_iota(jnp.int32, (n // per, LANES), 1) // slots
    acc = jnp.full((n // per, LANES), -1, jnp.int32)
    for j in range(per):
        rows = table[pl.ds(j, n // per, stride=per), :]
        acc = jnp.where(lane == j, rows if j == 0 else pltpu.roll(rows, j * slots, 1), acc)
    out_ref[...] = acc


def head_kernel(base, pieces, rows, cols, slots, *refs):
    k = len(pieces)
    far, rest = refs[:7], refs[7:]
    src_slabs, outs, rest = rest[:k], rest[k : k + 8], rest[k + 8 :]
    src_t, tgt_t, gh_ref, wt_ref, wh_ref, bt_ref, e_ref, m_ref = outs
    (s32, t32, og, table), near, sems = rest[:4], rest[4:-1], rest[-1]
    src_ref, tgt_ref, og_ref, ids_ref, w_in_ref, b_ref, w_out_ref = near
    fetches = [pltpu.make_async_copy(f, v, sems.at[i]) for i, (f, v) in enumerate(zip(far, near))]
    slabs = cuts(pieces, rows, cols, far[0], src_slabs, sems, 7)
    for copy in fetches[2:] + fetches[:2] + slabs:
        copy.start()
    px, n, _ = src_t.shape
    pitch = px + 1
    for fetch in fetches[2:]:
        fetch.wait()
    e_at, m_at = places(ids_ref[...], base, rows, cols)
    slotted(e_at, e_ref, table, slots)
    slotted(m_at, m_ref, table, slots)
    wt_ref[...] = w_in_ref[...].T
    rep = lax.axis_index("rep")
    wh_ref[...] = w_in_ref[pl.ds(pl.multiple_of(rep * px, px), px), :]
    bt_ref[...] = jnp.broadcast_to(b_ref[...], (LANES, b_ref.shape[1])).T
    picks = og_ref.shape[1]
    og[...] = jnp.zeros_like(og)
    for r in range(rows):
        for pick in range(picks):
            at = r * cols * (slots + 1) + pick
            og[pl.ds(at, cols, stride=slots + 1), :] = og_ref[r, pick].astype(F32)
    per = LANES // slots
    for g in range(n // per):
        block = jnp.concatenate(
            [og[b * (slots + 1) : b * (slots + 1) + slots, :] for b in range(g * per, (g + 1) * per)]
        ).astype(BF16)
        gh_ref[:, g * LANES : (g + 1) * LANES] = lax.dot_general(
            w_out_ref[...], block, NT, preferred_element_type=F32
        )
    for fetch in fetches[:2]:
        fetch.wait()
    for dst, src in ((s32, src_ref), (t32, tgt_ref)):

        def body(i, dst=dst, src=src):
            rows_of = src[i // cols, lax.rem(i, cols)]
            dst[pl.ds(i * pitch, px), :] = rows_of.astype(F32)

        loop(n, body, 8)

    def turn(p):
        src_t[p] = s32[pl.ds(p, n, stride=pitch), :].astype(BF16)
        tgt_t[p] = t32[pl.ds(p, n, stride=pitch), :].astype(BF16)

    loop(px, turn, 8)
    for copy in slabs:
        copy.wait()


def corr_kernel(px, n, ext, starts, slots, *refs):
    k = len(starts)
    own_t, src_t, e_ref, tgt_refs = refs[0], refs[1], refs[2], refs[3 : 3 + k]
    costs_ref, tgt_t, hot_ref, t32, corr = refs[3 + k :]
    ext_pad = tgt_t.shape[1]
    tiles = ext_pad // LANES
    pitch = px + 1
    inv_root = 1.0 / math.sqrt(tgt_t.shape[2])
    for start, ref in zip(starts, tgt_refs):
        widen(t32, start - n, ref, px, pitch)
    clear(t32, ext - n, ext_pad - n, px, pitch)

    def per_pixel(p):
        tp = t32[pl.ds(p, ext_pad - n, stride=pitch), :].astype(BF16)
        tp = jnp.concatenate([own_t[p], tp], axis=0)
        tgt_t[p] = tp
        c = lax.dot_general(src_t[p], tp, NT, preferred_element_type=F32) * inv_root
        for t in range(tiles):
            corr[t, pl.ds(p, n, stride=pitch), :] = c[:, t * LANES : (t + 1) * LANES]

    loop(px, per_pixel, px)
    per = LANES // slots
    for g in range(n // per):
        left = []
        for j in range(per):
            b = g * per + j
            for t in range(tiles):
                at = (b * tiles + t) * LANES
                hot_ref[at : at + LANES, :] = pick_hot(e_ref, b, slots, t)
                left.append(corr[t, b * pitch : b * pitch + px, :].astype(BF16))
        high = per * tiles * LANES
        costs_ref[:, g * LANES : (g + 1) * LANES] = jnp.dot(
            jnp.concatenate(left, axis=1),
            hot_ref[g * high : (g + 1) * high, :],
            preferred_element_type=F32,
        ).astype(BF16)


def gelu_slope(x):
    c = math.sqrt(2.0 / math.pi)
    x2 = x * x
    th = jnp.tanh(x * (c + (c * 0.044715) * x2))
    inner = x * (c + (c * 3.0 * 0.044715) * x2)
    return (0.5 + 0.5 * th) * (1.0 + (1.0 - th) * inner)


def decoder_kernel(rows, cols, slots, pieces, starts, counts, *refs):
    mine_ref, other_ref, gh_ref, wt_ref, bt_ref, w_ref, e_ref, m_ref = refs[:8]
    gc_ref, out_refs, whole = refs[8], refs[9:-1], refs[-1]
    px = mine_ref.shape[0]
    rep = lax.axis_index("rep")
    whole[pl.ds(pl.multiple_of(rep * px, px), px), :] = mine_ref[...]
    whole[pl.ds(pl.multiple_of((1 - rep) * px, px), px), :] = other_ref[...]
    w_half = w_ref[...]
    wide = 2
    bias = jnp.concatenate([bt_ref[...]] * wide, axis=1)
    width = wide * LANES
    for g in range(mine_ref.shape[1] // width):
        cut = slice(g * width, (g + 1) * width)
        pre = jnp.dot(wt_ref[...], whole[:, cut], preferred_element_type=F32) + bias
        grad = (gh_ref[:, cut] * gelu_slope(pre)).astype(BF16)
        gc_ref[:, cut] = jnp.dot(w_half, grad, preferred_element_type=F32).astype(BF16)
    send(rows, cols, slots, pieces, starts, counts, gc_ref, e_ref, m_ref, out_refs)


def send(rows, cols, slots, pieces, starts, counts, gc_ref, e_ref, m_ref, out_refs):
    per = LANES // slots
    wide = cols // per
    strip_at, sub_at = lax.axis_index("strip"), lax.axis_index("sub")
    lane = lax.broadcasted_iota(jnp.int32, (1, LANES), 1) // slots
    for (qz, qx), start, count, ref in zip(pieces, starts, counts, out_refs):
        r0 = 0 if qz is None else facing(qz, rows, strip_at)
        tail = None if qx is None else (sub_at + qx) % 2 == 0
        half = 0 if qx is None else jnp.where(tail, (cols - H) // per, 0)
        shift = 0 if qx is None else jnp.where(tail, (cols - H) % per, 0)
        i = 0
        for r in range(rows if qz is None else H):
            for h in range(wide if qx is None else 1):
                g = (r0 + r) * wide + half + h
                e, m = e_ref[pl.ds(g, 1), :], m_ref[pl.ds(g, 1), :]
                here = (e >= start) & (e < start + count)
                to = jnp.where(here, (lane - shift) * slots + m, -1)
                at = g * LANES
                at = at if isinstance(at, int) else pl.multiple_of(at, LANES)
                ref[:, i * LANES : (i + 1) * LANES] = lax.dot_general(
                    gc_ref[:, pl.ds(at, LANES)], hot(to), NT, preferred_element_type=F32
                ).astype(BF16)
                i += 1


def own_kernel(px, n, slots, gc_ref, hot_ref, tgt_t, src_t, sg_ref, own_ref, pw, s32):
    ext_pad = tgt_t.shape[1]
    pitch = px + 1
    inv_root = 1.0 / math.sqrt(tgt_t.shape[2])
    tiles = ext_pad // LANES
    per = LANES // slots
    high = per * tiles * LANES
    for g in range(n // per):
        w = lax.dot_general(
            gc_ref[:, g * LANES : (g + 1) * LANES],
            hot_ref[g * high : (g + 1) * high, :],
            NT,
            preferred_element_type=F32,
        )
        for j in range(per):
            b = g * per + j
            for t in range(tiles):
                at = (j * tiles + t) * LANES
                pw[t, b * pitch : b * pitch + px, :] = w[:, at : at + LANES]

    def per_pixel(p):
        tp = tgt_t[p]
        sg = jnp.zeros((n, tp.shape[1]), F32)
        for t in range(tiles):
            w = pw[t, pl.ds(p, n, stride=pitch), :].astype(BF16)
            sg += jnp.dot(w, tp[t * LANES : (t + 1) * LANES, :], preferred_element_type=F32)
            if t == 0:
                own_ref[p] = lax.dot_general(
                    w[:, :n], src_t[p], TN, preferred_element_type=F32
                )
        s32[pl.ds(p, n, stride=pitch), :] = sg * inv_root

    loop(px, per_pixel, px)

    def narrow(i):
        sg_ref[pl.ds(pl.multiple_of(i * px, px), px), :] = s32[pl.ds(i * pitch, px), :].astype(BF16)

    loop(n, narrow)


def halo_kernel(px, starts, *refs):
    k = len(starts)
    src_refs, out, s32 = refs[:k], refs[k], refs[k + 1]
    pitch = px + 1
    for start, ref in zip(starts, src_refs):
        widen(s32, start, ref, px, pitch)
    last = starts[-1] + src_refs[-1].shape[0] // px
    clear(s32, last, out.shape[1], px, pitch)

    def turn(p):
        out[p] = s32[pl.ds(p, out.shape[1], stride=pitch), :].astype(BF16)

    loop(px, turn, 8)


def total_kernel(px, n, slots, widths, own_ref, halo_t, *refs):
    k = len(widths)
    msg_refs, tg_ref, pw, t32 = refs[:k], refs[k], refs[k + 1], refs[k + 2]
    pitch = px + 1
    inv_root = 1.0 / math.sqrt(own_ref.shape[2])
    at = 0
    for width, ref in zip(widths, msg_refs):
        for g in range(ref.shape[1] // LANES):
            block = ref[:, g * LANES : (g + 1) * LANES].astype(F32)
            for j in range(width):
                turned = block if j == 0 else pltpu.roll(block, LANES - j * slots, 1)
                pw[at * pitch : at * pitch + px, :] = turned
                at += 1
    clear(pw, at, halo_t.shape[1], px, pitch)

    def per_pixel(p):
        w = pw[pl.ds(p, halo_t.shape[1], stride=pitch), :]
        tg = own_ref[p] + lax.dot_general(
            w[:, :n].astype(BF16), halo_t[p], TN, preferred_element_type=F32
        )
        t32[pl.ds(p, n, stride=pitch), :] = tg * inv_root

    loop(px, per_pixel, px // 2)

    def narrow(i):
        tg_ref[pl.ds(pl.multiple_of(i * px, px), px), :] = t32[pl.ds(i * pitch, px), :].astype(BF16)

    loop(n, narrow)


VM = pl.BlockSpec(memory_space=pltpu.VMEM)
HB = pl.BlockSpec(memory_space=pltpu.HBM)


def call(kernel, outs, scratch, args, us=2.0, far=0, sems=0, limit=24):
    return pl.pallas_call(
        kernel,
        out_shape=[jax.ShapeDtypeStruct(s, d) for s, d in outs],
        in_specs=[HB] * far + [VM] * (len(args) - far),
        out_specs=[VM] * len(outs),
        scratch_shapes=[pltpu.VMEM(s, d) for s, d in scratch]
        + ([pltpu.VMEM(x.shape, x.dtype) for x in args[:far]] if far else [])
        + ([pltpu.SemaphoreType.DMA((sems,))] if far else []),
        compiler_params=pltpu.CompilerParams(vmem_limit_bytes=limit * 2**20),
        cost_estimate=pl.CostEstimate(
            flops=0, bytes_accessed=int(us * 3 * 10**6), transcendentals=0
        ),
    )(*args)


def shards(source, target, target_ids, out_grad, w_in, b_in, w_out):
    rows, cols, px, channels = source.shape
    picks = target_ids.shape[2]
    n = rows * cols
    pitch = px + 1
    slots = 1 << (picks - 1).bit_length()
    per = LANES // slots
    groups = n // per
    assert n <= slots and cols % per == 0 and H <= per and groups * per == n
    pieces, base, ext = plan(rows, cols)
    ext_pad = -(-ext // LANES) * LANES

    shapes = [
        (rows if qz is None else H, cols if qx is None else H, px, channels) for qz, qx in pieces
    ]

    hidden = w_in.shape[1]
    outs = [(s, BF16) for s in shapes] + [
        ((px, n, channels), BF16),
        ((px, n, channels), BF16),
        ((hidden, n * slots), F32),
        ((hidden, 2 * px), BF16),
        ((px, hidden), BF16),
        ((hidden, LANES), F32),
        ((groups, LANES), jnp.int32),
        ((groups, LANES), jnp.int32),
    ]
    args = (
        source,
        target,
        jnp.swapaxes(out_grad, 1, 2),
        target_ids.reshape(n, picks),
        w_in,
        b_in.reshape(1, hidden),
        w_out,
    )
    args = tuple(pltpu.with_memory_space_constraint(a, pltpu.HBM) for a in args)
    made = call(
        partial(head_kernel, base, pieces, rows, cols, slots),
        outs,
        [((n * pitch, channels), F32)] * 2
        + [((n * (slots + 1), out_grad.shape[3]), F32), ((n, LANES), jnp.int32)],
        args,
        far=len(args),
        sems=len(args) + len(pieces),
        limit=24,
    )
    k = len(pieces)
    src_t, own_t, grad_hidden, w_t, w_half, b_t, e_ids, m_ids = made[k:]
    cut_t = pl.pallas_call(
        partial(cut_kernel, pieces, rows, cols),
        name="cut",
        out_shape=[jax.ShapeDtypeStruct(s, BF16) for s in shapes],
        in_specs=[HB],
        out_specs=[VM] * k,
        scratch_shapes=[pltpu.SemaphoreType.DMA((k,))],
        compiler_params=pltpu.CompilerParams(vmem_limit_bytes=4 * 2**20),
    )(args[1])

    def halo_of(slabs):
        got = []
        for x, (qz, qx) in zip(slabs, pieces):
            got.append(swap(x, qz, qx).reshape(-1, channels))
        return got

    tgt_halo = halo_of(cut_t)
    src_halo = halo_of(made[:k])
    starts = [base[q] for q in pieces]
    counts = [h.shape[0] // px for h in tgt_halo]
    costs, tgt_t, hots = call(
        partial(corr_kernel, px, n, ext, starts, slots),
        [
            ((px, n * slots), BF16),
            ((px, ext_pad, channels), BF16),
            ((n * ext_pad, LANES), BF16),
        ],
        [
            (((ext_pad - n) * pitch, channels), F32),
            ((ext_pad // LANES, n * pitch, LANES), F32),
        ],
        (own_t, src_t, e_ids, *tgt_halo),
        us=3,
    )
    reps = lax.axis_size("rep")
    other = lax.ppermute(costs, "rep", [(i, reps - 1 - i) for i in range(reps)])
    lanes = [
        (rows if qz is None else H) * (cols // per if qx is None else 1) * LANES
        for qz, qx in pieces
    ]
    gc, *sent = call(
        partial(decoder_kernel, rows, cols, slots, pieces, starts, counts),
        [((px, n * slots), BF16)] + [((px, w), BF16) for w in lanes],
        [((2 * px, n * slots), BF16)],
        (costs, other, grad_hidden, w_t, b_t, w_half, e_ids, m_ids),
        us=3,
    )
    got = []
    for x, (qz, qx) in zip(sent, pieces):
        got.append(swap(x, qz, qx))
    sg, own = call(
        partial(own_kernel, px, n, slots),
        [((n * px, channels), BF16), ((px, n, channels), F32)],
        [((ext_pad // LANES, n * pitch, LANES), F32), ((n * pitch, channels), F32)],
        (gc, hots, tgt_t, src_t),
        us=4,
    )
    halo_pad = -(-(ext - n) // 16) * 16
    (halo_t,) = call(
        partial(halo_kernel, px, [s - n for s in starts]),
        [((px, halo_pad, channels), BF16)],
        [((halo_pad * pitch, channels), F32)],
        tuple(src_halo),
        us=1,
    )
    (tg,) = call(
        partial(total_kernel, px, n, slots, [per if qx is None else H for _, qx in pieces]),
        [((n * px, channels), BF16)],
        [((halo_pad * pitch, LANES), F32), ((n * pitch, channels), F32)],
        (own, halo_t, *got),
        us=3,
    )
    return sg.reshape(source.shape), tg.reshape(source.shape)


def solution(mesh):
    cells = P(("groups", "strip"), "sub", "rep", None)
    placed = (
        cells,
        cells,
        P(("groups", "strip"), "sub", None),
        P(("groups", "strip"), "sub", None, None),
        P(),
        P(),
        P(),
    )

    return jax.shard_map(
        shards, mesh=mesh, in_specs=placed, out_specs=(cells, cells), check_vma=False
    )
```

```python
from functools import partial
import math

import jax
import jax.numpy as jnp
from jax import lax
from jax.experimental import pallas as pl
from jax.experimental.pallas import tpu as pltpu
from jax.sharding import PartitionSpec as P

H = 3
LANES = 128
NT = (((1,), (1,)), ((), ()))
TN = (((0,), (0,)), ((), ()))
F32 = jnp.float32
BF16 = jnp.bfloat16


def mate(i, q, n):
    j = i + 1 if (i + q) % 2 == 0 else i - 1
    return j if 0 <= j < n else None


def turns(n):
    return [q for q in (0, 1) if any(mate(i, q, n) is not None for i in range(n))]


def swap(x, qz, qx):
    strips, subs = lax.axis_size("strip"), lax.axis_size("sub")
    pairs = []
    for s in range(strips):
        for u in range(subs):
            t = s if qz is None else mate(s, qz, strips)
            v = u if qx is None else mate(u, qx, subs)
            if t is not None and v is not None:
                pairs.append((s * subs + u, t * subs + v))
    return lax.ppermute(x, ("strip", "sub"), pairs)


def plan(rows, cols):
    zs, xs = turns(lax.axis_size("strip")), turns(lax.axis_size("sub"))
    pieces = [(q, None) for q in zs]
    pieces += [(None, r) for r in xs]
    pieces += [(q, r) for q in zs for r in xs]
    base, at = {(None, None): 0}, rows * cols
    for qz, qx in pieces:
        base[qz, qx] = at
        at += (rows if qz is None else H) * (cols if qx is None else H)
    return pieces, base, at


def joined(piece):
    return piece[0] is not None and piece[1] is not None


def facing(q, extent, index):
    return jnp.where((index + q) % 2 == 0, extent - H, 0)


def scale_of(n):
    assert n & (n - 1) == 0
    return n.bit_length() - 1


def places(ids, base, rows, cols):
    total_cols = cols * lax.axis_size("sub")
    strip_at, sub_at = lax.axis_index("strip"), lax.axis_index("sub")

    def split(d, extent, index):
        side = jnp.where(d < 0, -1, jnp.where(d >= extent, 1, 0))
        inner = jnp.where(side < 0, d + H, jnp.where(side > 0, d - extent, d))
        ahead = jnp.where(index % 2 == 0, 1, -1)
        turn = jnp.where(side == 0, -1, jnp.where(side == ahead, 0, 1))
        return turn, inner

    row = lax.shift_right_arithmetic(ids, jnp.int32(scale_of(total_cols)))
    col = ids & (total_cols - 1)
    tz, dr = split(row - strip_at * rows, rows, strip_at)
    tx, dc = split(col - sub_at * cols, cols, sub_at)
    where_to = jnp.full(ids.shape, -1, jnp.int32)
    for (qz, qx), start in base.items():
        here = (tz == (-1 if qz is None else qz)) & (tx == (-1 if qx is None else qx))
        width = cols if qx is None else H
        where_to = jnp.where(here, start + dr * width + dc, where_to)
    assert scale_of(rows) + scale_of(cols) >= 0
    return where_to, (row & (rows - 1)) * cols + (col & (cols - 1))


def cuts(pieces, rows, cols, x_ref, out_refs, sems, at):
    strip_at, sub_at = lax.axis_index("strip"), lax.axis_index("sub")
    copies = []
    for i, ((qz, qx), ref) in enumerate(zip(pieces, out_refs)):
        r = pl.ds(0, rows) if qz is None else pl.ds(facing(qz, rows, strip_at), H)
        c = pl.ds(0, cols) if qx is None else pl.ds(facing(qx, cols, sub_at), H)
        copies.append(pltpu.make_async_copy(x_ref.at[r, c], ref, sems.at[at + i]))
    return copies


def loop(count, body, most=4):
    step = max(d for d in range(1, most + 1) if count % d == 0) if count else 1

    def run(i, _):
        body(i)
        return 0

    lax.fori_loop(0, count, run, 0, unroll=step)


def widen(dst, at, src_ref, px, pitch, count):
    def body(i):
        rows = src_ref[pl.ds(pl.multiple_of(i * px, px), px), :]
        dst[pl.ds((at + i) * pitch, px), :] = rows.astype(F32)

    loop(count, body)


def clear(dst, at, end, px, pitch):
    def body(i):
        dst[pl.ds((at + i) * pitch, px), :] = jnp.zeros((px, dst.shape[1]), F32)

    loop(end - at, body)


def hot(row, tile=0):
    e = lax.broadcasted_iota(jnp.int32, (LANES, LANES), 0) + tile * LANES
    return (e == row).astype(F32).astype(BF16)


def pick_hot(e_ref, b, slots, tile):
    group, j = divmod(b, LANES // slots)
    lane = lax.broadcasted_iota(jnp.int32, (1, LANES), 1) // slots
    return hot(jnp.where(lane == j, e_ref[group : group + 1, :], -1), tile)


def cut_kernel(pieces, rows, cols, x_ref, *refs):
    copies = cuts(pieces, rows, cols, x_ref, refs[:-1], refs[-1], 0)
    for copy in copies:
        copy.start()
    for copy in copies:
        copy.wait()


def slotted(x, out_ref, table, slots):
    n, picks = x.shape
    per = LANES // slots
    table[...] = jnp.full(table.shape, -1, jnp.int32)
    table[:, :picks] = x
    lane = lax.broadcasted_iota(jnp.int32, (n // per, LANES), 1) // slots
    acc = jnp.full((n // per, LANES), -1, jnp.int32)
    for j in range(per):
        rows = table[pl.ds(j, n // per, stride=per), :]
        acc = jnp.where(lane == j, rows if j == 0 else pltpu.roll(rows, j * slots, 1), acc)
    out_ref[...] = acc


def head_kernel(base, pieces, rows, cols, slots, *refs):
    k = len(pieces)
    far, rest = refs[:7], refs[7:]
    src_slabs, outs, rest = rest[:k], rest[k : k + 8], rest[k + 8 :]
    src_t, tgt_t, gh_ref, wt_ref, wh_ref, bt_ref, e_ref, m_ref = outs
    (s32, t32, og, table), near, sems = rest[:4], rest[4:-1], rest[-1]
    src_ref, tgt_ref, og_ref, ids_ref, w_in_ref, b_ref, w_out_ref = near
    fetches = [pltpu.make_async_copy(f, v, sems.at[i]) for i, (f, v) in enumerate(zip(far, near))]
    slabs = cuts(pieces, rows, cols, far[0], src_slabs, sems, 7)
    for copy in fetches[2:] + fetches[:2] + slabs:
        copy.start()
    px, n, _ = src_t.shape
    pitch = px + 1
    for fetch in fetches[2:]:
        fetch.wait()
    e_at, m_at = places(ids_ref[...], base, rows, cols)
    slotted(e_at, e_ref, table, slots)
    slotted(m_at, m_ref, table, slots)
    wt_ref[...] = w_in_ref[...].T
    rep = lax.axis_index("rep")
    wh_ref[...] = w_in_ref[pl.ds(pl.multiple_of(rep * px, px), px), :]
    bt_ref[...] = jnp.broadcast_to(b_ref[...], (LANES, b_ref.shape[1])).T
    picks = og_ref.shape[1]
    og[...] = jnp.zeros_like(og)
    for r in range(rows):
        for pick in range(picks):
            at = r * cols * (slots + 1) + pick
            og[pl.ds(at, cols, stride=slots + 1), :] = og_ref[r, pick].astype(F32)
    per = LANES // slots
    for g in range(n // per):
        block = jnp.concatenate(
            [og[b * (slots + 1) : b * (slots + 1) + slots, :] for b in range(g * per, (g + 1) * per)]
        ).astype(BF16)
        gh_ref[:, g * LANES : (g + 1) * LANES] = lax.dot_general(
            w_out_ref[...], block, NT, preferred_element_type=F32
        )
    for fetch in fetches[:2]:
        fetch.wait()
    for dst, src in ((s32, src_ref), (t32, tgt_ref)):

        def body(i, dst=dst, src=src):
            rows_of = src[i // cols, lax.rem(i, cols)]
            dst[pl.ds(i * pitch, px), :] = rows_of.astype(F32)

        loop(n, body, 8)

    def turn(p):
        src_t[p] = s32[pl.ds(p, n, stride=pitch), :].astype(BF16)
        tgt_t[p] = t32[pl.ds(p, n, stride=pitch), :].astype(BF16)

    loop(px, turn, 8)
    for copy in slabs:
        copy.wait()


def corr_kernel(px, n, ext, starts, slots, *refs):
    k = len(starts)
    own_t, src_t, e_ref, tgt_refs = refs[0], refs[1], refs[2], refs[3 : 3 + k]
    costs_ref, tgt_t, hot_ref, t32, corr = refs[3 + k :]
    ext_pad = tgt_t.shape[1]
    tiles = ext_pad // LANES
    pitch = px + 1
    inv_root = 1.0 / math.sqrt(tgt_t.shape[2])
    for start, ref in zip(starts, tgt_refs):
        widen(t32, start - n, ref, px, pitch, ref.shape[0] // px)
    clear(t32, ext - n, ext_pad - n, px, pitch)

    def per_pixel(p):
        tp = t32[pl.ds(p, ext_pad - n, stride=pitch), :].astype(BF16)
        tp = jnp.concatenate([own_t[p], tp], axis=0)
        tgt_t[p] = tp
        c = lax.dot_general(src_t[p], tp, NT, preferred_element_type=F32) * inv_root
        for t in range(tiles):
            corr[t, pl.ds(p, n, stride=pitch), :] = c[:, t * LANES : (t + 1) * LANES]

    loop(px, per_pixel, px)
    per = LANES // slots
    for g in range(n // per):
        left = []
        for j in range(per):
            b = g * per + j
            for t in range(tiles):
                at = (b * tiles + t) * LANES
                hot_ref[at : at + LANES, :] = pick_hot(e_ref, b, slots, t)
                left.append(corr[t, b * pitch : b * pitch + px, :].astype(BF16))
        high = per * tiles * LANES
        costs_ref[:, g * LANES : (g + 1) * LANES] = jnp.dot(
            jnp.concatenate(left, axis=1),
            hot_ref[g * high : (g + 1) * high, :],
            preferred_element_type=F32,
        ).astype(BF16)


def gelu_slope(x):
    c = math.sqrt(2.0 / math.pi)
    x2 = x * x
    th = jnp.tanh(x * (c + (c * 0.044715) * x2))
    inner = x * (c + (c * 3.0 * 0.044715) * x2)
    return (0.5 + 0.5 * th) * (1.0 + (1.0 - th) * inner)


def decoder_kernel(rows, cols, slots, pieces, starts, counts, *refs):
    both = sum(joined(piece) for piece in pieces)
    mine_ref, other_ref, gh_ref, wt_ref, bt_ref, w_ref, e_ref, m_ref = refs[:8]
    slab_refs, rest = refs[8 : 8 + both], refs[8 + both :]
    gc_ref, out_refs, whole = rest[0], rest[1:-1], rest[-1]
    for piece, ref in zip(pieces, out_refs):
        if joined(piece):
            slab = slab_refs[0].reshape(-1, LANES)
            slab_refs = slab_refs[1:]
            ref[: slab.shape[0], :] = slab[...]
    px = mine_ref.shape[0]
    rep = lax.axis_index("rep")
    whole[pl.ds(pl.multiple_of(rep * px, px), px), :] = mine_ref[...]
    whole[pl.ds(pl.multiple_of((1 - rep) * px, px), px), :] = other_ref[...]
    w_half = w_ref[...]
    wide = 2
    bias = jnp.concatenate([bt_ref[...]] * wide, axis=1)
    width = wide * LANES
    for g in range(mine_ref.shape[1] // width):
        cut = slice(g * width, (g + 1) * width)
        pre = jnp.dot(wt_ref[...], whole[:, cut], preferred_element_type=F32) + bias
        grad = (gh_ref[:, cut] * gelu_slope(pre)).astype(BF16)
        gc_ref[:, cut] = jnp.dot(w_half, grad, preferred_element_type=F32).astype(BF16)
    send(rows, cols, slots, pieces, starts, counts, gc_ref, e_ref, m_ref, out_refs)


def send(rows, cols, slots, pieces, starts, counts, gc_ref, e_ref, m_ref, out_refs):
    per = LANES // slots
    wide = cols // per
    strip_at, sub_at = lax.axis_index("strip"), lax.axis_index("sub")
    lane = lax.broadcasted_iota(jnp.int32, (1, LANES), 1) // slots
    for (qz, qx), start, count, ref in zip(pieces, starts, counts, out_refs):
        r0 = 0 if qz is None else facing(qz, rows, strip_at)
        tail = None if qx is None else (sub_at + qx) % 2 == 0
        half = 0 if qx is None else jnp.where(tail, (cols - H) // per, 0)
        shift = 0 if qx is None else jnp.where(tail, (cols - H) % per, 0)
        px = gc_ref.shape[0]
        i = count if joined((qz, qx)) else 0
        for r in range(rows if qz is None else H):
            for h in range(wide if qx is None else 1):
                g = (r0 + r) * wide + half + h
                e, m = e_ref[pl.ds(g, 1), :], m_ref[pl.ds(g, 1), :]
                here = (e >= start) & (e < start + count)
                to = jnp.where(here, (lane - shift) * slots + m, -1)
                at = g * LANES
                at = at if isinstance(at, int) else pl.multiple_of(at, LANES)
                ref[i * px : (i + 1) * px, :] = lax.dot_general(
                    gc_ref[:, pl.ds(at, LANES)], hot(to), NT, preferred_element_type=F32
                ).astype(BF16)
                i += 1


def own_kernel(px, n, slots, gc_ref, hot_ref, tgt_t, src_t, sg_ref, own_ref, pw, s32):
    ext_pad = tgt_t.shape[1]
    pitch = px + 1
    inv_root = 1.0 / math.sqrt(tgt_t.shape[2])
    tiles = ext_pad // LANES
    per = LANES // slots
    high = per * tiles * LANES
    for g in range(n // per):
        w = lax.dot_general(
            gc_ref[:, g * LANES : (g + 1) * LANES],
            hot_ref[g * high : (g + 1) * high, :],
            NT,
            preferred_element_type=F32,
        )
        for j in range(per):
            b = g * per + j
            for t in range(tiles):
                at = (j * tiles + t) * LANES
                pw[t, b * pitch : b * pitch + px, :] = w[:, at : at + LANES]

    def per_pixel(p):
        tp = tgt_t[p]
        sg = jnp.zeros((n, tp.shape[1]), F32)
        for t in range(tiles):
            w = pw[t, pl.ds(p, n, stride=pitch), :].astype(BF16)
            sg += jnp.dot(w, tp[t * LANES : (t + 1) * LANES, :], preferred_element_type=F32)
            if t == 0:
                own_ref[p] = lax.dot_general(
                    w[:, :n], src_t[p], TN, preferred_element_type=F32
                )
        s32[pl.ds(p, n, stride=pitch), :] = sg * inv_root

    loop(px, per_pixel, px)

    def narrow(i):
        sg_ref[pl.ds(pl.multiple_of(i * px, px), px), :] = s32[pl.ds(i * pitch, px), :].astype(BF16)

    loop(n, narrow)


def halo_kernel(px, starts, counts, *refs):
    k = len(starts)
    src_refs, out, s32 = refs[:k], refs[k], refs[k + 1]
    pitch = px + 1
    for start, count, ref in zip(starts, counts, src_refs):
        widen(s32, start, ref, px, pitch, count)
    last = starts[-1] + counts[-1]
    clear(s32, last, out.shape[1], px, pitch)

    def turn(p):
        out[p] = s32[pl.ds(p, out.shape[1], stride=pitch), :].astype(BF16)

    loop(px, turn, 8)


def total_kernel(px, n, slots, firsts, widths, own_ref, halo_t, *refs):
    k = len(widths)
    msg_refs, tg_ref, pw, t32 = refs[:k], refs[k], refs[k + 1], refs[k + 2]
    pitch = px + 1
    inv_root = 1.0 / math.sqrt(own_ref.shape[2])
    at = 0
    for first, width, ref in zip(firsts, widths, msg_refs):
        for g in range(first, ref.shape[0] // px):
            block = ref[g * px : (g + 1) * px, :].astype(F32)
            for j in range(width):
                turned = block if j == 0 else pltpu.roll(block, LANES - j * slots, 1)
                pw[at * pitch : at * pitch + px, :] = turned
                at += 1
    clear(pw, at, halo_t.shape[1], px, pitch)

    def per_pixel(p):
        w = pw[pl.ds(p, halo_t.shape[1], stride=pitch), :]
        tg = own_ref[p] + lax.dot_general(
            w[:, :n].astype(BF16), halo_t[p], TN, preferred_element_type=F32
        )
        t32[pl.ds(p, n, stride=pitch), :] = tg * inv_root

    loop(px, per_pixel, px // 2)

    def narrow(i):
        tg_ref[pl.ds(pl.multiple_of(i * px, px), px), :] = t32[pl.ds(i * pitch, px), :].astype(BF16)

    loop(n, narrow)


VM = pl.BlockSpec(memory_space=pltpu.VMEM)
HB = pl.BlockSpec(memory_space=pltpu.HBM)


def call(kernel, outs, scratch, args, us=2.0, far=0, sems=0, limit=24):
    return pl.pallas_call(
        kernel,
        out_shape=[jax.ShapeDtypeStruct(s, d) for s, d in outs],
        in_specs=[HB] * far + [VM] * (len(args) - far),
        out_specs=[VM] * len(outs),
        scratch_shapes=[pltpu.VMEM(s, d) for s, d in scratch]
        + ([pltpu.VMEM(x.shape, x.dtype) for x in args[:far]] if far else [])
        + ([pltpu.SemaphoreType.DMA((sems,))] if far else []),
        compiler_params=pltpu.CompilerParams(vmem_limit_bytes=limit * 2**20),
        cost_estimate=pl.CostEstimate(
            flops=0, bytes_accessed=int(us * 3 * 10**6), transcendentals=0
        ),
    )(*args)


def shards(source, target, target_ids, out_grad, w_in, b_in, w_out):
    rows, cols, px, channels = source.shape
    picks = target_ids.shape[2]
    n = rows * cols
    pitch = px + 1
    slots = 1 << (picks - 1).bit_length()
    per = LANES // slots
    groups = n // per
    assert n <= slots and cols % per == 0 and H <= per and groups * per == n
    pieces, base, ext = plan(rows, cols)
    ext_pad = -(-ext // LANES) * LANES

    shapes = [
        (rows if qz is None else H, cols if qx is None else H, px, channels) for qz, qx in pieces
    ]

    hidden = w_in.shape[1]
    outs = [(s, BF16) for s in shapes] + [
        ((px, n, channels), BF16),
        ((px, n, channels), BF16),
        ((hidden, n * slots), F32),
        ((hidden, 2 * px), BF16),
        ((px, hidden), BF16),
        ((hidden, LANES), F32),
        ((groups, LANES), jnp.int32),
        ((groups, LANES), jnp.int32),
    ]
    args = (
        source,
        target,
        jnp.swapaxes(out_grad, 1, 2),
        target_ids.reshape(n, picks),
        w_in,
        b_in.reshape(1, hidden),
        w_out,
    )
    args = tuple(pltpu.with_memory_space_constraint(a, pltpu.HBM) for a in args)
    made = call(
        partial(head_kernel, base, pieces, rows, cols, slots),
        outs,
        [((n * pitch, channels), F32)] * 2
        + [((n * (slots + 1), out_grad.shape[3]), F32), ((n, LANES), jnp.int32)],
        args,
        far=len(args),
        sems=len(args) + len(pieces),
        limit=24,
    )
    k = len(pieces)
    src_t, own_t, grad_hidden, w_t, w_half, b_t, e_ids, m_ids = made[k:]
    cut_t = pl.pallas_call(
        partial(cut_kernel, pieces, rows, cols),
        name="cut",
        out_shape=[jax.ShapeDtypeStruct(s, BF16) for s in shapes],
        in_specs=[HB],
        out_specs=[VM] * k,
        scratch_shapes=[pltpu.SemaphoreType.DMA((k,))],
        compiler_params=pltpu.CompilerParams(vmem_limit_bytes=4 * 2**20),
    )(args[1])

    def sent_to(arrays, keep):
        got = []
        for x, (qz, qx) in zip(arrays, pieces):
            if keep((qz, qx)):
                got.append(swap(x, qz, qx).reshape(-1, channels))
        return got

    assert channels == LANES
    slabs = made[:k]
    tgt_halo = sent_to(cut_t, lambda piece: True)
    src_halo = sent_to(slabs, lambda piece: not joined(piece))
    starts = [base[q] for q in pieces]
    counts = [h.shape[0] // px for h in tgt_halo]
    costs, tgt_t, hots = call(
        partial(corr_kernel, px, n, ext, starts, slots),
        [
            ((px, n * slots), BF16),
            ((px, ext_pad, channels), BF16),
            ((n * ext_pad, LANES), BF16),
        ],
        [
            (((ext_pad - n) * pitch, channels), F32),
            ((ext_pad // LANES, n * pitch, LANES), F32),
        ],
        (own_t, src_t, e_ids, *tgt_halo),
        us=3,
    )
    reps = lax.axis_size("rep")
    other = lax.ppermute(costs, "rep", [(i, reps - 1 - i) for i in range(reps)])
    firsts = [c if joined(piece) else 0 for c, piece in zip(counts, pieces)]
    lengths = [
        first + (rows if qz is None else H) * (cols // per if qx is None else 1)
        for first, (qz, qx) in zip(firsts, pieces)
    ]
    gc, *sent = call(
        partial(decoder_kernel, rows, cols, slots, pieces, starts, counts),
        [((px, n * slots), BF16)] + [((w * px, LANES), BF16) for w in lengths],
        [((2 * px, n * slots), BF16)],
        (
            *(costs, other, grad_hidden, w_t, b_t, w_half, e_ids, m_ids),
            *(slab for slab, piece in zip(slabs, pieces) if joined(piece)),
        ),
        us=3,
    )
    got = sent_to(sent, lambda piece: True)
    src_halo += [x for x, piece in zip(got, pieces) if joined(piece)]
    sg, own = call(
        partial(own_kernel, px, n, slots),
        [((n * px, channels), BF16), ((px, n, channels), F32)],
        [((ext_pad // LANES, n * pitch, LANES), F32), ((n * pitch, channels), F32)],
        (gc, hots, tgt_t, src_t),
        us=4,
    )
    halo_pad = -(-(ext - n) // 16) * 16
    (halo_t,) = call(
        partial(halo_kernel, px, [s - n for s in starts], counts),
        [((px, halo_pad, channels), BF16)],
        [((halo_pad * pitch, channels), F32)],
        tuple(src_halo),
        us=1,
    )
    (tg,) = call(
        partial(total_kernel, px, n, slots, firsts, [per if qx is None else H for _, qx in pieces]),
        [((n * px, channels), BF16)],
        [((halo_pad * pitch, LANES), F32), ((n * pitch, channels), F32)],
        (own, halo_t, *got),
        us=3,
    )
    return sg.reshape(source.shape), tg.reshape(source.shape)


def solution(mesh):
    cells = P(("groups", "strip"), "sub", "rep", None)
    placed = (
        cells,
        cells,
        P(("groups", "strip"), "sub", None),
        P(("groups", "strip"), "sub", None, None),
        P(),
        P(),
        P(),
    )

    return jax.shard_map(
        shards, mesh=mesh, in_specs=placed, out_specs=(cells, cells), check_vma=False
    )
```

```python
from functools import partial
import math

import jax
import jax.numpy as jnp
from jax import lax
from jax.experimental import pallas as pl
from jax.experimental.pallas import tpu as pltpu
from jax.sharding import PartitionSpec as P

H = 3
LANES = 128
NT = (((1,), (1,)), ((), ()))
TN = (((0,), (0,)), ((), ()))
F32 = jnp.float32
BF16 = jnp.bfloat16


def mate(i, q, n):
    j = i + 1 if (i + q) % 2 == 0 else i - 1
    return j if 0 <= j < n else None


def turns(n):
    return [q for q in (0, 1) if any(mate(i, q, n) is not None for i in range(n))]


def swap(x, qz, qx):
    strips, subs = lax.axis_size("strip"), lax.axis_size("sub")
    pairs = []
    for s in range(strips):
        for u in range(subs):
            t = s if qz is None else mate(s, qz, strips)
            v = u if qx is None else mate(u, qx, subs)
            if t is not None and v is not None:
                pairs.append((s * subs + u, t * subs + v))
    return lax.ppermute(x, ("strip", "sub"), pairs)


def plan(rows, cols):
    zs, xs = turns(lax.axis_size("strip")), turns(lax.axis_size("sub"))
    pieces = [(q, None) for q in zs]
    pieces += [(None, r) for r in xs]
    pieces += [(q, r) for q in zs for r in xs]
    base, at = {(None, None): 0}, rows * cols
    for qz, qx in pieces:
        base[qz, qx] = at
        at += (rows if qz is None else H) * (cols if qx is None else H)
    return pieces, base, at


def facing(q, extent, index):
    return jnp.where((index + q) % 2 == 0, extent - H, 0)


def scale_of(n):
    assert n & (n - 1) == 0
    return n.bit_length() - 1


def places(ids, base, rows, cols):
    total_cols = cols * lax.axis_size("sub")
    strip_at, sub_at = lax.axis_index("strip"), lax.axis_index("sub")

    def split(d, extent, index):
        side = jnp.where(d < 0, -1, jnp.where(d >= extent, 1, 0))
        inner = jnp.where(side < 0, d + H, jnp.where(side > 0, d - extent, d))
        ahead = jnp.where(index % 2 == 0, 1, -1)
        turn = jnp.where(side == 0, -1, jnp.where(side == ahead, 0, 1))
        return turn, inner

    row = lax.shift_right_arithmetic(ids, jnp.int32(scale_of(total_cols)))
    col = ids & (total_cols - 1)
    tz, dr = split(row - strip_at * rows, rows, strip_at)
    tx, dc = split(col - sub_at * cols, cols, sub_at)
    where_to = jnp.full(ids.shape, -1, jnp.int32)
    for (qz, qx), start in base.items():
        here = (tz == (-1 if qz is None else qz)) & (tx == (-1 if qx is None else qx))
        width = cols if qx is None else H
        where_to = jnp.where(here, start + dr * width + dc, where_to)
    assert scale_of(rows) + scale_of(cols) >= 0
    return where_to, (row & (rows - 1)) * cols + (col & (cols - 1))


def cuts(pieces, rows, cols, x_ref, out_refs, sems, at):
    strip_at, sub_at = lax.axis_index("strip"), lax.axis_index("sub")
    copies = []
    for i, ((qz, qx), ref) in enumerate(zip(pieces, out_refs)):
        r = pl.ds(0, rows) if qz is None else pl.ds(facing(qz, rows, strip_at), H)
        c = pl.ds(0, cols) if qx is None else pl.ds(facing(qx, cols, sub_at), H)
        copies.append(pltpu.make_async_copy(x_ref.at[r, c], ref, sems.at[at + i]))
    return copies


def loop(count, body, most=4):
    step = max(d for d in range(1, most + 1) if count % d == 0) if count else 1

    def run(i, _):
        body(i)
        return 0

    lax.fori_loop(0, count, run, 0, unroll=step)


def widen(dst, at, src_ref, px, pitch):
    def body(i):
        rows = src_ref[pl.ds(pl.multiple_of(i * px, px), px), :]
        dst[pl.ds((at + i) * pitch, px), :] = rows.astype(F32)

    loop(src_ref.shape[0] // px, body)


def clear(dst, at, end, px, pitch):
    def body(i):
        dst[pl.ds((at + i) * pitch, px), :] = jnp.zeros((px, dst.shape[1]), F32)

    loop(end - at, body)


def hot(row, tile=0):
    e = lax.broadcasted_iota(jnp.int32, (LANES, LANES), 0) + tile * LANES
    return (e == row).astype(F32).astype(BF16)


def pick_hot(e_ref, b, slots, tile):
    group, j = divmod(b, LANES // slots)
    lane = lax.broadcasted_iota(jnp.int32, (1, LANES), 1) // slots
    return hot(jnp.where(lane == j, e_ref[group : group + 1, :], -1), tile)


def cut_kernel(pieces, rows, cols, *refs):
    k = len(pieces)
    far, slabs, near, sems = refs[:7], refs[7 : 7 + k], refs[7 + k : -1], refs[-1]
    copies = cuts(pieces, rows, cols, far[1], slabs, sems, 0)
    for i, (f, v) in enumerate(zip(far, near)):
        copies.append(pltpu.make_async_copy(f, v, sems.at[k + i]))
    for copy in copies:
        copy.start()
    for copy in copies:
        copy.wait()


def slotted(x, out_ref, table, slots):
    n, picks = x.shape
    per = LANES // slots
    table[...] = jnp.full(table.shape, -1, jnp.int32)
    table[:, :picks] = x
    lane = lax.broadcasted_iota(jnp.int32, (n // per, LANES), 1) // slots
    acc = jnp.full((n // per, LANES), -1, jnp.int32)
    for j in range(per):
        rows = table[pl.ds(j, n // per, stride=per), :]
        acc = jnp.where(lane == j, rows if j == 0 else pltpu.roll(rows, j * slots, 1), acc)
    out_ref[...] = acc


def head_kernel(base, pieces, rows, cols, slots, *refs):
    k = len(pieces)
    far_ref, near, rest = refs[0], refs[1:8], refs[8:]
    src_slabs, outs, rest = rest[:k], rest[k : k + 8], rest[k + 8 :]
    src_t, tgt_t, gh_ref, wt_ref, wh_ref, bt_ref, e_ref, m_ref = outs
    s32, t32, og, table, sems = rest
    src_ref, tgt_ref, og_ref, ids_ref, w_in_ref, b_ref, w_out_ref = near
    slabs = cuts(pieces, rows, cols, far_ref, src_slabs, sems, 0)
    for copy in slabs:
        copy.start()
    px, n, _ = src_t.shape
    pitch = px + 1
    e_at, m_at = places(ids_ref[...], base, rows, cols)
    slotted(e_at, e_ref, table, slots)
    slotted(m_at, m_ref, table, slots)
    wt_ref[...] = w_in_ref[...].T
    rep = lax.axis_index("rep")
    wh_ref[...] = w_in_ref[pl.ds(pl.multiple_of(rep * px, px), px), :]
    bt_ref[...] = jnp.broadcast_to(b_ref[...], (LANES, b_ref.shape[1])).T
    picks = og_ref.shape[1]
    og[...] = jnp.zeros_like(og)
    for r in range(rows):
        for pick in range(picks):
            at = r * cols * (slots + 1) + pick
            og[pl.ds(at, cols, stride=slots + 1), :] = og_ref[r, pick].astype(F32)
    per = LANES // slots
    for g in range(n // per):
        block = jnp.concatenate(
            [og[b * (slots + 1) : b * (slots + 1) + slots, :] for b in range(g * per, (g + 1) * per)]
        ).astype(BF16)
        gh_ref[:, g * LANES : (g + 1) * LANES] = lax.dot_general(
            w_out_ref[...], block, NT, preferred_element_type=F32
        )
    for dst, src in ((s32, src_ref), (t32, tgt_ref)):

        def body(i, dst=dst, src=src):
            rows_of = src[i // cols, lax.rem(i, cols)]
            dst[pl.ds(i * pitch, px), :] = rows_of.astype(F32)

        loop(n, body, 8)

    def turn(p):
        src_t[p] = s32[pl.ds(p, n, stride=pitch), :].astype(BF16)
        tgt_t[p] = t32[pl.ds(p, n, stride=pitch), :].astype(BF16)

    loop(px, turn, 8)
    for copy in slabs:
        copy.wait()


def corr_kernel(px, n, ext, starts, slots, *refs):
    k = len(starts)
    own_t, src_t, e_ref, tgt_refs = refs[0], refs[1], refs[2], refs[3 : 3 + k]
    costs_ref, tgt_t, hot_ref, t32, corr = refs[3 + k :]
    ext_pad = tgt_t.shape[1]
    tiles = ext_pad // LANES
    pitch = px + 1
    inv_root = 1.0 / math.sqrt(tgt_t.shape[2])
    for start, ref in zip(starts, tgt_refs):
        widen(t32, start - n, ref, px, pitch)
    clear(t32, ext - n, ext_pad - n, px, pitch)

    def per_pixel(p):
        tp = t32[pl.ds(p, ext_pad - n, stride=pitch), :].astype(BF16)
        tp = jnp.concatenate([own_t[p], tp], axis=0)
        tgt_t[p] = tp
        c = lax.dot_general(src_t[p], tp, NT, preferred_element_type=F32) * inv_root
        for t in range(tiles):
            corr[t, pl.ds(p, n, stride=pitch), :] = c[:, t * LANES : (t + 1) * LANES]

    loop(px, per_pixel, px)
    per = LANES // slots
    for g in range(n // per):
        left = []
        for j in range(per):
            b = g * per + j
            for t in range(tiles):
                at = (b * tiles + t) * LANES
                hot_ref[at : at + LANES, :] = pick_hot(e_ref, b, slots, t)
                left.append(corr[t, b * pitch : b * pitch + px, :].astype(BF16))
        high = per * tiles * LANES
        costs_ref[:, g * LANES : (g + 1) * LANES] = jnp.dot(
            jnp.concatenate(left, axis=1),
            hot_ref[g * high : (g + 1) * high, :],
            preferred_element_type=F32,
        ).astype(BF16)


def gelu_slope(x):
    c = math.sqrt(2.0 / math.pi)
    x2 = x * x
    th = jnp.tanh(x * (c + (c * 0.044715) * x2))
    inner = x * (c + (c * 3.0 * 0.044715) * x2)
    return (0.5 + 0.5 * th) * (1.0 + (1.0 - th) * inner)


def decoder_kernel(rows, cols, slots, pieces, starts, counts, *refs):
    mine_ref, other_ref, gh_ref, wt_ref, bt_ref, w_ref, e_ref, m_ref = refs[:8]
    gc_ref, out_refs, whole = refs[8], refs[9:-1], refs[-1]
    px = mine_ref.shape[0]
    rep = lax.axis_index("rep")
    whole[pl.ds(pl.multiple_of(rep * px, px), px), :] = mine_ref[...]
    whole[pl.ds(pl.multiple_of((1 - rep) * px, px), px), :] = other_ref[...]
    w_half = w_ref[...]
    wide = 2
    bias = jnp.concatenate([bt_ref[...]] * wide, axis=1)
    width = wide * LANES
    for g in range(mine_ref.shape[1] // width):
        cut = slice(g * width, (g + 1) * width)
        pre = jnp.dot(wt_ref[...], whole[:, cut], preferred_element_type=F32) + bias
        grad = (gh_ref[:, cut] * gelu_slope(pre)).astype(BF16)
        gc_ref[:, cut] = jnp.dot(w_half, grad, preferred_element_type=F32).astype(BF16)
    send(rows, cols, slots, pieces, starts, counts, gc_ref, e_ref, m_ref, out_refs)


def send(rows, cols, slots, pieces, starts, counts, gc_ref, e_ref, m_ref, out_refs):
    per = LANES // slots
    wide = cols // per
    strip_at, sub_at = lax.axis_index("strip"), lax.axis_index("sub")
    lane = lax.broadcasted_iota(jnp.int32, (1, LANES), 1) // slots
    for (qz, qx), start, count, ref in zip(pieces, starts, counts, out_refs):
        r0 = 0 if qz is None else facing(qz, rows, strip_at)
        tail = None if qx is None else (sub_at + qx) % 2 == 0
        half = 0 if qx is None else jnp.where(tail, (cols - H) // per, 0)
        shift = 0 if qx is None else jnp.where(tail, (cols - H) % per, 0)
        i = 0
        for r in range(rows if qz is None else H):
            for h in range(wide if qx is None else 1):
                g = (r0 + r) * wide + half + h
                e, m = e_ref[pl.ds(g, 1), :], m_ref[pl.ds(g, 1), :]
                here = (e >= start) & (e < start + count)
                to = jnp.where(here, (lane - shift) * slots + m, -1)
                at = g * LANES
                at = at if isinstance(at, int) else pl.multiple_of(at, LANES)
                ref[:, i * LANES : (i + 1) * LANES] = lax.dot_general(
                    gc_ref[:, pl.ds(at, LANES)], hot(to), NT, preferred_element_type=F32
                ).astype(BF16)
                i += 1


def own_kernel(px, n, slots, gc_ref, hot_ref, tgt_t, src_t, sg_ref, own_ref, pw, s32):
    ext_pad = tgt_t.shape[1]
    pitch = px + 1
    inv_root = 1.0 / math.sqrt(tgt_t.shape[2])
    tiles = ext_pad // LANES
    per = LANES // slots
    high = per * tiles * LANES
    for g in range(n // per):
        w = lax.dot_general(
            gc_ref[:, g * LANES : (g + 1) * LANES],
            hot_ref[g * high : (g + 1) * high, :],
            NT,
            preferred_element_type=F32,
        )
        for j in range(per):
            b = g * per + j
            for t in range(tiles):
                at = (j * tiles + t) * LANES
                pw[t, b * pitch : b * pitch + px, :] = w[:, at : at + LANES]

    def per_pixel(p):
        tp = tgt_t[p]
        sg = jnp.zeros((n, tp.shape[1]), F32)
        for t in range(tiles):
            w = pw[t, pl.ds(p, n, stride=pitch), :].astype(BF16)
            sg += jnp.dot(w, tp[t * LANES : (t + 1) * LANES, :], preferred_element_type=F32)
            if t == 0:
                own_ref[p] = lax.dot_general(
                    w[:, :n], src_t[p], TN, preferred_element_type=F32
                )
        s32[pl.ds(p, n, stride=pitch), :] = sg * inv_root

    loop(px, per_pixel, px)

    def narrow(i):
        sg_ref[pl.ds(pl.multiple_of(i * px, px), px), :] = s32[pl.ds(i * pitch, px), :].astype(BF16)

    loop(n, narrow)


def halo_kernel(px, starts, *refs):
    k = len(starts)
    src_refs, out, s32 = refs[:k], refs[k], refs[k + 1]
    pitch = px + 1
    for start, ref in zip(starts, src_refs):
        widen(s32, start, ref, px, pitch)
    last = starts[-1] + src_refs[-1].shape[0] // px
    clear(s32, last, out.shape[1], px, pitch)

    def turn(p):
        out[p] = s32[pl.ds(p, out.shape[1], stride=pitch), :].astype(BF16)

    loop(px, turn, 8)


def total_kernel(px, n, slots, widths, own_ref, halo_t, *refs):
    k = len(widths)
    msg_refs, tg_ref, pw, t32 = refs[:k], refs[k], refs[k + 1], refs[k + 2]
    pitch = px + 1
    inv_root = 1.0 / math.sqrt(own_ref.shape[2])
    at = 0
    for width, ref in zip(widths, msg_refs):
        for g in range(ref.shape[1] // LANES):
            block = ref[:, g * LANES : (g + 1) * LANES].astype(F32)
            for j in range(width):
                turned = block if j == 0 else pltpu.roll(block, LANES - j * slots, 1)
                pw[at * pitch : at * pitch + px, :] = turned
                at += 1
    clear(pw, at, halo_t.shape[1], px, pitch)

    def per_pixel(p):
        w = pw[pl.ds(p, halo_t.shape[1], stride=pitch), :]
        tg = own_ref[p] + lax.dot_general(
            w[:, :n].astype(BF16), halo_t[p], TN, preferred_element_type=F32
        )
        t32[pl.ds(p, n, stride=pitch), :] = tg * inv_root

    loop(px, per_pixel, px // 2)

    def narrow(i):
        tg_ref[pl.ds(pl.multiple_of(i * px, px), px), :] = t32[pl.ds(i * pitch, px), :].astype(BF16)

    loop(n, narrow)


VM = pl.BlockSpec(memory_space=pltpu.VMEM)
HB = pl.BlockSpec(memory_space=pltpu.HBM)


def call(kernel, outs, scratch, args, us=2.0, far=0, sems=0, limit=24):
    return pl.pallas_call(
        kernel,
        out_shape=[jax.ShapeDtypeStruct(s, d) for s, d in outs],
        in_specs=[HB] * far + [VM] * (len(args) - far),
        out_specs=[VM] * len(outs),
        scratch_shapes=[pltpu.VMEM(s, d) for s, d in scratch]
        + ([pltpu.SemaphoreType.DMA((sems,))] if sems else []),
        compiler_params=pltpu.CompilerParams(vmem_limit_bytes=limit * 2**20),
        cost_estimate=pl.CostEstimate(
            flops=0, bytes_accessed=int(us * 3 * 10**6), transcendentals=0
        ),
    )(*args)


def shards(source, target, target_ids, out_grad, w_in, b_in, w_out):
    rows, cols, px, channels = source.shape
    picks = target_ids.shape[2]
    n = rows * cols
    pitch = px + 1
    slots = 1 << (picks - 1).bit_length()
    per = LANES // slots
    groups = n // per
    assert n <= slots and cols % per == 0 and H <= per and groups * per == n
    pieces, base, ext = plan(rows, cols)
    ext_pad = -(-ext // LANES) * LANES

    shapes = [
        (rows if qz is None else H, cols if qx is None else H, px, channels) for qz, qx in pieces
    ]

    hidden = w_in.shape[1]
    outs = [(s, BF16) for s in shapes] + [
        ((px, n, channels), BF16),
        ((px, n, channels), BF16),
        ((hidden, n * slots), F32),
        ((hidden, 2 * px), BF16),
        ((px, hidden), BF16),
        ((hidden, LANES), F32),
        ((groups, LANES), jnp.int32),
        ((groups, LANES), jnp.int32),
    ]
    args = (
        source,
        target,
        jnp.swapaxes(out_grad, 1, 2),
        target_ids.reshape(n, picks),
        w_in,
        b_in.reshape(1, hidden),
        w_out,
    )
    args = tuple(pltpu.with_memory_space_constraint(a, pltpu.HBM) for a in args)
    k = len(pieces)
    cut_t = pl.pallas_call(
        partial(cut_kernel, pieces, rows, cols),
        name="cut",
        out_shape=[jax.ShapeDtypeStruct(s, BF16) for s in shapes]
        + [jax.ShapeDtypeStruct(x.shape, x.dtype) for x in args],
        in_specs=[HB] * len(args),
        out_specs=[VM] * (k + len(args)),
        scratch_shapes=[pltpu.SemaphoreType.DMA((k + len(args),))],
        compiler_params=pltpu.CompilerParams(vmem_limit_bytes=8 * 2**20),
    )(*args)
    made = call(
        partial(head_kernel, base, pieces, rows, cols, slots),
        outs,
        [((n * pitch, channels), F32)] * 2
        + [((n * (slots + 1), out_grad.shape[3]), F32), ((n, LANES), jnp.int32)],
        (args[0], *cut_t[k:]),
        far=1,
        sems=k,
    )
    src_t, own_t, grad_hidden, w_t, w_half, b_t, e_ids, m_ids = made[k:]

    def halo_of(slabs):
        got = []
        for x, (qz, qx) in zip(slabs, pieces):
            got.append(swap(x, qz, qx).reshape(-1, channels))
        return got

    tgt_halo = halo_of(cut_t[:k])
    src_halo = halo_of(made[:k])
    starts = [base[q] for q in pieces]
    counts = [h.shape[0] // px for h in tgt_halo]
    costs, tgt_t, hots = call(
        partial(corr_kernel, px, n, ext, starts, slots),
        [
            ((px, n * slots), BF16),
            ((px, ext_pad, channels), BF16),
            ((n * ext_pad, LANES), BF16),
        ],
        [
            (((ext_pad - n) * pitch, channels), F32),
            ((ext_pad // LANES, n * pitch, LANES), F32),
        ],
        (own_t, src_t, e_ids, *tgt_halo),
        us=3,
    )
    reps = lax.axis_size("rep")
    other = lax.ppermute(costs, "rep", [(i, reps - 1 - i) for i in range(reps)])
    lanes = [
        (rows if qz is None else H) * (cols // per if qx is None else 1) * LANES
        for qz, qx in pieces
    ]
    gc, *sent = call(
        partial(decoder_kernel, rows, cols, slots, pieces, starts, counts),
        [((px, n * slots), BF16)] + [((px, w), BF16) for w in lanes],
        [((2 * px, n * slots), BF16)],
        (costs, other, grad_hidden, w_t, b_t, w_half, e_ids, m_ids),
        us=3,
    )
    got = []
    for x, (qz, qx) in zip(sent, pieces):
        got.append(swap(x, qz, qx))
    sg, own = call(
        partial(own_kernel, px, n, slots),
        [((n * px, channels), BF16), ((px, n, channels), F32)],
        [((ext_pad // LANES, n * pitch, LANES), F32), ((n * pitch, channels), F32)],
        (gc, hots, tgt_t, src_t),
        us=4,
    )
    halo_pad = -(-(ext - n) // 16) * 16
    (halo_t,) = call(
        partial(halo_kernel, px, [s - n for s in starts]),
        [((px, halo_pad, channels), BF16)],
        [((halo_pad * pitch, channels), F32)],
        tuple(src_halo),
        us=1,
    )
    (tg,) = call(
        partial(total_kernel, px, n, slots, [per if qx is None else H for _, qx in pieces]),
        [((n * px, channels), BF16)],
        [((halo_pad * pitch, LANES), F32), ((n * pitch, channels), F32)],
        (own, halo_t, *got),
        us=3,
    )
    return sg.reshape(source.shape), tg.reshape(source.shape)


def solution(mesh):
    cells = P(("groups", "strip"), "sub", "rep", None)
    placed = (
        cells,
        cells,
        P(("groups", "strip"), "sub", None),
        P(("groups", "strip"), "sub", None, None),
        P(),
        P(),
        P(),
    )

    return jax.shard_map(
        shards, mesh=mesh, in_specs=placed, out_specs=(cells, cells), check_vma=False
    )
```

```python
from functools import partial
import math

import jax
import jax.numpy as jnp
from jax import lax
from jax.experimental import pallas as pl
from jax.experimental.pallas import tpu as pltpu
from jax.sharding import PartitionSpec as P

H = 3
LANES = 128
NT = (((1,), (1,)), ((), ()))
TN = (((0,), (0,)), ((), ()))
F32 = jnp.float32
BF16 = jnp.bfloat16


def mate(i, q, n):
    j = i + 1 if (i + q) % 2 == 0 else i - 1
    return j if 0 <= j < n else None


def turns(n):
    return [q for q in (0, 1) if any(mate(i, q, n) is not None for i in range(n))]


def swap(x, qz, qx):
    strips, subs = lax.axis_size("strip"), lax.axis_size("sub")
    pairs = []
    for s in range(strips):
        for u in range(subs):
            t = s if qz is None else mate(s, qz, strips)
            v = u if qx is None else mate(u, qx, subs)
            if t is not None and v is not None:
                pairs.append((s * subs + u, t * subs + v))
    return lax.ppermute(x, ("strip", "sub"), pairs)


def plan(rows, cols):
    zs, xs = turns(lax.axis_size("strip")), turns(lax.axis_size("sub"))
    pieces = [(q, None) for q in zs]
    pieces += [(None, r) for r in xs]
    pieces += [(q, r) for q in zs for r in xs]
    base, at = {(None, None): 0}, rows * cols
    for qz, qx in pieces:
        base[qz, qx] = at
        at += (rows if qz is None else H) * (cols if qx is None else H)
    return pieces, base, at


def facing(q, extent, index):
    return jnp.where((index + q) % 2 == 0, extent - H, 0)


def scale_of(n):
    assert n & (n - 1) == 0
    return n.bit_length() - 1


def places(ids, base, rows, cols):
    total_cols = cols * lax.axis_size("sub")
    strip_at, sub_at = lax.axis_index("strip"), lax.axis_index("sub")

    def split(d, extent, index):
        side = jnp.where(d < 0, -1, jnp.where(d >= extent, 1, 0))
        inner = jnp.where(side < 0, d + H, jnp.where(side > 0, d - extent, d))
        ahead = jnp.where(index % 2 == 0, 1, -1)
        turn = jnp.where(side == 0, -1, jnp.where(side == ahead, 0, 1))
        return turn, inner

    row = lax.shift_right_arithmetic(ids, jnp.int32(scale_of(total_cols)))
    col = ids & (total_cols - 1)
    tz, dr = split(row - strip_at * rows, rows, strip_at)
    tx, dc = split(col - sub_at * cols, cols, sub_at)
    where_to = jnp.full(ids.shape, -1, jnp.int32)
    for (qz, qx), start in base.items():
        here = (tz == (-1 if qz is None else qz)) & (tx == (-1 if qx is None else qx))
        width = cols if qx is None else H
        where_to = jnp.where(here, start + dr * width + dc, where_to)
    assert scale_of(rows) + scale_of(cols) >= 0
    return where_to, (row & (rows - 1)) * cols + (col & (cols - 1))


def cuts(pieces, rows, cols, x_ref, out_refs, sems, at):
    strip_at, sub_at = lax.axis_index("strip"), lax.axis_index("sub")
    copies = []
    for i, ((qz, qx), ref) in enumerate(zip(pieces, out_refs)):
        r = pl.ds(0, rows) if qz is None else pl.ds(facing(qz, rows, strip_at), H)
        c = pl.ds(0, cols) if qx is None else pl.ds(facing(qx, cols, sub_at), H)
        copies.append(pltpu.make_async_copy(x_ref.at[r, c], ref, sems.at[at + i]))
    return copies


def loop(count, body, most=4):
    step = max(d for d in range(1, most + 1) if count % d == 0) if count else 1

    def run(i, _):
        body(i)
        return 0

    lax.fori_loop(0, count, run, 0, unroll=step)


def widen(dst, at, src_ref, px, pitch):
    def body(i):
        rows = src_ref[pl.ds(pl.multiple_of(i * px, px), px), :]
        dst[pl.ds((at + i) * pitch, px), :] = rows.astype(F32)

    loop(src_ref.shape[0] // px, body)


def clear(dst, at, end, px, pitch):
    def body(i):
        dst[pl.ds((at + i) * pitch, px), :] = jnp.zeros((px, dst.shape[1]), F32)

    loop(end - at, body)


def hot(row, tile=0):
    e = lax.broadcasted_iota(jnp.int32, (LANES, LANES), 0) + tile * LANES
    return (e == row).astype(F32).astype(BF16)


def pick_hot(e_ref, b, slots, tile):
    group, j = divmod(b, LANES // slots)
    lane = lax.broadcasted_iota(jnp.int32, (1, LANES), 1) // slots
    return hot(jnp.where(lane == j, e_ref[group : group + 1, :], -1), tile)


def cut_kernel(pieces, rows, cols, x_ref, *refs):
    copies = cuts(pieces, rows, cols, x_ref, refs[:-1], refs[-1], 0)
    for copy in copies:
        copy.start()
    for copy in copies:
        copy.wait()


def slotted(x, out_ref, table, slots):
    n, picks = x.shape
    per = LANES // slots
    table[...] = jnp.full(table.shape, -1, jnp.int32)
    table[:, :picks] = x
    lane = lax.broadcasted_iota(jnp.int32, (n // per, LANES), 1) // slots
    acc = jnp.full((n // per, LANES), -1, jnp.int32)
    for j in range(per):
        rows = table[pl.ds(j, n // per, stride=per), :]
        acc = jnp.where(lane == j, rows if j == 0 else pltpu.roll(rows, j * slots, 1), acc)
    out_ref[...] = acc


def head_kernel(base, pieces, rows, cols, slots, *refs):
    k = len(pieces)
    far, rest = refs[:7], refs[7:]
    src_slabs, outs, rest = rest[:k], rest[k : k + 8], rest[k + 8 :]
    src_t, tgt_t, gh_ref, wt_ref, wh_ref, bt_ref, e_ref, m_ref = outs
    (s32, t32, og, table), near, sems = rest[:4], rest[4:-1], rest[-1]
    src_ref, tgt_ref, og_ref, ids_ref, w_in_ref, b_ref, w_out_ref = near
    fetches = [pltpu.make_async_copy(f, v, sems.at[i]) for i, (f, v) in enumerate(zip(far, near))]
    slabs = cuts(pieces, rows, cols, far[0], src_slabs, sems, 7)
    for copy in fetches[2:] + fetches[:2] + slabs:
        copy.start()
    px, n, _ = src_t.shape
    pitch = px + 1
    for fetch in fetches[2:]:
        fetch.wait()
    e_at, m_at = places(ids_ref[...], base, rows, cols)
    slotted(e_at, e_ref, table, slots)
    slotted(m_at, m_ref, table, slots)
    wt_ref[...] = w_in_ref[...].T
    rep = lax.axis_index("rep")
    wh_ref[...] = w_in_ref[pl.ds(pl.multiple_of(rep * px, px), px), :]
    bt_ref[...] = jnp.broadcast_to(b_ref[...], (LANES, b_ref.shape[1])).T
    picks = og_ref.shape[1]
    og[...] = jnp.zeros_like(og)
    for r in range(rows):
        for pick in range(picks):
            at = r * cols * (slots + 1) + pick
            og[pl.ds(at, cols, stride=slots + 1), :] = og_ref[r, pick].astype(F32)
    per = LANES // slots
    for g in range(n // per):
        block = jnp.concatenate(
            [og[b * (slots + 1) : b * (slots + 1) + slots, :] for b in range(g * per, (g + 1) * per)]
        ).astype(BF16)
        gh_ref[:, g * LANES : (g + 1) * LANES] = lax.dot_general(
            w_out_ref[...], block, NT, preferred_element_type=F32
        )
    for fetch in fetches[:2]:
        fetch.wait()
    for dst, src in ((s32, src_ref), (t32, tgt_ref)):

        def body(i, dst=dst, src=src):
            rows_of = src[i // cols, lax.rem(i, cols)]
            dst[pl.ds(i * pitch, px), :] = rows_of.astype(F32)

        loop(n, body, 8)

    def turn(p):
        src_t[p] = s32[pl.ds(p, n, stride=pitch), :].astype(BF16)
        tgt_t[p] = t32[pl.ds(p, n, stride=pitch), :].astype(BF16)

    loop(px, turn, 8)
    for copy in slabs:
        copy.wait()


def corr_kernel(px, n, ext, starts, slots, *refs):
    k = len(starts)
    own_t, src_t, e_ref, tgt_refs = refs[0], refs[1], refs[2], refs[3 : 3 + k]
    costs_ref, tgt_t, hot_ref, t32, corr = refs[3 + k :]
    ext_pad = tgt_t.shape[1]
    tiles = ext_pad // LANES
    pitch = px + 1
    inv_root = 1.0 / math.sqrt(tgt_t.shape[2])
    for start, ref in zip(starts, tgt_refs):
        widen(t32, start - n, ref, px, pitch)
    clear(t32, ext - n, ext_pad - n, px, pitch)

    def per_pixel(p):
        tp = t32[pl.ds(p, ext_pad - n, stride=pitch), :].astype(BF16)
        tp = jnp.concatenate([own_t[p], tp], axis=0)
        tgt_t[p] = tp
        c = lax.dot_general(src_t[p], tp, NT, preferred_element_type=F32) * inv_root
        for t in range(tiles):
            corr[t, pl.ds(p, n, stride=pitch), :] = c[:, t * LANES : (t + 1) * LANES]

    loop(px, per_pixel, px)
    per = LANES // slots
    for g in range(n // per):
        left = []
        for j in range(per):
            b = g * per + j
            for t in range(tiles):
                at = (b * tiles + t) * LANES
                hot_ref[at : at + LANES, :] = pick_hot(e_ref, b, slots, t)
                left.append(corr[t, b * pitch : b * pitch + px, :].astype(BF16))
        high = per * tiles * LANES
        costs_ref[:, g * LANES : (g + 1) * LANES] = jnp.dot(
            jnp.concatenate(left, axis=1),
            hot_ref[g * high : (g + 1) * high, :],
            preferred_element_type=F32,
        ).astype(BF16)


def gelu_slope(x):
    c = math.sqrt(2.0 / math.pi)
    x2 = x * x
    th = jnp.tanh(x * (c + (c * 0.044715) * x2))
    inner = x * (c + (c * 3.0 * 0.044715) * x2)
    return (0.5 + 0.5 * th) * (1.0 + (1.0 - th) * inner)


def decoder_kernel(rows, cols, slots, pieces, *refs):
    mine_ref, other_ref, gh_ref, wt_ref, bt_ref, w_ref, table_ref = refs[:7]
    gc_ref, out_refs, whole = refs[7], refs[8:-1], refs[-1]
    px = mine_ref.shape[0]
    rep = lax.axis_index("rep")
    whole[pl.ds(pl.multiple_of(rep * px, px), px), :] = mine_ref[...]
    whole[pl.ds(pl.multiple_of((1 - rep) * px, px), px), :] = other_ref[...]
    w_half = w_ref[...]
    wide = 2
    bias = jnp.concatenate([bt_ref[...]] * wide, axis=1)
    width = wide * LANES
    for g in range(mine_ref.shape[1] // width):
        cut = slice(g * width, (g + 1) * width)
        pre = jnp.dot(wt_ref[...], whole[:, cut], preferred_element_type=F32) + bias
        grad = (gh_ref[:, cut] * gelu_slope(pre)).astype(BF16)
        gc_ref[:, cut] = jnp.dot(w_half, grad, preferred_element_type=F32).astype(BF16)
    send(rows, cols, slots, pieces, gc_ref, table_ref, out_refs)


def picked(rows, cols, per, piece):
    qz, qx = piece
    strip_at, sub_at = lax.axis_index("strip"), lax.axis_index("sub")
    wide = cols // per
    r0 = 0 if qz is None else facing(qz, rows, strip_at)
    tail = None if qx is None else (sub_at + qx) % 2 == 0
    half = 0 if qx is None else jnp.where(tail, (cols - H) // per, 0)
    shift = 0 if qx is None else jnp.where(tail, (cols - H) % per, 0)
    groups = [
        (r0 + r) * wide + half + h
        for r in range(rows if qz is None else H)
        for h in range(wide if qx is None else 1)
    ]
    return groups, shift


def table_kernel(rows, cols, slots, pieces, starts, counts, e_ref, m_ref, out_ref):
    per = LANES // slots
    lane = lax.broadcasted_iota(jnp.int32, (1, LANES), 1) // slots
    i = 0
    for piece, start, count in zip(pieces, starts, counts):
        groups, shift = picked(rows, cols, per, piece)
        for g in groups:
            e, m = e_ref[pl.ds(g, 1), :], m_ref[pl.ds(g, 1), :]
            here = (e >= start) & (e < start + count)
            out_ref[i * LANES : (i + 1) * LANES, :] = hot(
                jnp.where(here, (lane - shift) * slots + m, -1)
            )
            i += 1


def send(rows, cols, slots, pieces, gc_ref, table_ref, out_refs):
    per = LANES // slots
    i = 0
    for piece, ref in zip(pieces, out_refs):
        groups, _ = picked(rows, cols, per, piece)
        for at, g in enumerate(groups):
            lane = g * LANES
            lane = lane if isinstance(lane, int) else pl.multiple_of(lane, LANES)
            ref[:, at * LANES : (at + 1) * LANES] = lax.dot_general(
                gc_ref[:, pl.ds(lane, LANES)],
                table_ref[i * LANES : (i + 1) * LANES, :],
                NT,
                preferred_element_type=F32,
            ).astype(BF16)
            i += 1


def own_kernel(px, n, slots, gc_ref, hot_ref, tgt_t, src_t, sg_ref, own_ref, pw, s32):
    ext_pad = tgt_t.shape[1]
    pitch = px + 1
    inv_root = 1.0 / math.sqrt(tgt_t.shape[2])
    tiles = ext_pad // LANES
    per = LANES // slots
    high = per * tiles * LANES
    for g in range(n // per):
        w = lax.dot_general(
            gc_ref[:, g * LANES : (g + 1) * LANES],
            hot_ref[g * high : (g + 1) * high, :],
            NT,
            preferred_element_type=F32,
        )
        for j in range(per):
            b = g * per + j
            for t in range(tiles):
                at = (j * tiles + t) * LANES
                pw[t, b * pitch : b * pitch + px, :] = w[:, at : at + LANES]

    def per_pixel(p):
        tp = tgt_t[p]
        sg = jnp.zeros((n, tp.shape[1]), F32)
        for t in range(tiles):
            w = pw[t, pl.ds(p, n, stride=pitch), :].astype(BF16)
            sg += jnp.dot(w, tp[t * LANES : (t + 1) * LANES, :], preferred_element_type=F32)
            if t == 0:
                own_ref[p] = lax.dot_general(
                    w[:, :n], src_t[p], TN, preferred_element_type=F32
                )
        s32[pl.ds(p, n, stride=pitch), :] = sg * inv_root

    loop(px, per_pixel, px)

    def narrow(i):
        sg_ref[pl.ds(pl.multiple_of(i * px, px), px), :] = s32[pl.ds(i * pitch, px), :].astype(BF16)

    loop(n, narrow)


def halo_kernel(px, starts, *refs):
    k = len(starts)
    src_refs, out, s32 = refs[:k], refs[k], refs[k + 1]
    pitch = px + 1
    for start, ref in zip(starts, src_refs):
        widen(s32, start, ref, px, pitch)
    last = starts[-1] + src_refs[-1].shape[0] // px
    clear(s32, last, out.shape[1], px, pitch)

    def turn(p):
        out[p] = s32[pl.ds(p, out.shape[1], stride=pitch), :].astype(BF16)

    loop(px, turn, 8)


def total_kernel(px, n, slots, widths, own_ref, halo_t, *refs):
    k = len(widths)
    msg_refs, tg_ref, pw, t32 = refs[:k], refs[k], refs[k + 1], refs[k + 2]
    pitch = px + 1
    inv_root = 1.0 / math.sqrt(own_ref.shape[2])
    at = 0
    for width, ref in zip(widths, msg_refs):
        for g in range(ref.shape[1] // LANES):
            block = ref[:, g * LANES : (g + 1) * LANES].astype(F32)
            for j in range(width):
                turned = block if j == 0 else pltpu.roll(block, LANES - j * slots, 1)
                pw[at * pitch : at * pitch + px, :] = turned
                at += 1
    clear(pw, at, halo_t.shape[1], px, pitch)

    def per_pixel(p):
        w = pw[pl.ds(p, halo_t.shape[1], stride=pitch), :]
        tg = own_ref[p] + lax.dot_general(
            w[:, :n].astype(BF16), halo_t[p], TN, preferred_element_type=F32
        )
        t32[pl.ds(p, n, stride=pitch), :] = tg * inv_root

    loop(px, per_pixel, px // 2)

    def narrow(i):
        tg_ref[pl.ds(pl.multiple_of(i * px, px), px), :] = t32[pl.ds(i * pitch, px), :].astype(BF16)

    loop(n, narrow)


VM = pl.BlockSpec(memory_space=pltpu.VMEM)
HB = pl.BlockSpec(memory_space=pltpu.HBM)


def call(kernel, outs, scratch, args, us=2.0, far=0, sems=0, limit=24, near=False):
    return pl.pallas_call(
        kernel,
        out_shape=[pltpu.VMEM(s, d) if near else jax.ShapeDtypeStruct(s, d) for s, d in outs],
        in_specs=[HB] * far + [VM] * (len(args) - far),
        out_specs=[VM] * len(outs),
        scratch_shapes=[pltpu.VMEM(s, d) for s, d in scratch]
        + ([pltpu.VMEM(x.shape, x.dtype) for x in args[:far]] if far else [])
        + ([pltpu.SemaphoreType.DMA((sems,))] if far else []),
        compiler_params=pltpu.CompilerParams(vmem_limit_bytes=limit * 2**20),
        cost_estimate=pl.CostEstimate(
            flops=0, bytes_accessed=int(us * 3 * 10**6), transcendentals=0
        ),
    )(*args)


def shards(source, target, target_ids, out_grad, w_in, b_in, w_out):
    rows, cols, px, channels = source.shape
    picks = target_ids.shape[2]
    n = rows * cols
    pitch = px + 1
    slots = 1 << (picks - 1).bit_length()
    per = LANES // slots
    groups = n // per
    assert n <= slots and cols % per == 0 and H <= per and groups * per == n
    pieces, base, ext = plan(rows, cols)
    ext_pad = -(-ext // LANES) * LANES

    shapes = [
        (rows if qz is None else H, cols if qx is None else H, px, channels) for qz, qx in pieces
    ]

    hidden = w_in.shape[1]
    outs = [(s, BF16) for s in shapes] + [
        ((px, n, channels), BF16),
        ((px, n, channels), BF16),
        ((hidden, n * slots), F32),
        ((hidden, 2 * px), BF16),
        ((px, hidden), BF16),
        ((hidden, LANES), F32),
        ((groups, LANES), jnp.int32),
        ((groups, LANES), jnp.int32),
    ]
    args = (
        source,
        target,
        jnp.swapaxes(out_grad, 1, 2),
        target_ids.reshape(n, picks),
        w_in,
        b_in.reshape(1, hidden),
        w_out,
    )
    args = tuple(pltpu.with_memory_space_constraint(a, pltpu.HBM) for a in args)
    made = call(
        partial(head_kernel, base, pieces, rows, cols, slots),
        outs,
        [((n * pitch, channels), F32)] * 2
        + [((n * (slots + 1), out_grad.shape[3]), F32), ((n, LANES), jnp.int32)],
        args,
        far=len(args),
        sems=len(args) + len(pieces),
        limit=24,
    )
    k = len(pieces)
    src_t, own_t, grad_hidden, w_t, w_half, b_t, e_ids, m_ids = made[k:]
    cut_t = pl.pallas_call(
        partial(cut_kernel, pieces, rows, cols),
        name="cut",
        out_shape=[jax.ShapeDtypeStruct(s, BF16) for s in shapes],
        in_specs=[HB],
        out_specs=[VM] * k,
        scratch_shapes=[pltpu.SemaphoreType.DMA((k,))],
        compiler_params=pltpu.CompilerParams(vmem_limit_bytes=4 * 2**20),
    )(args[1])

    def halo_of(slabs):
        got = []
        for x, (qz, qx) in zip(slabs, pieces):
            got.append(swap(x, qz, qx).reshape(-1, channels))
        return got

    tgt_halo = halo_of(cut_t)
    src_halo = halo_of(made[:k])
    starts = [base[q] for q in pieces]
    counts = [h.shape[0] // px for h in tgt_halo]
    costs, tgt_t, hots = call(
        partial(corr_kernel, px, n, ext, starts, slots),
        [
            ((px, n * slots), BF16),
            ((px, ext_pad, channels), BF16),
            ((n * ext_pad, LANES), BF16),
        ],
        [
            (((ext_pad - n) * pitch, channels), F32),
            ((ext_pad // LANES, n * pitch, LANES), F32),
        ],
        (own_t, src_t, e_ids, *tgt_halo),
        us=3,
    )
    reps = lax.axis_size("rep")
    other = lax.ppermute(costs, "rep", [(i, reps - 1 - i) for i in range(reps)])
    lanes = [
        (rows if qz is None else H) * (cols // per if qx is None else 1) * LANES
        for qz, qx in pieces
    ]
    (tables,) = call(
        partial(table_kernel, rows, cols, slots, pieces, starts, counts),
        [((sum(lanes), LANES), BF16)],
        [],
        (e_ids, m_ids),
        us=0.5,
    )
    gc, *sent = call(
        partial(decoder_kernel, rows, cols, slots, pieces),
        [((px, n * slots), BF16)] + [((px, w), BF16) for w in lanes],
        [((2 * px, n * slots), BF16)],
        (costs, other, grad_hidden, w_t, b_t, w_half, tables),
        us=3,
    )
    got = []
    for x, (qz, qx) in zip(sent, pieces):
        got.append(swap(x, qz, qx))
    sg, own = call(
        partial(own_kernel, px, n, slots),
        [((n * px, channels), BF16), ((px, n, channels), F32)],
        [((ext_pad // LANES, n * pitch, LANES), F32), ((n * pitch, channels), F32)],
        (gc, hots, tgt_t, src_t),
        us=4,
    )
    halo_pad = -(-(ext - n) // 16) * 16
    (halo_t,) = call(
        partial(halo_kernel, px, [s - n for s in starts]),
        [((px, halo_pad, channels), BF16)],
        [((halo_pad * pitch, channels), F32)],
        tuple(src_halo),
        us=1,
    )
    (tg,) = call(
        partial(total_kernel, px, n, slots, [per if qx is None else H for _, qx in pieces]),
        [((n * px, channels), BF16)],
        [((halo_pad * pitch, LANES), F32), ((n * pitch, channels), F32)],
        (own, halo_t, *got),
        us=3,
    )
    return sg.reshape(source.shape), tg.reshape(source.shape)


def solution(mesh):
    cells = P(("groups", "strip"), "sub", "rep", None)
    placed = (
        cells,
        cells,
        P(("groups", "strip"), "sub", None),
        P(("groups", "strip"), "sub", None, None),
        P(),
        P(),
        P(),
    )

    return jax.shard_map(
        shards, mesh=mesh, in_specs=placed, out_specs=(cells, cells), check_vma=False
    )
```

```python
from functools import partial
import math

import jax
import jax.numpy as jnp
from jax import lax
from jax.experimental import pallas as pl
from jax.experimental.pallas import tpu as pltpu
from jax.sharding import PartitionSpec as P

H = 3
LANES = 128
NT = (((1,), (1,)), ((), ()))
TN = (((0,), (0,)), ((), ()))
F32 = jnp.float32
BF16 = jnp.bfloat16


def mate(i, q, n):
    j = i + 1 if (i + q) % 2 == 0 else i - 1
    return j if 0 <= j < n else None


def turns(n):
    return [q for q in (0, 1) if any(mate(i, q, n) is not None for i in range(n))]


def swap(x, qz, qx):
    strips, subs = lax.axis_size("strip"), lax.axis_size("sub")
    pairs = []
    for s in range(strips):
        for u in range(subs):
            t = s if qz is None else mate(s, qz, strips)
            v = u if qx is None else mate(u, qx, subs)
            if t is not None and v is not None:
                pairs.append((s * subs + u, t * subs + v))
    return lax.ppermute(x, ("strip", "sub"), pairs)


def plan(rows, cols):
    zs, xs = turns(lax.axis_size("strip")), turns(lax.axis_size("sub"))
    pieces = [(q, None) for q in zs]
    pieces += [(None, r) for r in xs]
    pieces += [(q, r) for q in zs for r in xs]
    base, at = {(None, None): 0}, rows * cols
    for qz, qx in pieces:
        base[qz, qx] = at
        at += (rows if qz is None else H) * (cols if qx is None else H)
    return pieces, base, at


def facing(q, extent, index):
    return jnp.where((index + q) % 2 == 0, extent - H, 0)


def scale_of(n):
    assert n & (n - 1) == 0
    return n.bit_length() - 1


def places(ids, base, rows, cols):
    total_cols = cols * lax.axis_size("sub")
    strip_at, sub_at = lax.axis_index("strip"), lax.axis_index("sub")

    def split(d, extent, index):
        side = jnp.where(d < 0, -1, jnp.where(d >= extent, 1, 0))
        inner = jnp.where(side < 0, d + H, jnp.where(side > 0, d - extent, d))
        ahead = jnp.where(index % 2 == 0, 1, -1)
        turn = jnp.where(side == 0, -1, jnp.where(side == ahead, 0, 1))
        return turn, inner

    row = lax.shift_right_arithmetic(ids, jnp.int32(scale_of(total_cols)))
    col = ids & (total_cols - 1)
    tz, dr = split(row - strip_at * rows, rows, strip_at)
    tx, dc = split(col - sub_at * cols, cols, sub_at)
    where_to = jnp.full(ids.shape, -1, jnp.int32)
    for (qz, qx), start in base.items():
        here = (tz == (-1 if qz is None else qz)) & (tx == (-1 if qx is None else qx))
        width = cols if qx is None else H
        where_to = jnp.where(here, start + dr * width + dc, where_to)
    assert scale_of(rows) + scale_of(cols) >= 0
    return where_to, (row & (rows - 1)) * cols + (col & (cols - 1))


def cuts(pieces, rows, cols, x_ref, out_refs, sems, at):
    strip_at, sub_at = lax.axis_index("strip"), lax.axis_index("sub")
    copies = []
    for i, ((qz, qx), ref) in enumerate(zip(pieces, out_refs)):
        r = pl.ds(0, rows) if qz is None else pl.ds(facing(qz, rows, strip_at), H)
        c = pl.ds(0, cols) if qx is None else pl.ds(facing(qx, cols, sub_at), H)
        copies.append(pltpu.make_async_copy(x_ref.at[r, c], ref, sems.at[at + i]))
    return copies


def loop(count, body, most=4):
    step = max(d for d in range(1, most + 1) if count % d == 0) if count else 1

    def run(i, _):
        body(i)
        return 0

    lax.fori_loop(0, count, run, 0, unroll=step)


def widen(dst, at, src_ref, px, pitch):
    def body(i):
        rows = src_ref[pl.ds(pl.multiple_of(i * px, px), px), :]
        dst[pl.ds((at + i) * pitch, px), :] = rows.astype(F32)

    loop(src_ref.shape[0] // px, body)


def clear(dst, at, end, px, pitch):
    def body(i):
        dst[pl.ds((at + i) * pitch, px), :] = jnp.zeros((px, dst.shape[1]), F32)

    loop(end - at, body)


def hot(row, tile=0):
    e = lax.broadcasted_iota(jnp.int32, (LANES, LANES), 0) + tile * LANES
    return (e == row).astype(F32).astype(BF16)


def pick_hot(e_ref, b, slots, tile):
    group, j = divmod(b, LANES // slots)
    lane = lax.broadcasted_iota(jnp.int32, (1, LANES), 1) // slots
    return hot(jnp.where(lane == j, e_ref[group : group + 1, :], -1), tile)


def cut_kernel(pieces, rows, cols, x_ref, *refs):
    copies = cuts(pieces, rows, cols, x_ref, refs[:-1], refs[-1], 0)
    for copy in copies:
        copy.start()
    for copy in copies:
        copy.wait()


def slotted(x, out_ref, table, slots):
    n, picks = x.shape
    per = LANES // slots
    table[...] = jnp.full(table.shape, -1, jnp.int32)
    table[:, :picks] = x
    lane = lax.broadcasted_iota(jnp.int32, (n // per, LANES), 1) // slots
    acc = jnp.full((n // per, LANES), -1, jnp.int32)
    for j in range(per):
        rows = table[pl.ds(j, n // per, stride=per), :]
        acc = jnp.where(lane == j, rows if j == 0 else pltpu.roll(rows, j * slots, 1), acc)
    out_ref[...] = acc


def head_kernel(base, pieces, rows, cols, slots, *refs):
    k = len(pieces)
    far, rest = refs[:7], refs[7:]
    src_slabs, outs, rest = rest[:k], rest[k : k + 8], rest[k + 8 :]
    src_t, tgt_t, gh_ref, wt_ref, wh_ref, bt_ref, e_ref, m_ref = outs
    (s32, t32, og, table), near, sems = rest[:4], rest[4:-1], rest[-1]
    src_ref, tgt_ref, og_ref, ids_ref, w_in_ref, b_ref, w_out_ref = near
    fetches = [pltpu.make_async_copy(f, v, sems.at[i]) for i, (f, v) in enumerate(zip(far, near))]
    slabs = cuts(pieces, rows, cols, far[0], src_slabs, sems, 7)
    for copy in fetches[2:] + fetches[:2] + slabs:
        copy.start()
    px, n, _ = src_t.shape
    pitch = px + 1
    for fetch in fetches[2:]:
        fetch.wait()
    e_at, m_at = places(ids_ref[...], base, rows, cols)
    slotted(e_at, e_ref, table, slots)
    slotted(m_at, m_ref, table, slots)
    wt_ref[...] = w_in_ref[...].T
    rep = lax.axis_index("rep")
    wh_ref[...] = w_in_ref[pl.ds(pl.multiple_of(rep * px, px), px), :]
    bt_ref[...] = jnp.broadcast_to(b_ref[...], (LANES, b_ref.shape[1])).T
    picks = og_ref.shape[1]
    og[...] = jnp.zeros_like(og)
    for r in range(rows):
        for pick in range(picks):
            at = r * cols * (slots + 1) + pick
            og[pl.ds(at, cols, stride=slots + 1), :] = og_ref[r, pick].astype(F32)
    per = LANES // slots
    for g in range(n // per):
        block = jnp.concatenate(
            [og[b * (slots + 1) : b * (slots + 1) + slots, :] for b in range(g * per, (g + 1) * per)]
        ).astype(BF16)
        gh_ref[:, g * LANES : (g + 1) * LANES] = lax.dot_general(
            w_out_ref[...], block, NT, preferred_element_type=F32
        )
    for fetch in fetches[:2]:
        fetch.wait()
    for dst, src in ((s32, src_ref), (t32, tgt_ref)):

        def body(i, dst=dst, src=src):
            rows_of = src[i // cols, lax.rem(i, cols)]
            dst[pl.ds(i * pitch, px), :] = rows_of.astype(F32)

        loop(n, body, 8)

    def turn(p):
        src_t[p] = s32[pl.ds(p, n, stride=pitch), :].astype(BF16)
        tgt_t[p] = t32[pl.ds(p, n, stride=pitch), :].astype(BF16)

    loop(px, turn, 8)
    for copy in slabs:
        copy.wait()


def corr_kernel(px, n, ext, starts, slots, *refs):
    k = len(starts)
    own_t, src_t, e_ref, tgt_refs = refs[0], refs[1], refs[2], refs[3 : 3 + k]
    costs_ref, tgt_t, hot_ref, t32, corr = refs[3 + k :]
    ext_pad = tgt_t.shape[1]
    tiles = ext_pad // LANES
    pitch = px + 1
    inv_root = 1.0 / math.sqrt(tgt_t.shape[2])
    for start, ref in zip(starts, tgt_refs):
        widen(t32, start - n, ref, px, pitch)
    clear(t32, ext - n, ext_pad - n, px, pitch)

    def per_pixel(p):
        tp = t32[pl.ds(p, ext_pad - n, stride=pitch), :].astype(BF16)
        tp = jnp.concatenate([own_t[p], tp], axis=0)
        tgt_t[p] = tp
        c = lax.dot_general(src_t[p], tp, NT, preferred_element_type=F32) * inv_root
        for t in range(tiles):
            corr[t, pl.ds(p, n, stride=pitch), :] = c[:, t * LANES : (t + 1) * LANES]

    loop(px, per_pixel, px)
    per = LANES // slots
    for g in range(n // per):
        left = []
        for j in range(per):
            b = g * per + j
            for t in range(tiles):
                at = (b * tiles + t) * LANES
                hot_ref[at : at + LANES, :] = pick_hot(e_ref, b, slots, t)
                left.append(corr[t, b * pitch : b * pitch + px, :].astype(BF16))
        high = per * tiles * LANES
        costs_ref[:, g * LANES : (g + 1) * LANES] = jnp.dot(
            jnp.concatenate(left, axis=1),
            hot_ref[g * high : (g + 1) * high, :],
            preferred_element_type=F32,
        ).astype(BF16)


def gelu_slope(x):
    c = math.sqrt(2.0 / math.pi)
    x2 = x * x
    th = jnp.tanh(x * (c + (c * 0.044715) * x2))
    inner = x * (c + (c * 3.0 * 0.044715) * x2)
    return (0.5 + 0.5 * th) * (1.0 + (1.0 - th) * inner)


def decoder_kernel(rows, cols, slots, pieces, *refs):
    mine_ref, other_ref, gh_ref, wt_ref, bt_ref, w_ref, table_ref = refs[:7]
    gc_ref, out_refs, whole = refs[7], refs[8:-1], refs[-1]
    px = mine_ref.shape[0]
    rep = lax.axis_index("rep")
    whole[pl.ds(pl.multiple_of(rep * px, px), px), :] = mine_ref[...]
    whole[pl.ds(pl.multiple_of((1 - rep) * px, px), px), :] = other_ref[...]
    w_half = w_ref[...]
    bias = jnp.concatenate([bt_ref[...]] * (mine_ref.shape[1] // LANES), axis=1)
    pre = jnp.dot(wt_ref[...], whole[...], preferred_element_type=F32) + bias
    grad = (gh_ref[...] * gelu_slope(pre)).astype(BF16)
    gc_ref[...] = jnp.dot(w_half, grad, preferred_element_type=F32).astype(BF16)
    send(rows, cols, slots, pieces, gc_ref, table_ref, out_refs)


def picked(rows, cols, per, piece):
    qz, qx = piece
    strip_at, sub_at = lax.axis_index("strip"), lax.axis_index("sub")
    wide = cols // per
    r0 = 0 if qz is None else facing(qz, rows, strip_at)
    tail = None if qx is None else (sub_at + qx) % 2 == 0
    half = 0 if qx is None else jnp.where(tail, (cols - H) // per, 0)
    shift = 0 if qx is None else jnp.where(tail, (cols - H) % per, 0)
    groups = [
        (r0 + r) * wide + half + h
        for r in range(rows if qz is None else H)
        for h in range(wide if qx is None else 1)
    ]
    return groups, shift


def table_kernel(rows, cols, slots, pieces, starts, counts, e_ref, m_ref, out_ref):
    per = LANES // slots
    lane = lax.broadcasted_iota(jnp.int32, (1, LANES), 1) // slots
    i = 0
    for piece, start, count in zip(pieces, starts, counts):
        groups, shift = picked(rows, cols, per, piece)
        for g in groups:
            e, m = e_ref[pl.ds(g, 1), :], m_ref[pl.ds(g, 1), :]
            here = (e >= start) & (e < start + count)
            out_ref[i * LANES : (i + 1) * LANES, :] = hot(
                jnp.where(here, (lane - shift) * slots + m, -1)
            )
            i += 1


def send(rows, cols, slots, pieces, gc_ref, table_ref, out_refs):
    per = LANES // slots
    i = 0
    for piece, ref in zip(pieces, out_refs):
        groups, _ = picked(rows, cols, per, piece)
        for at, g in enumerate(groups):
            lane = g * LANES
            lane = lane if isinstance(lane, int) else pl.multiple_of(lane, LANES)
            ref[:, at * LANES : (at + 1) * LANES] = lax.dot_general(
                gc_ref[:, pl.ds(lane, LANES)],
                table_ref[i * LANES : (i + 1) * LANES, :],
                NT,
                preferred_element_type=F32,
            ).astype(BF16)
            i += 1


def own_kernel(px, n, slots, gc_ref, hot_ref, tgt_t, sg_ref, pw, s32):
    ext_pad = tgt_t.shape[1]
    pitch = px + 1
    inv_root = 1.0 / math.sqrt(tgt_t.shape[2])
    tiles = ext_pad // LANES
    per = LANES // slots
    high = per * tiles * LANES
    for g in range(n // per):
        w = lax.dot_general(
            gc_ref[:, g * LANES : (g + 1) * LANES],
            hot_ref[g * high : (g + 1) * high, :],
            NT,
            preferred_element_type=F32,
        )
        for j in range(per):
            b = g * per + j
            for t in range(tiles):
                at = (j * tiles + t) * LANES
                pw[t, b * pitch : b * pitch + px, :] = w[:, at : at + LANES]

    def per_pixel(p):
        tp = tgt_t[p]
        sg = jnp.zeros((n, tp.shape[1]), F32)
        for t in range(tiles):
            w = pw[t, pl.ds(p, n, stride=pitch), :].astype(BF16)
            sg += jnp.dot(w, tp[t * LANES : (t + 1) * LANES, :], preferred_element_type=F32)
        s32[pl.ds(p, n, stride=pitch), :] = sg * inv_root

    loop(px, per_pixel, px)

    def narrow(i):
        sg_ref[pl.ds(pl.multiple_of(i * px, px), px), :] = s32[pl.ds(i * pitch, px), :].astype(BF16)

    loop(n, narrow)


def halo_kernel(px, starts, *refs):
    k = len(starts)
    src_refs, out, s32 = refs[:k], refs[k], refs[k + 1]
    pitch = px + 1
    for start, ref in zip(starts, src_refs):
        widen(s32, start, ref, px, pitch)
    last = starts[-1] + src_refs[-1].shape[0] // px
    clear(s32, last, out.shape[1], px, pitch)

    def turn(p):
        out[p] = s32[pl.ds(p, out.shape[1], stride=pitch), :].astype(BF16)

    loop(px, turn, 8)


def total_kernel(px, n, slots, widths, pw_own, src_t, halo_t, *refs):
    k = len(widths)
    msg_refs, tg_ref, pw, t32 = refs[:k], refs[k], refs[k + 1], refs[k + 2]
    pitch = px + 1
    inv_root = 1.0 / math.sqrt(src_t.shape[2])
    at = 0
    for width, ref in zip(widths, msg_refs):
        for g in range(ref.shape[1] // LANES):
            block = ref[:, g * LANES : (g + 1) * LANES].astype(F32)
            for j in range(width):
                turned = block if j == 0 else pltpu.roll(block, LANES - j * slots, 1)
                pw[at * pitch : at * pitch + px, :] = turned
                at += 1
    clear(pw, at, halo_t.shape[1], px, pitch)

    def per_pixel(p):
        near = pw_own[0, pl.ds(p, n, stride=pitch), :]
        far = pw[pl.ds(p, halo_t.shape[1], stride=pitch), :]
        w = jnp.concatenate([near, far], axis=0)[:, :n].astype(BF16)
        s = jnp.concatenate([src_t[p], halo_t[p]], axis=0)
        tg = lax.dot_general(w, s, TN, preferred_element_type=F32)
        t32[pl.ds(p, n, stride=pitch), :] = tg * inv_root

    loop(px, per_pixel, px // 2)

    def narrow(i):
        tg_ref[pl.ds(pl.multiple_of(i * px, px), px), :] = t32[pl.ds(i * pitch, px), :].astype(BF16)

    loop(n, narrow)


VM = pl.BlockSpec(memory_space=pltpu.VMEM)
HB = pl.BlockSpec(memory_space=pltpu.HBM)


def call(kernel, outs, scratch, args, us=2.0, far=0, sems=0, limit=24, near=False):
    return pl.pallas_call(
        kernel,
        out_shape=[pltpu.VMEM(s, d) if near else jax.ShapeDtypeStruct(s, d) for s, d in outs],
        in_specs=[HB] * far + [VM] * (len(args) - far),
        out_specs=[VM] * len(outs),
        scratch_shapes=[pltpu.VMEM(s, d) for s, d in scratch]
        + ([pltpu.VMEM(x.shape, x.dtype) for x in args[:far]] if far else [])
        + ([pltpu.SemaphoreType.DMA((sems,))] if far else []),
        compiler_params=pltpu.CompilerParams(vmem_limit_bytes=limit * 2**20),
        cost_estimate=pl.CostEstimate(
            flops=0, bytes_accessed=int(us * 3 * 10**6), transcendentals=0
        ),
    )(*args)


def shards(source, target, target_ids, out_grad, w_in, b_in, w_out):
    rows, cols, px, channels = source.shape
    picks = target_ids.shape[2]
    n = rows * cols
    pitch = px + 1
    slots = 1 << (picks - 1).bit_length()
    per = LANES // slots
    groups = n // per
    assert n <= slots and cols % per == 0 and H <= per and groups * per == n
    pieces, base, ext = plan(rows, cols)
    ext_pad = -(-ext // LANES) * LANES

    shapes = [
        (rows if qz is None else H, cols if qx is None else H, px, channels) for qz, qx in pieces
    ]

    hidden = w_in.shape[1]
    outs = [(s, BF16) for s in shapes] + [
        ((px, n, channels), BF16),
        ((px, n, channels), BF16),
        ((hidden, n * slots), F32),
        ((hidden, 2 * px), BF16),
        ((px, hidden), BF16),
        ((hidden, LANES), F32),
        ((groups, LANES), jnp.int32),
        ((groups, LANES), jnp.int32),
    ]
    args = (
        source,
        target,
        jnp.swapaxes(out_grad, 1, 2),
        target_ids.reshape(n, picks),
        w_in,
        b_in.reshape(1, hidden),
        w_out,
    )
    args = tuple(pltpu.with_memory_space_constraint(a, pltpu.HBM) for a in args)
    made = call(
        partial(head_kernel, base, pieces, rows, cols, slots),
        outs,
        [((n * pitch, channels), F32)] * 2
        + [((n * (slots + 1), out_grad.shape[3]), F32), ((n, LANES), jnp.int32)],
        args,
        far=len(args),
        sems=len(args) + len(pieces),
        limit=24,
    )
    k = len(pieces)
    src_t, own_t, grad_hidden, w_t, w_half, b_t, e_ids, m_ids = made[k:]
    cut_t = pl.pallas_call(
        partial(cut_kernel, pieces, rows, cols),
        name="cut",
        out_shape=[jax.ShapeDtypeStruct(s, BF16) for s in shapes],
        in_specs=[HB],
        out_specs=[VM] * k,
        scratch_shapes=[pltpu.SemaphoreType.DMA((k,))],
        compiler_params=pltpu.CompilerParams(vmem_limit_bytes=4 * 2**20),
    )(args[1])

    def halo_of(slabs):
        got = []
        for x, (qz, qx) in zip(slabs, pieces):
            got.append(swap(x, qz, qx).reshape(-1, channels))
        return got

    tgt_halo = halo_of(cut_t)
    src_halo = halo_of(made[:k])
    starts = [base[q] for q in pieces]
    counts = [h.shape[0] // px for h in tgt_halo]
    costs, tgt_t, hots = call(
        partial(corr_kernel, px, n, ext, starts, slots),
        [
            ((px, n * slots), BF16),
            ((px, ext_pad, channels), BF16),
            ((n * ext_pad, LANES), BF16),
        ],
        [
            (((ext_pad - n) * pitch, channels), F32),
            ((ext_pad // LANES, n * pitch, LANES), F32),
        ],
        (own_t, src_t, e_ids, *tgt_halo),
        us=3,
    )
    reps = lax.axis_size("rep")
    other = lax.ppermute(costs, "rep", [(i, reps - 1 - i) for i in range(reps)])
    lanes = [
        (rows if qz is None else H) * (cols // per if qx is None else 1) * LANES
        for qz, qx in pieces
    ]
    (tables,) = call(
        partial(table_kernel, rows, cols, slots, pieces, starts, counts),
        [((sum(lanes), LANES), BF16)],
        [],
        (e_ids, m_ids),
        us=0.5,
    )
    gc, *sent = call(
        partial(decoder_kernel, rows, cols, slots, pieces),
        [((px, n * slots), BF16)] + [((px, w), BF16) for w in lanes],
        [((2 * px, n * slots), BF16)],
        (costs, other, grad_hidden, w_t, b_t, w_half, tables),
        us=3,
    )
    got = []
    for x, (qz, qx) in zip(sent, pieces):
        got.append(swap(x, qz, qx))
    sg, pw_own = call(
        partial(own_kernel, px, n, slots),
        [((n * px, channels), BF16), ((ext_pad // LANES, n * pitch, LANES), F32)],
        [((n * pitch, channels), F32)],
        (gc, hots, tgt_t),
        us=4,
    )
    halo_pad = -(-(ext - n) // 16) * 16
    (halo_t,) = call(
        partial(halo_kernel, px, [s - n for s in starts]),
        [((px, halo_pad, channels), BF16)],
        [((halo_pad * pitch, channels), F32)],
        tuple(src_halo),
        us=1,
    )
    (tg,) = call(
        partial(total_kernel, px, n, slots, [per if qx is None else H for _, qx in pieces]),
        [((n * px, channels), BF16)],
        [((halo_pad * pitch, LANES), F32), ((n * pitch, channels), F32)],
        (pw_own, src_t, halo_t, *got),
        us=3,
    )
    return sg.reshape(source.shape), tg.reshape(source.shape)


def solution(mesh):
    cells = P(("groups", "strip"), "sub", "rep", None)
    placed = (
        cells,
        cells,
        P(("groups", "strip"), "sub", None),
        P(("groups", "strip"), "sub", None, None),
        P(),
        P(),
        P(),
    )

    return jax.shard_map(
        shards, mesh=mesh, in_specs=placed, out_specs=(cells, cells), check_vma=False
    )
```

```python
from functools import partial
import math

import jax
import jax.numpy as jnp
from jax import lax
from jax.experimental import pallas as pl
from jax.experimental.pallas import tpu as pltpu
from jax.sharding import PartitionSpec as P

H = 3
LANES = 128
NT = (((1,), (1,)), ((), ()))
TN = (((0,), (0,)), ((), ()))
F32 = jnp.float32
BF16 = jnp.bfloat16


def mate(i, q, n):
    j = i + 1 if (i + q) % 2 == 0 else i - 1
    return j if 0 <= j < n else None


def turns(n):
    return [q for q in (0, 1) if any(mate(i, q, n) is not None for i in range(n))]


def swap(x, qz, qx):
    strips, subs = lax.axis_size("strip"), lax.axis_size("sub")
    pairs = []
    for s in range(strips):
        for u in range(subs):
            t = s if qz is None else mate(s, qz, strips)
            v = u if qx is None else mate(u, qx, subs)
            if t is not None and v is not None:
                pairs.append((s * subs + u, t * subs + v))
    return lax.ppermute(x, ("strip", "sub"), pairs)


def plan(rows, cols):
    zs, xs = turns(lax.axis_size("strip")), turns(lax.axis_size("sub"))
    pieces = [(q, None) for q in zs]
    pieces += [(None, r) for r in xs]
    pieces += [(q, r) for q in zs for r in xs]
    base, at = {(None, None): 0}, rows * cols
    for qz, qx in pieces:
        base[qz, qx] = at
        at += (rows if qz is None else H) * (cols if qx is None else H)
    return pieces, base, at


def joined(piece):
    return piece[0] == 1 and piece[1] is not None


def facing(q, extent, index):
    return jnp.where((index + q) % 2 == 0, extent - H, 0)


def scale_of(n):
    assert n & (n - 1) == 0
    return n.bit_length() - 1


def places(ids, base, rows, cols):
    total_cols = cols * lax.axis_size("sub")
    strip_at, sub_at = lax.axis_index("strip"), lax.axis_index("sub")

    def split(d, extent, index):
        side = jnp.where(d < 0, -1, jnp.where(d >= extent, 1, 0))
        inner = jnp.where(side < 0, d + H, jnp.where(side > 0, d - extent, d))
        ahead = jnp.where(index % 2 == 0, 1, -1)
        turn = jnp.where(side == 0, -1, jnp.where(side == ahead, 0, 1))
        return turn, inner

    row = lax.shift_right_arithmetic(ids, jnp.int32(scale_of(total_cols)))
    col = ids & (total_cols - 1)
    tz, dr = split(row - strip_at * rows, rows, strip_at)
    tx, dc = split(col - sub_at * cols, cols, sub_at)
    where_to = jnp.full(ids.shape, -1, jnp.int32)
    for (qz, qx), start in base.items():
        here = (tz == (-1 if qz is None else qz)) & (tx == (-1 if qx is None else qx))
        width = cols if qx is None else H
        where_to = jnp.where(here, start + dr * width + dc, where_to)
    assert scale_of(rows) + scale_of(cols) >= 0
    return where_to, (row & (rows - 1)) * cols + (col & (cols - 1))


def cuts(pieces, rows, cols, x_ref, out_refs, sems, at):
    strip_at, sub_at = lax.axis_index("strip"), lax.axis_index("sub")
    copies = []
    for i, ((qz, qx), ref) in enumerate(zip(pieces, out_refs)):
        r = pl.ds(0, rows) if qz is None else pl.ds(facing(qz, rows, strip_at), H)
        c = pl.ds(0, cols) if qx is None else pl.ds(facing(qx, cols, sub_at), H)
        copies.append(pltpu.make_async_copy(x_ref.at[r, c], ref, sems.at[at + i]))
    return copies


def loop(count, body, most=4):
    step = max(d for d in range(1, most + 1) if count % d == 0) if count else 1

    def run(i, _):
        body(i)
        return 0

    lax.fori_loop(0, count, run, 0, unroll=step)


def widen(dst, at, src_ref, px, pitch, count):
    def body(i):
        rows = src_ref[pl.ds(pl.multiple_of(i * px, px), px), :]
        dst[pl.ds((at + i) * pitch, px), :] = rows.astype(F32)

    loop(count, body)


def clear(dst, at, end, px, pitch):
    def body(i):
        dst[pl.ds((at + i) * pitch, px), :] = jnp.zeros((px, dst.shape[1]), F32)

    loop(end - at, body)


def hot(row, tile=0):
    e = lax.broadcasted_iota(jnp.int32, (LANES, LANES), 0) + tile * LANES
    return (e == row).astype(F32).astype(BF16)


def pick_hot(e_ref, b, slots, tile):
    group, j = divmod(b, LANES // slots)
    lane = lax.broadcasted_iota(jnp.int32, (1, LANES), 1) // slots
    return hot(jnp.where(lane == j, e_ref[group : group + 1, :], -1), tile)


def cut_kernel(pieces, rows, cols, x_ref, *refs):
    copies = cuts(pieces, rows, cols, x_ref, refs[:-1], refs[-1], 0)
    for copy in copies:
        copy.start()
    for copy in copies:
        copy.wait()


def slotted(x, out_ref, table, slots):
    n, picks = x.shape
    per = LANES // slots
    table[...] = jnp.full(table.shape, -1, jnp.int32)
    table[:, :picks] = x
    lane = lax.broadcasted_iota(jnp.int32, (n // per, LANES), 1) // slots
    acc = jnp.full((n // per, LANES), -1, jnp.int32)
    for j in range(per):
        rows = table[pl.ds(j, n // per, stride=per), :]
        acc = jnp.where(lane == j, rows if j == 0 else pltpu.roll(rows, j * slots, 1), acc)
    out_ref[...] = acc


def head_kernel(base, pieces, rows, cols, slots, *refs):
    k = len(pieces)
    far, rest = refs[:7], refs[7:]
    src_slabs, outs, rest = rest[:k], rest[k : k + 8], rest[k + 8 :]
    src_t, tgt_t, gh_ref, wt_ref, wh_ref, bt_ref, e_ref, m_ref = outs
    (s32, t32, og, table), near, sems = rest[:4], rest[4:-1], rest[-1]
    src_ref, tgt_ref, og_ref, ids_ref, w_in_ref, b_ref, w_out_ref = near
    fetches = [pltpu.make_async_copy(f, v, sems.at[i]) for i, (f, v) in enumerate(zip(far, near))]
    slabs = cuts(pieces, rows, cols, far[0], src_slabs, sems, 7)
    for copy in fetches[2:] + fetches[:2] + slabs:
        copy.start()
    px, n, _ = src_t.shape
    pitch = px + 1
    for fetch in fetches[2:]:
        fetch.wait()
    e_at, m_at = places(ids_ref[...], base, rows, cols)
    slotted(e_at, e_ref, table, slots)
    slotted(m_at, m_ref, table, slots)
    wt_ref[...] = w_in_ref[...].T
    rep = lax.axis_index("rep")
    wh_ref[...] = w_in_ref[pl.ds(pl.multiple_of(rep * px, px), px), :]
    bt_ref[...] = jnp.broadcast_to(b_ref[...], (LANES, b_ref.shape[1])).T
    picks = og_ref.shape[1]
    og[...] = jnp.zeros_like(og)
    for r in range(rows):
        for pick in range(picks):
            at = r * cols * (slots + 1) + pick
            og[pl.ds(at, cols, stride=slots + 1), :] = og_ref[r, pick].astype(F32)
    per = LANES // slots
    for g in range(n // per):
        block = jnp.concatenate(
            [og[b * (slots + 1) : b * (slots + 1) + slots, :] for b in range(g * per, (g + 1) * per)]
        ).astype(BF16)
        gh_ref[:, g * LANES : (g + 1) * LANES] = lax.dot_general(
            w_out_ref[...], block, NT, preferred_element_type=F32
        )
    for fetch in fetches[:2]:
        fetch.wait()
    for dst, src in ((s32, src_ref), (t32, tgt_ref)):

        def body(i, dst=dst, src=src):
            rows_of = src[i // cols, lax.rem(i, cols)]
            dst[pl.ds(i * pitch, px), :] = rows_of.astype(F32)

        loop(n, body, 8)

    def turn(p):
        src_t[p] = s32[pl.ds(p, n, stride=pitch), :].astype(BF16)
        tgt_t[p] = t32[pl.ds(p, n, stride=pitch), :].astype(BF16)

    loop(px, turn, 8)
    for copy in slabs:
        copy.wait()


def corr_kernel(px, n, ext, starts, slots, *refs):
    k = len(starts)
    own_t, src_t, e_ref, tgt_refs = refs[0], refs[1], refs[2], refs[3 : 3 + k]
    costs_ref, tgt_t, hot_ref, t32, corr = refs[3 + k :]
    ext_pad = tgt_t.shape[1]
    tiles = ext_pad // LANES
    pitch = px + 1
    inv_root = 1.0 / math.sqrt(tgt_t.shape[2])
    for start, ref in zip(starts, tgt_refs):
        widen(t32, start - n, ref, px, pitch, ref.shape[0] // px)
    clear(t32, ext - n, ext_pad - n, px, pitch)

    def per_pixel(p):
        tp = t32[pl.ds(p, ext_pad - n, stride=pitch), :].astype(BF16)
        tp = jnp.concatenate([own_t[p], tp], axis=0)
        tgt_t[p] = tp
        c = lax.dot_general(src_t[p], tp, NT, preferred_element_type=F32) * inv_root
        for t in range(tiles):
            corr[t, pl.ds(p, n, stride=pitch), :] = c[:, t * LANES : (t + 1) * LANES]

    loop(px, per_pixel, px)
    per = LANES // slots
    for g in range(n // per):
        left = []
        for j in range(per):
            b = g * per + j
            for t in range(tiles):
                at = (b * tiles + t) * LANES
                hot_ref[at : at + LANES, :] = pick_hot(e_ref, b, slots, t)
                left.append(corr[t, b * pitch : b * pitch + px, :].astype(BF16))
        high = per * tiles * LANES
        costs_ref[:, g * LANES : (g + 1) * LANES] = jnp.dot(
            jnp.concatenate(left, axis=1),
            hot_ref[g * high : (g + 1) * high, :],
            preferred_element_type=F32,
        ).astype(BF16)


def gelu_slope(x):
    c = math.sqrt(2.0 / math.pi)
    x2 = x * x
    th = jnp.tanh(x * (c + (c * 0.044715) * x2))
    inner = x * (c + (c * 3.0 * 0.044715) * x2)
    return (0.5 + 0.5 * th) * (1.0 + (1.0 - th) * inner)


def decoder_kernel(rows, cols, slots, pieces, *refs):
    both = sum(joined(piece) for piece in pieces)
    mine_ref, other_ref, gh_ref, wt_ref, bt_ref, w_ref, table_ref = refs[:7]
    slab_refs, rest = refs[7 : 7 + both], refs[7 + both :]
    gc_ref, out_refs, whole = rest[0], rest[1:-1], rest[-1]
    for piece, ref in zip(pieces, out_refs):
        if joined(piece):
            slab, slab_refs = slab_refs[0], slab_refs[1:]
            ref[: slab.shape[0], :] = slab[...]
    px = mine_ref.shape[0]
    rep = lax.axis_index("rep")
    whole[pl.ds(pl.multiple_of(rep * px, px), px), :] = mine_ref[...]
    whole[pl.ds(pl.multiple_of((1 - rep) * px, px), px), :] = other_ref[...]
    w_half = w_ref[...]
    bias = jnp.concatenate([bt_ref[...]] * (mine_ref.shape[1] // LANES), axis=1)
    pre = jnp.dot(wt_ref[...], whole[...], preferred_element_type=F32) + bias
    grad = (gh_ref[...] * gelu_slope(pre)).astype(BF16)
    gc_ref[...] = jnp.dot(w_half, grad, preferred_element_type=F32).astype(BF16)
    send(rows, cols, slots, pieces, gc_ref, table_ref, out_refs)


def picked(rows, cols, per, piece):
    qz, qx = piece
    strip_at, sub_at = lax.axis_index("strip"), lax.axis_index("sub")
    wide = cols // per
    r0 = 0 if qz is None else facing(qz, rows, strip_at)
    tail = None if qx is None else (sub_at + qx) % 2 == 0
    half = 0 if qx is None else jnp.where(tail, (cols - H) // per, 0)
    shift = 0 if qx is None else jnp.where(tail, (cols - H) % per, 0)
    groups = [
        (r0 + r) * wide + half + h
        for r in range(rows if qz is None else H)
        for h in range(wide if qx is None else 1)
    ]
    return groups, shift


def table_kernel(rows, cols, slots, pieces, starts, counts, e_ref, m_ref, out_ref):
    per = LANES // slots
    lane = lax.broadcasted_iota(jnp.int32, (1, LANES), 1) // slots
    i = 0
    for piece, start, count in zip(pieces, starts, counts):
        groups, shift = picked(rows, cols, per, piece)
        for g in groups:
            e, m = e_ref[pl.ds(g, 1), :], m_ref[pl.ds(g, 1), :]
            here = (e >= start) & (e < start + count)
            out_ref[i * LANES : (i + 1) * LANES, :] = hot(
                jnp.where(here, (lane - shift) * slots + m, -1)
            )
            i += 1


def send(rows, cols, slots, pieces, gc_ref, table_ref, out_refs):
    per = LANES // slots
    px = gc_ref.shape[0]
    i = 0
    for piece, ref in zip(pieces, out_refs):
        groups, _ = picked(rows, cols, per, piece)
        first = ref.shape[0] // px - len(groups)
        for at, g in enumerate(groups, first):
            lane = g * LANES
            lane = lane if isinstance(lane, int) else pl.multiple_of(lane, LANES)
            ref[at * px : (at + 1) * px, :] = lax.dot_general(
                gc_ref[:, pl.ds(lane, LANES)],
                table_ref[i * LANES : (i + 1) * LANES, :],
                NT,
                preferred_element_type=F32,
            ).astype(BF16)
            i += 1


def own_kernel(px, n, slots, gc_ref, hot_ref, tgt_t, sg_ref, pw, s32):
    ext_pad = tgt_t.shape[1]
    pitch = px + 1
    inv_root = 1.0 / math.sqrt(tgt_t.shape[2])
    tiles = ext_pad // LANES
    per = LANES // slots
    high = per * tiles * LANES
    for g in range(n // per):
        w = lax.dot_general(
            gc_ref[:, g * LANES : (g + 1) * LANES],
            hot_ref[g * high : (g + 1) * high, :],
            NT,
            preferred_element_type=F32,
        )
        for j in range(per):
            b = g * per + j
            for t in range(tiles):
                at = (j * tiles + t) * LANES
                pw[t, b * pitch : b * pitch + px, :] = w[:, at : at + LANES]

    def per_pixel(p):
        tp = tgt_t[p]
        sg = jnp.zeros((n, tp.shape[1]), F32)
        for t in range(tiles):
            w = pw[t, pl.ds(p, n, stride=pitch), :].astype(BF16)
            sg += jnp.dot(w, tp[t * LANES : (t + 1) * LANES, :], preferred_element_type=F32)
        s32[pl.ds(p, n, stride=pitch), :] = sg * inv_root

    loop(px, per_pixel, px)

    def narrow(i):
        sg_ref[pl.ds(pl.multiple_of(i * px, px), px), :] = s32[pl.ds(i * pitch, px), :].astype(BF16)

    loop(n, narrow)


def halo_kernel(px, starts, counts, *refs):
    k = len(starts)
    src_refs, out, s32 = refs[:k], refs[k], refs[k + 1]
    pitch = px + 1
    for start, count, ref in zip(starts, counts, src_refs):
        widen(s32, start, ref, px, pitch, count)
    last = starts[-1] + counts[-1]
    clear(s32, last, out.shape[1], px, pitch)

    def turn(p):
        out[p] = s32[pl.ds(p, out.shape[1], stride=pitch), :].astype(BF16)

    loop(px, turn, 8)


def total_kernel(px, n, slots, firsts, widths, pw_own, src_t, halo_t, *refs):
    k = len(widths)
    msg_refs, tg_ref, pw, t32 = refs[:k], refs[k], refs[k + 1], refs[k + 2]
    pitch = px + 1
    inv_root = 1.0 / math.sqrt(src_t.shape[2])
    at = 0
    for first, width, ref in zip(firsts, widths, msg_refs):
        for g in range(first, ref.shape[0] // px):
            block = ref[g * px : (g + 1) * px, :].astype(F32)
            for j in range(width):
                turned = block if j == 0 else pltpu.roll(block, LANES - j * slots, 1)
                pw[at * pitch : at * pitch + px, :] = turned
                at += 1
    clear(pw, at, halo_t.shape[1], px, pitch)

    def per_pixel(p):
        near = pw_own[0, pl.ds(p, n, stride=pitch), :]
        far = pw[pl.ds(p, halo_t.shape[1], stride=pitch), :]
        w = jnp.concatenate([near, far], axis=0)[:, :n].astype(BF16)
        s = jnp.concatenate([src_t[p], halo_t[p]], axis=0)
        tg = lax.dot_general(w, s, TN, preferred_element_type=F32)
        t32[pl.ds(p, n, stride=pitch), :] = tg * inv_root

    loop(px, per_pixel, px // 2)

    def narrow(i):
        tg_ref[pl.ds(pl.multiple_of(i * px, px), px), :] = t32[pl.ds(i * pitch, px), :].astype(BF16)

    loop(n, narrow)


VM = pl.BlockSpec(memory_space=pltpu.VMEM)
HB = pl.BlockSpec(memory_space=pltpu.HBM)


def call(kernel, outs, scratch, args, us=2.0, far=0, sems=0, limit=24, near=False):
    return pl.pallas_call(
        kernel,
        out_shape=[pltpu.VMEM(s, d) if near else jax.ShapeDtypeStruct(s, d) for s, d in outs],
        in_specs=[HB] * far + [VM] * (len(args) - far),
        out_specs=[VM] * len(outs),
        scratch_shapes=[pltpu.VMEM(s, d) for s, d in scratch]
        + ([pltpu.VMEM(x.shape, x.dtype) for x in args[:far]] if far else [])
        + ([pltpu.SemaphoreType.DMA((sems,))] if far else []),
        compiler_params=pltpu.CompilerParams(vmem_limit_bytes=limit * 2**20),
        cost_estimate=pl.CostEstimate(
            flops=0, bytes_accessed=int(us * 3 * 10**6), transcendentals=0
        ),
    )(*args)


def shards(source, target, target_ids, out_grad, w_in, b_in, w_out):
    rows, cols, px, channels = source.shape
    picks = target_ids.shape[2]
    n = rows * cols
    pitch = px + 1
    slots = 1 << (picks - 1).bit_length()
    per = LANES // slots
    groups = n // per
    assert n <= slots and cols % per == 0 and H <= per and groups * per == n
    pieces, base, ext = plan(rows, cols)
    ext_pad = -(-ext // LANES) * LANES

    shapes = [
        (rows if qz is None else H, cols if qx is None else H, px, channels) for qz, qx in pieces
    ]

    hidden = w_in.shape[1]
    outs = [(s, BF16) for s in shapes] + [
        ((px, n, channels), BF16),
        ((px, n, channels), BF16),
        ((hidden, n * slots), F32),
        ((hidden, 2 * px), BF16),
        ((px, hidden), BF16),
        ((hidden, LANES), F32),
        ((groups, LANES), jnp.int32),
        ((groups, LANES), jnp.int32),
    ]
    args = (
        source,
        target,
        jnp.swapaxes(out_grad, 1, 2),
        target_ids.reshape(n, picks),
        w_in,
        b_in.reshape(1, hidden),
        w_out,
    )
    args = tuple(pltpu.with_memory_space_constraint(a, pltpu.HBM) for a in args)
    made = call(
        partial(head_kernel, base, pieces, rows, cols, slots),
        outs,
        [((n * pitch, channels), F32)] * 2
        + [((n * (slots + 1), out_grad.shape[3]), F32), ((n, LANES), jnp.int32)],
        args,
        far=len(args),
        sems=len(args) + len(pieces),
        limit=24,
    )
    k = len(pieces)
    src_t, own_t, grad_hidden, w_t, w_half, b_t, e_ids, m_ids = made[k:]
    cut_t = pl.pallas_call(
        partial(cut_kernel, pieces, rows, cols),
        name="cut",
        out_shape=[jax.ShapeDtypeStruct(s, BF16) for s in shapes],
        in_specs=[HB],
        out_specs=[VM] * k,
        scratch_shapes=[pltpu.SemaphoreType.DMA((k,))],
        compiler_params=pltpu.CompilerParams(vmem_limit_bytes=4 * 2**20),
    )(args[1])

    def sent_to(arrays, there=lambda piece: True):
        got = []
        for x, (qz, qx) in zip(arrays, pieces):
            if there((qz, qx)):
                got.append(swap(x, qz, qx).reshape(-1, channels))
            else:
                got.append(None)
        return got

    assert channels == LANES
    slabs = made[:k]
    tgt_halo = sent_to(cut_t)
    src_halo = sent_to(slabs, lambda piece: not joined(piece))
    starts = [base[q] for q in pieces]
    counts = [h.shape[0] // px for h in tgt_halo]
    costs, tgt_t, hots = call(
        partial(corr_kernel, px, n, ext, starts, slots),
        [
            ((px, n * slots), BF16),
            ((px, ext_pad, channels), BF16),
            ((n * ext_pad, LANES), BF16),
        ],
        [
            (((ext_pad - n) * pitch, channels), F32),
            ((ext_pad // LANES, n * pitch, LANES), F32),
        ],
        (own_t, src_t, e_ids, *tgt_halo),
        us=3,
    )
    reps = lax.axis_size("rep")
    other = lax.ppermute(costs, "rep", [(i, reps - 1 - i) for i in range(reps)])
    lanes = [
        (rows if qz is None else H) * (cols // per if qx is None else 1) * LANES
        for qz, qx in pieces
    ]
    firsts = [c if joined(piece) else 0 for c, piece in zip(counts, pieces)]
    (tables,) = call(
        partial(table_kernel, rows, cols, slots, pieces, starts, counts),
        [((sum(lanes), LANES), BF16)],
        [],
        (e_ids, m_ids),
        us=0.5,
    )
    gc, *sent = call(
        partial(decoder_kernel, rows, cols, slots, pieces),
        [((px, n * slots), BF16)]
        + [((f * px + w // LANES * px, LANES), BF16) for f, w in zip(firsts, lanes)],
        [((2 * px, n * slots), BF16)],
        (
            *(costs, other, grad_hidden, w_t, b_t, w_half, tables),
            *(x.reshape(-1, LANES) for x, piece in zip(slabs, pieces) if joined(piece)),
        ),
        us=3,
    )
    got = sent_to(sent)
    src_halo = [m if h is None else h for h, m in zip(src_halo, got)]
    sg, pw_own = call(
        partial(own_kernel, px, n, slots),
        [((n * px, channels), BF16), ((ext_pad // LANES, n * pitch, LANES), F32)],
        [((n * pitch, channels), F32)],
        (gc, hots, tgt_t),
        us=4,
    )
    halo_pad = -(-(ext - n) // 16) * 16
    (halo_t,) = call(
        partial(halo_kernel, px, [s - n for s in starts], counts),
        [((px, halo_pad, channels), BF16)],
        [((halo_pad * pitch, channels), F32)],
        tuple(src_halo),
        us=1,
    )
    (tg,) = call(
        partial(total_kernel, px, n, slots, firsts, [per if qx is None else H for _, qx in pieces]),
        [((n * px, channels), BF16)],
        [((halo_pad * pitch, LANES), F32), ((n * pitch, channels), F32)],
        (pw_own, src_t, halo_t, *got),
        us=3,
    )
    return sg.reshape(source.shape), tg.reshape(source.shape)


def solution(mesh):
    cells = P(("groups", "strip"), "sub", "rep", None)
    placed = (
        cells,
        cells,
        P(("groups", "strip"), "sub", None),
        P(("groups", "strip"), "sub", None, None),
        P(),
        P(),
        P(),
    )

    return jax.shard_map(
        shards, mesh=mesh, in_specs=placed, out_specs=(cells, cells), check_vma=False
    )
```

```python
from functools import partial
import math

import jax
import jax.numpy as jnp
from jax import lax
from jax.experimental import pallas as pl
from jax.experimental.pallas import tpu as pltpu
from jax.sharding import PartitionSpec as P

H = 3
LANES = 128
NT = (((1,), (1,)), ((), ()))
TN = (((0,), (0,)), ((), ()))
F32 = jnp.float32
BF16 = jnp.bfloat16


def mate(i, q, n):
    j = i + 1 if (i + q) % 2 == 0 else i - 1
    return j if 0 <= j < n else None


def turns(n):
    return [q for q in (0, 1) if any(mate(i, q, n) is not None for i in range(n))]


def swap(x, qz, qx):
    strips, subs = lax.axis_size("strip"), lax.axis_size("sub")
    pairs = []
    for s in range(strips):
        for u in range(subs):
            t = s if qz is None else mate(s, qz, strips)
            v = u if qx is None else mate(u, qx, subs)
            if t is not None and v is not None:
                pairs.append((s * subs + u, t * subs + v))
    return lax.ppermute(x, ("strip", "sub"), pairs)


def plan(rows, cols):
    zs, xs = turns(lax.axis_size("strip")), turns(lax.axis_size("sub"))
    pieces = [(q, None) for q in zs]
    pieces += [(None, r) for r in xs]
    pieces += [(q, r) for q in zs for r in xs]
    base, at = {(None, None): 0}, rows * cols
    for qz, qx in pieces:
        base[qz, qx] = at
        at += (rows if qz is None else H) * (cols if qx is None else H)
    return pieces, base, at


def facing(q, extent, index):
    return jnp.where((index + q) % 2 == 0, extent - H, 0)


def scale_of(n):
    assert n & (n - 1) == 0
    return n.bit_length() - 1


def places(ids, base, rows, cols):
    total_cols = cols * lax.axis_size("sub")
    strip_at, sub_at = lax.axis_index("strip"), lax.axis_index("sub")

    def split(d, extent, index):
        side = jnp.where(d < 0, -1, jnp.where(d >= extent, 1, 0))
        inner = jnp.where(side < 0, d + H, jnp.where(side > 0, d - extent, d))
        ahead = jnp.where(index % 2 == 0, 1, -1)
        turn = jnp.where(side == 0, -1, jnp.where(side == ahead, 0, 1))
        return turn, inner

    row = lax.shift_right_arithmetic(ids, jnp.int32(scale_of(total_cols)))
    col = ids & (total_cols - 1)
    tz, dr = split(row - strip_at * rows, rows, strip_at)
    tx, dc = split(col - sub_at * cols, cols, sub_at)
    where_to = jnp.full(ids.shape, -1, jnp.int32)
    for (qz, qx), start in base.items():
        here = (tz == (-1 if qz is None else qz)) & (tx == (-1 if qx is None else qx))
        width = cols if qx is None else H
        where_to = jnp.where(here, start + dr * width + dc, where_to)
    assert scale_of(rows) + scale_of(cols) >= 0
    return where_to, (row & (rows - 1)) * cols + (col & (cols - 1))


def cuts(pieces, rows, cols, x_ref, out_refs, sems, at):
    strip_at, sub_at = lax.axis_index("strip"), lax.axis_index("sub")
    copies = []
    for i, ((qz, qx), ref) in enumerate(zip(pieces, out_refs)):
        r = pl.ds(0, rows) if qz is None else pl.ds(facing(qz, rows, strip_at), H)
        c = pl.ds(0, cols) if qx is None else pl.ds(facing(qx, cols, sub_at), H)
        copies.append(pltpu.make_async_copy(x_ref.at[r, c], ref, sems.at[at + i]))
    return copies


def loop(count, body, most=4):
    step = max(d for d in range(1, most + 1) if count % d == 0) if count else 1

    def run(i, _):
        body(i)
        return 0

    lax.fori_loop(0, count, run, 0, unroll=step)


def widen(dst, at, src_ref, px, pitch):
    def body(i):
        rows = src_ref[pl.ds(pl.multiple_of(i * px, px), px), :]
        dst[pl.ds((at + i) * pitch, px), :] = rows.astype(F32)

    loop(src_ref.shape[0] // px, body)


def clear(dst, at, end, px, pitch):
    def body(i):
        dst[pl.ds((at + i) * pitch, px), :] = jnp.zeros((px, dst.shape[1]), F32)

    loop(end - at, body)


def hot(row, tile=0):
    e = lax.broadcasted_iota(jnp.int32, (LANES, LANES), 0) + tile * LANES
    return (e == row).astype(F32).astype(BF16)


def pick_hot(e_ref, b, slots, tile):
    group, j = divmod(b, LANES // slots)
    lane = lax.broadcasted_iota(jnp.int32, (1, LANES), 1) // slots
    return hot(jnp.where(lane == j, e_ref[group : group + 1, :], -1), tile)


def cut_kernel(pieces, rows, cols, *refs):
    k = len(pieces)
    x_ref, small, slabs, near, sems = refs[0], refs[1:6], refs[6 : 6 + k], refs[6 + k : -1], refs[-1]
    copies = cuts(pieces, rows, cols, x_ref, slabs, sems, 0)
    for i, (f, v) in enumerate(zip(small, near)):
        copies.append(pltpu.make_async_copy(f, v, sems.at[k + i]))
    for copy in copies:
        copy.start()
    for copy in copies:
        copy.wait()


def slotted(x, out_ref, table, slots):
    n, picks = x.shape
    per = LANES // slots
    table[...] = jnp.full(table.shape, -1, jnp.int32)
    table[:, :picks] = x
    lane = lax.broadcasted_iota(jnp.int32, (n // per, LANES), 1) // slots
    acc = jnp.full((n // per, LANES), -1, jnp.int32)
    for j in range(per):
        rows = table[pl.ds(j, n // per, stride=per), :]
        acc = jnp.where(lane == j, rows if j == 0 else pltpu.roll(rows, j * slots, 1), acc)
    out_ref[...] = acc


def head_kernel(base, pieces, rows, cols, slots, *refs):
    k = len(pieces)
    far, small, rest = refs[:2], refs[2:7], refs[7:]
    src_slabs, outs, rest = rest[:k], rest[k : k + 8], rest[k + 8 :]
    src_t, tgt_t, gh_ref, wt_ref, wh_ref, bt_ref, e_ref, m_ref = outs
    (s32, t32, og, table), near, sems = rest[:4], rest[4:-1], rest[-1]
    src_ref, tgt_ref = near
    og_ref, ids_ref, w_in_ref, b_ref, w_out_ref = small
    fetches = [pltpu.make_async_copy(f, v, sems.at[i]) for i, (f, v) in enumerate(zip(far, near))]
    slabs = cuts(pieces, rows, cols, far[0], src_slabs, sems, 2)
    for copy in fetches + slabs:
        copy.start()
    px, n, _ = src_t.shape
    pitch = px + 1
    e_at, m_at = places(ids_ref[...], base, rows, cols)
    slotted(e_at, e_ref, table, slots)
    slotted(m_at, m_ref, table, slots)
    wt_ref[...] = w_in_ref[...].T
    rep = lax.axis_index("rep")
    wh_ref[...] = w_in_ref[pl.ds(pl.multiple_of(rep * px, px), px), :]
    bt_ref[...] = jnp.broadcast_to(b_ref[...], (LANES, b_ref.shape[1])).T
    picks = og_ref.shape[1]
    og[...] = jnp.zeros_like(og)
    for r in range(rows):
        for pick in range(picks):
            at = r * cols * (slots + 1) + pick
            og[pl.ds(at, cols, stride=slots + 1), :] = og_ref[r, pick].astype(F32)
    per = LANES // slots
    for g in range(n // per):
        block = jnp.concatenate(
            [og[b * (slots + 1) : b * (slots + 1) + slots, :] for b in range(g * per, (g + 1) * per)]
        ).astype(BF16)
        gh_ref[:, g * LANES : (g + 1) * LANES] = lax.dot_general(
            w_out_ref[...], block, NT, preferred_element_type=F32
        )
    for fetch in fetches:
        fetch.wait()
    for dst, src in ((s32, src_ref), (t32, tgt_ref)):

        def body(i, dst=dst, src=src):
            rows_of = src[i // cols, lax.rem(i, cols)]
            dst[pl.ds(i * pitch, px), :] = rows_of.astype(F32)

        loop(n, body, 8)

    def turn(p):
        src_t[p] = s32[pl.ds(p, n, stride=pitch), :].astype(BF16)
        tgt_t[p] = t32[pl.ds(p, n, stride=pitch), :].astype(BF16)

    loop(px, turn, 8)
    for copy in slabs:
        copy.wait()


def corr_kernel(px, n, ext, starts, slots, *refs):
    k = len(starts)
    own_t, src_t, e_ref, tgt_refs = refs[0], refs[1], refs[2], refs[3 : 3 + k]
    costs_ref, tgt_t, hot_ref, t32, corr = refs[3 + k :]
    ext_pad = tgt_t.shape[1]
    tiles = ext_pad // LANES
    pitch = px + 1
    inv_root = 1.0 / math.sqrt(tgt_t.shape[2])
    for start, ref in zip(starts, tgt_refs):
        widen(t32, start - n, ref, px, pitch)
    clear(t32, ext - n, ext_pad - n, px, pitch)

    def per_pixel(p):
        tp = t32[pl.ds(p, ext_pad - n, stride=pitch), :].astype(BF16)
        tp = jnp.concatenate([own_t[p], tp], axis=0)
        tgt_t[p] = tp
        c = lax.dot_general(src_t[p], tp, NT, preferred_element_type=F32) * inv_root
        for t in range(tiles):
            corr[t, pl.ds(p, n, stride=pitch), :] = c[:, t * LANES : (t + 1) * LANES]

    loop(px, per_pixel, px)
    per = LANES // slots
    for g in range(n // per):
        left = []
        for j in range(per):
            b = g * per + j
            for t in range(tiles):
                at = (b * tiles + t) * LANES
                hot_ref[at : at + LANES, :] = pick_hot(e_ref, b, slots, t)
                left.append(corr[t, b * pitch : b * pitch + px, :].astype(BF16))
        high = per * tiles * LANES
        costs_ref[:, g * LANES : (g + 1) * LANES] = jnp.dot(
            jnp.concatenate(left, axis=1),
            hot_ref[g * high : (g + 1) * high, :],
            preferred_element_type=F32,
        ).astype(BF16)


def gelu_slope(x):
    c = math.sqrt(2.0 / math.pi)
    x2 = x * x
    th = jnp.tanh(x * (c + (c * 0.044715) * x2))
    inner = x * (c + (c * 3.0 * 0.044715) * x2)
    return (0.5 + 0.5 * th) * (1.0 + (1.0 - th) * inner)


def decoder_kernel(rows, cols, slots, pieces, *refs):
    mine_ref, other_ref, gh_ref, wt_ref, bt_ref, w_ref, table_ref = refs[:7]
    gc_ref, out_refs, whole = refs[7], refs[8:-1], refs[-1]
    px = mine_ref.shape[0]
    rep = lax.axis_index("rep")
    whole[pl.ds(pl.multiple_of(rep * px, px), px), :] = mine_ref[...]
    whole[pl.ds(pl.multiple_of((1 - rep) * px, px), px), :] = other_ref[...]
    w_half = w_ref[...]
    bias = jnp.concatenate([bt_ref[...]] * (mine_ref.shape[1] // LANES), axis=1)
    pre = jnp.dot(wt_ref[...], whole[...], preferred_element_type=F32) + bias
    grad = (gh_ref[...] * gelu_slope(pre)).astype(BF16)
    gc_ref[...] = jnp.dot(w_half, grad, preferred_element_type=F32).astype(BF16)
    send(rows, cols, slots, pieces, gc_ref, table_ref, out_refs)


def picked(rows, cols, per, piece):
    qz, qx = piece
    strip_at, sub_at = lax.axis_index("strip"), lax.axis_index("sub")
    wide = cols // per
    r0 = 0 if qz is None else facing(qz, rows, strip_at)
    tail = None if qx is None else (sub_at + qx) % 2 == 0
    half = 0 if qx is None else jnp.where(tail, (cols - H) // per, 0)
    shift = 0 if qx is None else jnp.where(tail, (cols - H) % per, 0)
    groups = [
        (r0 + r) * wide + half + h
        for r in range(rows if qz is None else H)
        for h in range(wide if qx is None else 1)
    ]
    return groups, shift


def table_kernel(rows, cols, slots, pieces, starts, counts, e_ref, m_ref, out_ref):
    per = LANES // slots
    lane = lax.broadcasted_iota(jnp.int32, (1, LANES), 1) // slots
    i = 0
    for piece, start, count in zip(pieces, starts, counts):
        groups, shift = picked(rows, cols, per, piece)
        for g in groups:
            e, m = e_ref[pl.ds(g, 1), :], m_ref[pl.ds(g, 1), :]
            here = (e >= start) & (e < start + count)
            out_ref[i * LANES : (i + 1) * LANES, :] = hot(
                jnp.where(here, (lane - shift) * slots + m, -1)
            )
            i += 1


def send(rows, cols, slots, pieces, gc_ref, table_ref, out_refs):
    per = LANES // slots
    i = 0
    for piece, ref in zip(pieces, out_refs):
        groups, _ = picked(rows, cols, per, piece)
        for at, g in enumerate(groups):
            lane = g * LANES
            lane = lane if isinstance(lane, int) else pl.multiple_of(lane, LANES)
            ref[:, at * LANES : (at + 1) * LANES] = lax.dot_general(
                gc_ref[:, pl.ds(lane, LANES)],
                table_ref[i * LANES : (i + 1) * LANES, :],
                NT,
                preferred_element_type=F32,
            ).astype(BF16)
            i += 1


def own_kernel(px, n, slots, gc_ref, hot_ref, tgt_t, sg_ref, pw, s32):
    ext_pad = tgt_t.shape[1]
    pitch = px + 1
    inv_root = 1.0 / math.sqrt(tgt_t.shape[2])
    tiles = ext_pad // LANES
    per = LANES // slots
    high = per * tiles * LANES
    for g in range(n // per):
        w = lax.dot_general(
            gc_ref[:, g * LANES : (g + 1) * LANES],
            hot_ref[g * high : (g + 1) * high, :],
            NT,
            preferred_element_type=F32,
        )
        for j in range(per):
            b = g * per + j
            for t in range(tiles):
                at = (j * tiles + t) * LANES
                pw[t, b * pitch : b * pitch + px, :] = w[:, at : at + LANES]

    def per_pixel(p):
        tp = tgt_t[p]
        sg = jnp.zeros((n, tp.shape[1]), F32)
        for t in range(tiles):
            w = pw[t, pl.ds(p, n, stride=pitch), :].astype(BF16)
            sg += jnp.dot(w, tp[t * LANES : (t + 1) * LANES, :], preferred_element_type=F32)
        s32[pl.ds(p, n, stride=pitch), :] = sg * inv_root

    loop(px, per_pixel, px)

    def narrow(i):
        sg_ref[pl.ds(pl.multiple_of(i * px, px), px), :] = s32[pl.ds(i * pitch, px), :].astype(BF16)

    loop(n, narrow)


def halo_kernel(px, starts, *refs):
    k = len(starts)
    src_refs, out, s32 = refs[:k], refs[k], refs[k + 1]
    pitch = px + 1
    for start, ref in zip(starts, src_refs):
        widen(s32, start, ref, px, pitch)
    last = starts[-1] + src_refs[-1].shape[0] // px
    clear(s32, last, out.shape[1], px, pitch)

    def turn(p):
        out[p] = s32[pl.ds(p, out.shape[1], stride=pitch), :].astype(BF16)

    loop(px, turn, 8)


def total_kernel(px, n, slots, widths, pw_own, src_t, halo_t, *refs):
    k = len(widths)
    msg_refs, tg_ref, pw, t32 = refs[:k], refs[k], refs[k + 1], refs[k + 2]
    pitch = px + 1
    inv_root = 1.0 / math.sqrt(src_t.shape[2])
    at = 0
    for width, ref in zip(widths, msg_refs):
        for g in range(ref.shape[1] // LANES):
            block = ref[:, g * LANES : (g + 1) * LANES].astype(F32)
            for j in range(width):
                turned = block if j == 0 else pltpu.roll(block, LANES - j * slots, 1)
                pw[at * pitch : at * pitch + px, :] = turned
                at += 1
    clear(pw, at, halo_t.shape[1], px, pitch)

    def per_pixel(p):
        near = pw_own[0, pl.ds(p, n, stride=pitch), :]
        far = pw[pl.ds(p, halo_t.shape[1], stride=pitch), :]
        w = jnp.concatenate([near, far], axis=0)[:, :n].astype(BF16)
        s = jnp.concatenate([src_t[p], halo_t[p]], axis=0)
        tg = lax.dot_general(w, s, TN, preferred_element_type=F32)
        t32[pl.ds(p, n, stride=pitch), :] = tg * inv_root

    loop(px, per_pixel, px // 2)

    def narrow(i):
        tg_ref[pl.ds(pl.multiple_of(i * px, px), px), :] = t32[pl.ds(i * pitch, px), :].astype(BF16)

    loop(n, narrow)


VM = pl.BlockSpec(memory_space=pltpu.VMEM)
HB = pl.BlockSpec(memory_space=pltpu.HBM)


def call(kernel, outs, scratch, args, us=2.0, far=0, sems=0, limit=24, near=False):
    return pl.pallas_call(
        kernel,
        out_shape=[pltpu.VMEM(s, d) if near else jax.ShapeDtypeStruct(s, d) for s, d in outs],
        in_specs=[HB] * far + [VM] * (len(args) - far),
        out_specs=[VM] * len(outs),
        scratch_shapes=[pltpu.VMEM(s, d) for s, d in scratch]
        + ([pltpu.VMEM(x.shape, x.dtype) for x in args[:far]] if far else [])
        + ([pltpu.SemaphoreType.DMA((sems,))] if far else []),
        compiler_params=pltpu.CompilerParams(vmem_limit_bytes=limit * 2**20),
        cost_estimate=pl.CostEstimate(
            flops=0, bytes_accessed=int(us * 3 * 10**6), transcendentals=0
        ),
    )(*args)


def shards(source, target, target_ids, out_grad, w_in, b_in, w_out):
    rows, cols, px, channels = source.shape
    picks = target_ids.shape[2]
    n = rows * cols
    pitch = px + 1
    slots = 1 << (picks - 1).bit_length()
    per = LANES // slots
    groups = n // per
    assert n <= slots and cols % per == 0 and H <= per and groups * per == n
    pieces, base, ext = plan(rows, cols)
    ext_pad = -(-ext // LANES) * LANES

    shapes = [
        (rows if qz is None else H, cols if qx is None else H, px, channels) for qz, qx in pieces
    ]

    hidden = w_in.shape[1]
    outs = [(s, BF16) for s in shapes] + [
        ((px, n, channels), BF16),
        ((px, n, channels), BF16),
        ((hidden, n * slots), F32),
        ((hidden, 2 * px), BF16),
        ((px, hidden), BF16),
        ((hidden, LANES), F32),
        ((groups, LANES), jnp.int32),
        ((groups, LANES), jnp.int32),
    ]
    args = (
        source,
        target,
        jnp.swapaxes(out_grad, 1, 2),
        target_ids.reshape(n, picks),
        w_in,
        b_in.reshape(1, hidden),
        w_out,
    )
    args = tuple(pltpu.with_memory_space_constraint(a, pltpu.HBM) for a in args)
    k = len(pieces)
    small = args[2:]
    cut_t = pl.pallas_call(
        partial(cut_kernel, pieces, rows, cols),
        name="cut",
        out_shape=[jax.ShapeDtypeStruct(s, BF16) for s in shapes]
        + [jax.ShapeDtypeStruct(x.shape, x.dtype) for x in small],
        in_specs=[HB] * (1 + len(small)),
        out_specs=[VM] * (k + len(small)),
        scratch_shapes=[pltpu.SemaphoreType.DMA((k + len(small),))],
        compiler_params=pltpu.CompilerParams(vmem_limit_bytes=6 * 2**20),
    )(args[1], *small)
    made = call(
        partial(head_kernel, base, pieces, rows, cols, slots),
        outs,
        [((n * pitch, channels), F32)] * 2
        + [((n * (slots + 1), out_grad.shape[3]), F32), ((n, LANES), jnp.int32)],
        (*args[:2], *cut_t[k:]),
        far=2,
        sems=2 + k,
    )
    src_t, own_t, grad_hidden, w_t, w_half, b_t, e_ids, m_ids = made[k:]

    def halo_of(slabs):
        got = []
        for x, (qz, qx) in zip(slabs, pieces):
            got.append(swap(x, qz, qx).reshape(-1, channels))
        return got

    tgt_halo = halo_of(cut_t[:k])
    src_halo = halo_of(made[:k])
    starts = [base[q] for q in pieces]
    counts = [h.shape[0] // px for h in tgt_halo]
    costs, tgt_t, hots = call(
        partial(corr_kernel, px, n, ext, starts, slots),
        [
            ((px, n * slots), BF16),
            ((px, ext_pad, channels), BF16),
            ((n * ext_pad, LANES), BF16),
        ],
        [
            (((ext_pad - n) * pitch, channels), F32),
            ((ext_pad // LANES, n * pitch, LANES), F32),
        ],
        (own_t, src_t, e_ids, *tgt_halo),
        us=3,
    )
    reps = lax.axis_size("rep")
    other = lax.ppermute(costs, "rep", [(i, reps - 1 - i) for i in range(reps)])
    lanes = [
        (rows if qz is None else H) * (cols // per if qx is None else 1) * LANES
        for qz, qx in pieces
    ]
    (tables,) = call(
        partial(table_kernel, rows, cols, slots, pieces, starts, counts),
        [((sum(lanes), LANES), BF16)],
        [],
        (e_ids, m_ids),
        us=0.5,
    )
    gc, *sent = call(
        partial(decoder_kernel, rows, cols, slots, pieces),
        [((px, n * slots), BF16)] + [((px, w), BF16) for w in lanes],
        [((2 * px, n * slots), BF16)],
        (costs, other, grad_hidden, w_t, b_t, w_half, tables),
        us=3,
    )
    got = []
    for x, (qz, qx) in zip(sent, pieces):
        got.append(swap(x, qz, qx))
    sg, pw_own = call(
        partial(own_kernel, px, n, slots),
        [((n * px, channels), BF16), ((ext_pad // LANES, n * pitch, LANES), F32)],
        [((n * pitch, channels), F32)],
        (gc, hots, tgt_t),
        us=4,
    )
    halo_pad = -(-(ext - n) // 16) * 16
    (halo_t,) = call(
        partial(halo_kernel, px, [s - n for s in starts]),
        [((px, halo_pad, channels), BF16)],
        [((halo_pad * pitch, channels), F32)],
        tuple(src_halo),
        us=1,
    )
    (tg,) = call(
        partial(total_kernel, px, n, slots, [per if qx is None else H for _, qx in pieces]),
        [((n * px, channels), BF16)],
        [((halo_pad * pitch, LANES), F32), ((n * pitch, channels), F32)],
        (pw_own, src_t, halo_t, *got),
        us=3,
    )
    return sg.reshape(source.shape), tg.reshape(source.shape)


def solution(mesh):
    cells = P(("groups", "strip"), "sub", "rep", None)
    placed = (
        cells,
        cells,
        P(("groups", "strip"), "sub", None),
        P(("groups", "strip"), "sub", None, None),
        P(),
        P(),
        P(),
    )

    return jax.shard_map(
        shards, mesh=mesh, in_specs=placed, out_specs=(cells, cells), check_vma=False
    )
```

```python
from functools import partial
import math

import jax
import jax.numpy as jnp
from jax import lax
from jax.experimental import pallas as pl
from jax.experimental.pallas import tpu as pltpu
from jax.sharding import PartitionSpec as P

H = 3
LANES = 128
NT = (((1,), (1,)), ((), ()))
TN = (((0,), (0,)), ((), ()))
F32 = jnp.float32
BF16 = jnp.bfloat16


def mate(i, q, n):
    j = i + 1 if (i + q) % 2 == 0 else i - 1
    return j if 0 <= j < n else None


def turns(n):
    return [q for q in (0, 1) if any(mate(i, q, n) is not None for i in range(n))]


def swap(x, qz, qx):
    strips, subs = lax.axis_size("strip"), lax.axis_size("sub")
    pairs = []
    for s in range(strips):
        for u in range(subs):
            t = s if qz is None else mate(s, qz, strips)
            v = u if qx is None else mate(u, qx, subs)
            if t is not None and v is not None:
                pairs.append((s * subs + u, t * subs + v))
    return lax.ppermute(x, ("strip", "sub"), pairs)


def plan(rows, cols):
    zs, xs = turns(lax.axis_size("strip")), turns(lax.axis_size("sub"))
    pieces = [(q, None) for q in zs]
    pieces += [(None, r) for r in xs]
    pieces += [(q, r) for q in zs for r in xs]
    base, at = {(None, None): 0}, rows * cols
    for qz, qx in pieces:
        base[qz, qx] = at
        at += (rows if qz is None else H) * (cols if qx is None else H)
    return pieces, base, at


def facing(q, extent, index):
    return jnp.where((index + q) % 2 == 0, extent - H, 0)


def scale_of(n):
    assert n & (n - 1) == 0
    return n.bit_length() - 1


def places(ids, base, rows, cols):
    total_cols = cols * lax.axis_size("sub")
    strip_at, sub_at = lax.axis_index("strip"), lax.axis_index("sub")

    def split(d, extent, index):
        side = jnp.where(d < 0, -1, jnp.where(d >= extent, 1, 0))
        inner = jnp.where(side < 0, d + H, jnp.where(side > 0, d - extent, d))
        ahead = jnp.where(index % 2 == 0, 1, -1)
        turn = jnp.where(side == 0, -1, jnp.where(side == ahead, 0, 1))
        return turn, inner

    row = lax.shift_right_arithmetic(ids, jnp.int32(scale_of(total_cols)))
    col = ids & (total_cols - 1)
    tz, dr = split(row - strip_at * rows, rows, strip_at)
    tx, dc = split(col - sub_at * cols, cols, sub_at)
    where_to = jnp.full(ids.shape, -1, jnp.int32)
    for (qz, qx), start in base.items():
        here = (tz == (-1 if qz is None else qz)) & (tx == (-1 if qx is None else qx))
        width = cols if qx is None else H
        where_to = jnp.where(here, start + dr * width + dc, where_to)
    assert scale_of(rows) + scale_of(cols) >= 0
    return where_to, (row & (rows - 1)) * cols + (col & (cols - 1))


def cuts(pieces, rows, cols, x_ref, out_refs, sems, at):
    strip_at, sub_at = lax.axis_index("strip"), lax.axis_index("sub")
    copies = []
    for i, ((qz, qx), ref) in enumerate(zip(pieces, out_refs)):
        r = pl.ds(0, rows) if qz is None else pl.ds(facing(qz, rows, strip_at), H)
        c = pl.ds(0, cols) if qx is None else pl.ds(facing(qx, cols, sub_at), H)
        copies.append(pltpu.make_async_copy(x_ref.at[r, c], ref, sems.at[at + i]))
    return copies


def loop(count, body, most=4):
    step = max(d for d in range(1, most + 1) if count % d == 0) if count else 1

    def run(i, _):
        body(i)
        return 0

    lax.fori_loop(0, count, run, 0, unroll=step)


def widen(dst, at, src_ref, px, pitch):
    def body(i):
        rows = src_ref[pl.ds(pl.multiple_of(i * px, px), px), :]
        dst[pl.ds((at + i) * pitch, px), :] = rows.astype(F32)

    loop(src_ref.shape[0] // px, body)


def clear(dst, at, end, px, pitch):
    def body(i):
        dst[pl.ds((at + i) * pitch, px), :] = jnp.zeros((px, dst.shape[1]), F32)

    loop(end - at, body)


def hot(row, tile=0):
    e = lax.broadcasted_iota(jnp.int32, (LANES, LANES), 0) + tile * LANES
    return (e == row).astype(F32).astype(BF16)


def pick_hot(e_ref, b, slots, tile):
    group, j = divmod(b, LANES // slots)
    lane = lax.broadcasted_iota(jnp.int32, (1, LANES), 1) // slots
    return hot(jnp.where(lane == j, e_ref[group : group + 1, :], -1), tile)


def cut_kernel(pieces, rows, cols, x_ref, *refs):
    copies = cuts(pieces, rows, cols, x_ref, refs[:-1], refs[-1], 0)
    for copy in copies:
        copy.start()
    for copy in copies:
        copy.wait()


def slotted(x, out_ref, table, slots):
    n, picks = x.shape
    per = LANES // slots
    table[...] = jnp.full(table.shape, -1, jnp.int32)
    table[:, :picks] = x
    lane = lax.broadcasted_iota(jnp.int32, (n // per, LANES), 1) // slots
    acc = jnp.full((n // per, LANES), -1, jnp.int32)
    for j in range(per):
        rows = table[pl.ds(j, n // per, stride=per), :]
        acc = jnp.where(lane == j, rows if j == 0 else pltpu.roll(rows, j * slots, 1), acc)
    out_ref[...] = acc


def head_kernel(base, pieces, rows, cols, slots, *refs):
    k = len(pieces)
    far, rest = refs[:7], refs[7:]
    src_slabs, outs, rest = rest[:k], rest[k : k + 8], rest[k + 8 :]
    src_t, tgt_t, gh_ref, wt_ref, wh_ref, bt_ref, e_ref, m_ref = outs
    (s32, t32, og, table), near, sems = rest[:4], rest[4:-1], rest[-1]
    src_ref, tgt_ref, og_ref, ids_ref, w_in_ref, b_ref, w_out_ref = near
    fetches = [pltpu.make_async_copy(f, v, sems.at[i]) for i, (f, v) in enumerate(zip(far, near))]
    slabs = cuts(pieces, rows, cols, src_ref, src_slabs, sems, 7)
    for copy in fetches[2:] + fetches[:2]:
        copy.start()
    px, n, _ = src_t.shape
    pitch = px + 1
    for fetch in fetches[2:]:
        fetch.wait()
    e_at, m_at = places(ids_ref[...], base, rows, cols)
    slotted(e_at, e_ref, table, slots)
    slotted(m_at, m_ref, table, slots)
    wt_ref[...] = w_in_ref[...].T
    rep = lax.axis_index("rep")
    wh_ref[...] = w_in_ref[pl.ds(pl.multiple_of(rep * px, px), px), :]
    bt_ref[...] = jnp.broadcast_to(b_ref[...], (LANES, b_ref.shape[1])).T
    picks = og_ref.shape[1]
    og[...] = jnp.zeros_like(og)
    for r in range(rows):
        for pick in range(picks):
            at = r * cols * (slots + 1) + pick
            og[pl.ds(at, cols, stride=slots + 1), :] = og_ref[r, pick].astype(F32)
    per = LANES // slots
    for g in range(n // per):
        block = jnp.concatenate(
            [og[b * (slots + 1) : b * (slots + 1) + slots, :] for b in range(g * per, (g + 1) * per)]
        ).astype(BF16)
        gh_ref[:, g * LANES : (g + 1) * LANES] = lax.dot_general(
            w_out_ref[...], block, NT, preferred_element_type=F32
        )
    for fetch in fetches[:2]:
        fetch.wait()
    for copy in slabs:
        copy.start()
    for dst, src in ((s32, src_ref), (t32, tgt_ref)):

        def body(i, dst=dst, src=src):
            rows_of = src[i // cols, lax.rem(i, cols)]
            dst[pl.ds(i * pitch, px), :] = rows_of.astype(F32)

        loop(n, body, 8)

    def turn(p):
        src_t[p] = s32[pl.ds(p, n, stride=pitch), :].astype(BF16)
        tgt_t[p] = t32[pl.ds(p, n, stride=pitch), :].astype(BF16)

    loop(px, turn, 8)
    for copy in slabs:
        copy.wait()


def corr_kernel(px, n, ext, starts, slots, *refs):
    k = len(starts)
    own_t, src_t, e_ref, tgt_refs = refs[0], refs[1], refs[2], refs[3 : 3 + k]
    costs_ref, tgt_t, hot_ref, t32, corr = refs[3 + k :]
    ext_pad = tgt_t.shape[1]
    tiles = ext_pad // LANES
    pitch = px + 1
    inv_root = 1.0 / math.sqrt(tgt_t.shape[2])
    for start, ref in zip(starts, tgt_refs):
        widen(t32, start - n, ref, px, pitch)
    clear(t32, ext - n, ext_pad - n, px, pitch)

    def per_pixel(p):
        tp = t32[pl.ds(p, ext_pad - n, stride=pitch), :].astype(BF16)
        tp = jnp.concatenate([own_t[p], tp], axis=0)
        tgt_t[p] = tp
        c = lax.dot_general(src_t[p], tp, NT, preferred_element_type=F32) * inv_root
        for t in range(tiles):
            corr[t, pl.ds(p, n, stride=pitch), :] = c[:, t * LANES : (t + 1) * LANES]

    loop(px, per_pixel, px)
    per = LANES // slots
    for g in range(n // per):
        left = []
        for j in range(per):
            b = g * per + j
            for t in range(tiles):
                at = (b * tiles + t) * LANES
                hot_ref[at : at + LANES, :] = pick_hot(e_ref, b, slots, t)
                left.append(corr[t, b * pitch : b * pitch + px, :].astype(BF16))
        high = per * tiles * LANES
        costs_ref[:, g * LANES : (g + 1) * LANES] = jnp.dot(
            jnp.concatenate(left, axis=1),
            hot_ref[g * high : (g + 1) * high, :],
            preferred_element_type=F32,
        ).astype(BF16)


def gelu_slope(x):
    c = math.sqrt(2.0 / math.pi)
    x2 = x * x
    th = jnp.tanh(x * (c + (c * 0.044715) * x2))
    inner = x * (c + (c * 3.0 * 0.044715) * x2)
    return (0.5 + 0.5 * th) * (1.0 + (1.0 - th) * inner)


def decoder_kernel(rows, cols, slots, pieces, *refs):
    mine_ref, other_ref, gh_ref, wt_ref, bt_ref, w_ref, table_ref = refs[:7]
    gc_ref, out_refs, whole = refs[7], refs[8:-1], refs[-1]
    px = mine_ref.shape[0]
    rep = lax.axis_index("rep")
    whole[pl.ds(pl.multiple_of(rep * px, px), px), :] = mine_ref[...]
    whole[pl.ds(pl.multiple_of((1 - rep) * px, px), px), :] = other_ref[...]
    w_half = w_ref[...]
    bias = jnp.concatenate([bt_ref[...]] * (mine_ref.shape[1] // LANES), axis=1)
    pre = jnp.dot(wt_ref[...], whole[...], preferred_element_type=F32) + bias
    grad = (gh_ref[...] * gelu_slope(pre)).astype(BF16)
    gc_ref[...] = jnp.dot(w_half, grad, preferred_element_type=F32).astype(BF16)
    send(rows, cols, slots, pieces, gc_ref, table_ref, out_refs)


def picked(rows, cols, per, piece):
    qz, qx = piece
    strip_at, sub_at = lax.axis_index("strip"), lax.axis_index("sub")
    wide = cols // per
    r0 = 0 if qz is None else facing(qz, rows, strip_at)
    tail = None if qx is None else (sub_at + qx) % 2 == 0
    half = 0 if qx is None else jnp.where(tail, (cols - H) // per, 0)
    shift = 0 if qx is None else jnp.where(tail, (cols - H) % per, 0)
    groups = [
        (r0 + r) * wide + half + h
        for r in range(rows if qz is None else H)
        for h in range(wide if qx is None else 1)
    ]
    return groups, shift


def table_kernel(rows, cols, slots, pieces, starts, counts, e_ref, m_ref, out_ref):
    per = LANES // slots
    lane = lax.broadcasted_iota(jnp.int32, (1, LANES), 1) // slots
    i = 0
    for piece, start, count in zip(pieces, starts, counts):
        groups, shift = picked(rows, cols, per, piece)
        for g in groups:
            e, m = e_ref[pl.ds(g, 1), :], m_ref[pl.ds(g, 1), :]
            here = (e >= start) & (e < start + count)
            out_ref[i * LANES : (i + 1) * LANES, :] = hot(
                jnp.where(here, (lane - shift) * slots + m, -1)
            )
            i += 1


def send(rows, cols, slots, pieces, gc_ref, table_ref, out_refs):
    per = LANES // slots
    i = 0
    for piece, ref in zip(pieces, out_refs):
        groups, _ = picked(rows, cols, per, piece)
        for at, g in enumerate(groups):
            lane = g * LANES
            lane = lane if isinstance(lane, int) else pl.multiple_of(lane, LANES)
            ref[:, at * LANES : (at + 1) * LANES] = lax.dot_general(
                gc_ref[:, pl.ds(lane, LANES)],
                table_ref[i * LANES : (i + 1) * LANES, :],
                NT,
                preferred_element_type=F32,
            ).astype(BF16)
            i += 1


def own_kernel(px, n, slots, gc_ref, hot_ref, tgt_t, sg_ref, pw, s32):
    ext_pad = tgt_t.shape[1]
    pitch = px + 1
    inv_root = 1.0 / math.sqrt(tgt_t.shape[2])
    tiles = ext_pad // LANES
    per = LANES // slots
    high = per * tiles * LANES
    for g in range(n // per):
        w = lax.dot_general(
            gc_ref[:, g * LANES : (g + 1) * LANES],
            hot_ref[g * high : (g + 1) * high, :],
            NT,
            preferred_element_type=F32,
        )
        for j in range(per):
            b = g * per + j
            for t in range(tiles):
                at = (j * tiles + t) * LANES
                pw[t, b * pitch : b * pitch + px, :] = w[:, at : at + LANES]

    def per_pixel(p):
        tp = tgt_t[p]
        sg = jnp.zeros((n, tp.shape[1]), F32)
        for t in range(tiles):
            w = pw[t, pl.ds(p, n, stride=pitch), :].astype(BF16)
            sg += jnp.dot(w, tp[t * LANES : (t + 1) * LANES, :], preferred_element_type=F32)
        s32[pl.ds(p, n, stride=pitch), :] = sg * inv_root

    loop(px, per_pixel, px)

    def narrow(i):
        sg_ref[pl.ds(pl.multiple_of(i * px, px), px), :] = s32[pl.ds(i * pitch, px), :].astype(BF16)

    loop(n, narrow)


def halo_kernel(px, starts, *refs):
    k = len(starts)
    src_refs, out, s32 = refs[:k], refs[k], refs[k + 1]
    pitch = px + 1
    for start, ref in zip(starts, src_refs):
        widen(s32, start, ref, px, pitch)
    last = starts[-1] + src_refs[-1].shape[0] // px
    clear(s32, last, out.shape[1], px, pitch)

    def turn(p):
        out[p] = s32[pl.ds(p, out.shape[1], stride=pitch), :].astype(BF16)

    loop(px, turn, 8)


def total_kernel(px, n, slots, widths, pw_own, src_t, halo_t, *refs):
    k = len(widths)
    msg_refs, tg_ref, pw, t32 = refs[:k], refs[k], refs[k + 1], refs[k + 2]
    pitch = px + 1
    inv_root = 1.0 / math.sqrt(src_t.shape[2])
    at = 0
    for width, ref in zip(widths, msg_refs):
        for g in range(ref.shape[1] // LANES):
            block = ref[:, g * LANES : (g + 1) * LANES].astype(F32)
            for j in range(width):
                turned = block if j == 0 else pltpu.roll(block, LANES - j * slots, 1)
                pw[at * pitch : at * pitch + px, :] = turned
                at += 1
    clear(pw, at, halo_t.shape[1], px, pitch)

    def per_pixel(p):
        near = pw_own[0, pl.ds(p, n, stride=pitch), :]
        far = pw[pl.ds(p, halo_t.shape[1], stride=pitch), :]
        w = jnp.concatenate([near, far], axis=0)[:, :n].astype(BF16)
        s = jnp.concatenate([src_t[p], halo_t[p]], axis=0)
        tg = lax.dot_general(w, s, TN, preferred_element_type=F32)
        t32[pl.ds(p, n, stride=pitch), :] = tg * inv_root

    loop(px, per_pixel, px // 2)

    def narrow(i):
        tg_ref[pl.ds(pl.multiple_of(i * px, px), px), :] = t32[pl.ds(i * pitch, px), :].astype(BF16)

    loop(n, narrow)


VM = pl.BlockSpec(memory_space=pltpu.VMEM)
HB = pl.BlockSpec(memory_space=pltpu.HBM)


def call(kernel, outs, scratch, args, us=2.0, far=0, sems=0, limit=24, near=False):
    return pl.pallas_call(
        kernel,
        out_shape=[pltpu.VMEM(s, d) if near else jax.ShapeDtypeStruct(s, d) for s, d in outs],
        in_specs=[HB] * far + [VM] * (len(args) - far),
        out_specs=[VM] * len(outs),
        scratch_shapes=[pltpu.VMEM(s, d) for s, d in scratch]
        + ([pltpu.VMEM(x.shape, x.dtype) for x in args[:far]] if far else [])
        + ([pltpu.SemaphoreType.DMA((sems,))] if far else []),
        compiler_params=pltpu.CompilerParams(vmem_limit_bytes=limit * 2**20),
        cost_estimate=pl.CostEstimate(
            flops=0, bytes_accessed=int(us * 3 * 10**6), transcendentals=0
        ),
    )(*args)


def shards(source, target, target_ids, out_grad, w_in, b_in, w_out):
    rows, cols, px, channels = source.shape
    picks = target_ids.shape[2]
    n = rows * cols
    pitch = px + 1
    slots = 1 << (picks - 1).bit_length()
    per = LANES // slots
    groups = n // per
    assert n <= slots and cols % per == 0 and H <= per and groups * per == n
    pieces, base, ext = plan(rows, cols)
    ext_pad = -(-ext // LANES) * LANES

    shapes = [
        (rows if qz is None else H, cols if qx is None else H, px, channels) for qz, qx in pieces
    ]

    hidden = w_in.shape[1]
    outs = [(s, BF16) for s in shapes] + [
        ((px, n, channels), BF16),
        ((px, n, channels), BF16),
        ((hidden, n * slots), F32),
        ((hidden, 2 * px), BF16),
        ((px, hidden), BF16),
        ((hidden, LANES), F32),
        ((groups, LANES), jnp.int32),
        ((groups, LANES), jnp.int32),
    ]
    args = (
        source,
        target,
        jnp.swapaxes(out_grad, 1, 2),
        target_ids.reshape(n, picks),
        w_in,
        b_in.reshape(1, hidden),
        w_out,
    )
    args = tuple(pltpu.with_memory_space_constraint(a, pltpu.HBM) for a in args)
    made = call(
        partial(head_kernel, base, pieces, rows, cols, slots),
        outs,
        [((n * pitch, channels), F32)] * 2
        + [((n * (slots + 1), out_grad.shape[3]), F32), ((n, LANES), jnp.int32)],
        args,
        far=len(args),
        sems=len(args) + len(pieces),
        limit=24,
    )
    k = len(pieces)
    src_t, own_t, grad_hidden, w_t, w_half, b_t, e_ids, m_ids = made[k:]
    cut_t = pl.pallas_call(
        partial(cut_kernel, pieces, rows, cols),
        name="cut",
        out_shape=[jax.ShapeDtypeStruct(s, BF16) for s in shapes],
        in_specs=[HB],
        out_specs=[VM] * k,
        scratch_shapes=[pltpu.SemaphoreType.DMA((k,))],
        compiler_params=pltpu.CompilerParams(vmem_limit_bytes=4 * 2**20),
    )(args[1])

    def halo_of(slabs):
        got = []
        for x, (qz, qx) in zip(slabs, pieces):
            got.append(swap(x, qz, qx).reshape(-1, channels))
        return got

    tgt_halo = halo_of(cut_t)
    src_halo = halo_of(made[:k])
    starts = [base[q] for q in pieces]
    counts = [h.shape[0] // px for h in tgt_halo]
    costs, tgt_t, hots = call(
        partial(corr_kernel, px, n, ext, starts, slots),
        [
            ((px, n * slots), BF16),
            ((px, ext_pad, channels), BF16),
            ((n * ext_pad, LANES), BF16),
        ],
        [
            (((ext_pad - n) * pitch, channels), F32),
            ((ext_pad // LANES, n * pitch, LANES), F32),
        ],
        (own_t, src_t, e_ids, *tgt_halo),
        us=3,
    )
    reps = lax.axis_size("rep")
    other = lax.ppermute(costs, "rep", [(i, reps - 1 - i) for i in range(reps)])
    lanes = [
        (rows if qz is None else H) * (cols // per if qx is None else 1) * LANES
        for qz, qx in pieces
    ]
    (tables,) = call(
        partial(table_kernel, rows, cols, slots, pieces, starts, counts),
        [((sum(lanes), LANES), BF16)],
        [],
        (e_ids, m_ids),
        us=0.5,
    )
    gc, *sent = call(
        partial(decoder_kernel, rows, cols, slots, pieces),
        [((px, n * slots), BF16)] + [((px, w), BF16) for w in lanes],
        [((2 * px, n * slots), BF16)],
        (costs, other, grad_hidden, w_t, b_t, w_half, tables),
        us=3,
    )
    got = []
    for x, (qz, qx) in zip(sent, pieces):
        got.append(swap(x, qz, qx))
    sg, pw_own = call(
        partial(own_kernel, px, n, slots),
        [((n * px, channels), BF16), ((ext_pad // LANES, n * pitch, LANES), F32)],
        [((n * pitch, channels), F32)],
        (gc, hots, tgt_t),
        us=4,
    )
    halo_pad = -(-(ext - n) // 16) * 16
    (halo_t,) = call(
        partial(halo_kernel, px, [s - n for s in starts]),
        [((px, halo_pad, channels), BF16)],
        [((halo_pad * pitch, channels), F32)],
        tuple(src_halo),
        us=1,
    )
    (tg,) = call(
        partial(total_kernel, px, n, slots, [per if qx is None else H for _, qx in pieces]),
        [((n * px, channels), BF16)],
        [((halo_pad * pitch, LANES), F32), ((n * pitch, channels), F32)],
        (pw_own, src_t, halo_t, *got),
        us=3,
    )
    return sg.reshape(source.shape), tg.reshape(source.shape)


def solution(mesh):
    cells = P(("groups", "strip"), "sub", "rep", None)
    placed = (
        cells,
        cells,
        P(("groups", "strip"), "sub", None),
        P(("groups", "strip"), "sub", None, None),
        P(),
        P(),
        P(),
    )

    return jax.shard_map(
        shards, mesh=mesh, in_specs=placed, out_specs=(cells, cells), check_vma=False
    )
```

```python
from functools import partial
import math

import jax
import jax.numpy as jnp
from jax import lax
from jax.experimental import pallas as pl
from jax.experimental.pallas import tpu as pltpu
from jax.sharding import PartitionSpec as P

H = 3
LANES = 128
NT = (((1,), (1,)), ((), ()))
TN = (((0,), (0,)), ((), ()))
F32 = jnp.float32
BF16 = jnp.bfloat16


def mate(i, q, n):
    j = i + 1 if (i + q) % 2 == 0 else i - 1
    return j if 0 <= j < n else None


def turns(n):
    return [q for q in (0, 1) if any(mate(i, q, n) is not None for i in range(n))]


def swap(x, qz, qx):
    strips, subs = lax.axis_size("strip"), lax.axis_size("sub")
    pairs = []
    for s in range(strips):
        for u in range(subs):
            t = s if qz is None else mate(s, qz, strips)
            v = u if qx is None else mate(u, qx, subs)
            if t is not None and v is not None:
                pairs.append((s * subs + u, t * subs + v))
    return lax.ppermute(x, ("strip", "sub"), pairs)


def plan(rows, cols):
    zs, xs = turns(lax.axis_size("strip")), turns(lax.axis_size("sub"))
    pieces = [(q, None) for q in zs]
    pieces += [(None, r) for r in xs]
    pieces += [(q, r) for q in zs for r in xs]
    base, at = {(None, None): 0}, rows * cols
    for qz, qx in pieces:
        base[qz, qx] = at
        at += (rows if qz is None else H) * (cols if qx is None else H)
    return pieces, base, at


def facing(q, extent, index):
    return jnp.where((index + q) % 2 == 0, extent - H, 0)


def scale_of(n):
    assert n & (n - 1) == 0
    return n.bit_length() - 1


def places(ids, base, rows, cols):
    total_cols = cols * lax.axis_size("sub")
    strip_at, sub_at = lax.axis_index("strip"), lax.axis_index("sub")

    def split(d, extent, index):
        side = jnp.where(d < 0, -1, jnp.where(d >= extent, 1, 0))
        inner = jnp.where(side < 0, d + H, jnp.where(side > 0, d - extent, d))
        ahead = jnp.where(index % 2 == 0, 1, -1)
        turn = jnp.where(side == 0, -1, jnp.where(side == ahead, 0, 1))
        return turn, inner

    row = lax.shift_right_arithmetic(ids, jnp.int32(scale_of(total_cols)))
    col = ids & (total_cols - 1)
    tz, dr = split(row - strip_at * rows, rows, strip_at)
    tx, dc = split(col - sub_at * cols, cols, sub_at)
    where_to = jnp.full(ids.shape, -1, jnp.int32)
    for (qz, qx), start in base.items():
        here = (tz == (-1 if qz is None else qz)) & (tx == (-1 if qx is None else qx))
        width = cols if qx is None else H
        where_to = jnp.where(here, start + dr * width + dc, where_to)
    assert scale_of(rows) + scale_of(cols) >= 0
    return where_to, (row & (rows - 1)) * cols + (col & (cols - 1))


def cuts(pieces, rows, cols, x_ref, out_refs, sems, at):
    strip_at, sub_at = lax.axis_index("strip"), lax.axis_index("sub")
    copies = []
    for i, ((qz, qx), ref) in enumerate(zip(pieces, out_refs)):
        r = pl.ds(0, rows) if qz is None else pl.ds(facing(qz, rows, strip_at), H)
        c = pl.ds(0, cols) if qx is None else pl.ds(facing(qx, cols, sub_at), H)
        copies.append(pltpu.make_async_copy(x_ref.at[r, c], ref, sems.at[at + i]))
    return copies


def loop(count, body, most=12):
    step = max(d for d in range(1, most + 1) if count % d == 0) if count else 1

    def run(i, _):
        body(i)
        return 0

    lax.fori_loop(0, count, run, 0, unroll=step)


def widen(dst, at, src_ref, px, pitch):
    def body(i):
        rows = src_ref[pl.ds(pl.multiple_of(i * px, px), px), :]
        dst[pl.ds((at + i) * pitch, px), :] = rows.astype(F32)

    loop(src_ref.shape[0] // px, body)


def clear(dst, at, end, px, pitch):
    def body(i):
        dst[pl.ds((at + i) * pitch, px), :] = jnp.zeros((px, dst.shape[1]), F32)

    loop(end - at, body)


def hot(row, tile=0):
    e = lax.broadcasted_iota(jnp.int32, (LANES, LANES), 0) + tile * LANES
    return (e == row).astype(F32).astype(BF16)


def pick_hot(e_ref, b, slots, tile):
    group, j = divmod(b, LANES // slots)
    lane = lax.broadcasted_iota(jnp.int32, (1, LANES), 1) // slots
    return hot(jnp.where(lane == j, e_ref[group : group + 1, :], -1), tile)


def cut_kernel(pieces, rows, cols, x_ref, *refs):
    copies = cuts(pieces, rows, cols, x_ref, refs[:-1], refs[-1], 0)
    for copy in copies:
        copy.start()
    for copy in copies:
        copy.wait()


def slotted(x, out_ref, table, slots):
    n, picks = x.shape
    per = LANES // slots
    table[...] = jnp.full(table.shape, -1, jnp.int32)
    table[:, :picks] = x
    lane = lax.broadcasted_iota(jnp.int32, (n // per, LANES), 1) // slots
    acc = jnp.full((n // per, LANES), -1, jnp.int32)
    for j in range(per):
        rows = table[pl.ds(j, n // per, stride=per), :]
        acc = jnp.where(lane == j, rows if j == 0 else pltpu.roll(rows, j * slots, 1), acc)
    out_ref[...] = acc


def head_kernel(base, pieces, rows, cols, slots, *refs):
    k = len(pieces)
    far, rest = refs[:7], refs[7:]
    src_slabs, outs, rest = rest[:k], rest[k : k + 8], rest[k + 8 :]
    src_t, tgt_t, gh_ref, wt_ref, wh_ref, bt_ref, e_ref, m_ref = outs
    (s32, t32, og, table), near, sems = rest[:4], rest[4:-1], rest[-1]
    src_ref, tgt_ref, og_ref, ids_ref, w_in_ref, b_ref, w_out_ref = near
    fetches = [pltpu.make_async_copy(f, v, sems.at[i]) for i, (f, v) in enumerate(zip(far, near))]
    slabs = cuts(pieces, rows, cols, far[0], src_slabs, sems, 7)
    for copy in fetches[2:] + fetches[:2] + slabs:
        copy.start()
    px, n, _ = src_t.shape
    pitch = px + 1
    for fetch in fetches[2:]:
        fetch.wait()
    e_at, m_at = places(ids_ref[...], base, rows, cols)
    slotted(e_at, e_ref, table, slots)
    slotted(m_at, m_ref, table, slots)
    wt_ref[...] = w_in_ref[...].T
    rep = lax.axis_index("rep")
    wh_ref[...] = w_in_ref[pl.ds(pl.multiple_of(rep * px, px), px), :]
    bt_ref[...] = jnp.broadcast_to(b_ref[...], (LANES, b_ref.shape[1])).T
    picks = og_ref.shape[1]
    og[...] = jnp.zeros_like(og)
    for r in range(rows):
        for pick in range(picks):
            at = r * cols * (slots + 1) + pick
            og[pl.ds(at, cols, stride=slots + 1), :] = og_ref[r, pick].astype(F32)
    per = LANES // slots
    for g in range(n // per):
        block = jnp.concatenate(
            [og[b * (slots + 1) : b * (slots + 1) + slots, :] for b in range(g * per, (g + 1) * per)]
        ).astype(BF16)
        gh_ref[:, g * LANES : (g + 1) * LANES] = lax.dot_general(
            w_out_ref[...], block, NT, preferred_element_type=F32
        )
    for fetch in fetches[:2]:
        fetch.wait()
    for dst, src in ((s32, src_ref), (t32, tgt_ref)):

        def body(i, dst=dst, src=src):
            rows_of = src[i // cols, lax.rem(i, cols)]
            dst[pl.ds(i * pitch, px), :] = rows_of.astype(F32)

        loop(n, body, n)

    def turn(p):
        src_t[p] = s32[pl.ds(p, n, stride=pitch), :].astype(BF16)
        tgt_t[p] = t32[pl.ds(p, n, stride=pitch), :].astype(BF16)

    loop(px, turn, px)
    for copy in slabs:
        copy.wait()


def corr_kernel(px, n, ext, starts, slots, *refs):
    k = len(starts)
    own_t, src_t, e_ref, tgt_refs = refs[0], refs[1], refs[2], refs[3 : 3 + k]
    costs_ref, tgt_t, hot_ref, t32, corr = refs[3 + k :]
    ext_pad = tgt_t.shape[1]
    tiles = ext_pad // LANES
    pitch = px + 1
    inv_root = 1.0 / math.sqrt(tgt_t.shape[2])
    for start, ref in zip(starts, tgt_refs):
        widen(t32, start - n, ref, px, pitch)
    clear(t32, ext - n, ext_pad - n, px, pitch)

    def per_pixel(p):
        tp = t32[pl.ds(p, ext_pad - n, stride=pitch), :].astype(BF16)
        tp = jnp.concatenate([own_t[p], tp], axis=0)
        tgt_t[p] = tp
        c = lax.dot_general(src_t[p], tp, NT, preferred_element_type=F32) * inv_root
        for t in range(tiles):
            corr[t, pl.ds(p, n, stride=pitch), :] = c[:, t * LANES : (t + 1) * LANES]

    loop(px, per_pixel, px)
    per = LANES // slots
    for g in range(n // per):
        left = []
        for j in range(per):
            b = g * per + j
            for t in range(tiles):
                at = (b * tiles + t) * LANES
                hot_ref[at : at + LANES, :] = pick_hot(e_ref, b, slots, t)
                left.append(corr[t, b * pitch : b * pitch + px, :].astype(BF16))
        high = per * tiles * LANES
        costs_ref[:, g * LANES : (g + 1) * LANES] = jnp.dot(
            jnp.concatenate(left, axis=1),
            hot_ref[g * high : (g + 1) * high, :],
            preferred_element_type=F32,
        ).astype(BF16)


def gelu_slope(x):
    c = math.sqrt(2.0 / math.pi)
    x2 = x * x
    th = jnp.tanh(x * (c + (c * 0.044715) * x2))
    inner = x * (c + (c * 3.0 * 0.044715) * x2)
    return (0.5 + 0.5 * th) * (1.0 + (1.0 - th) * inner)


def decoder_kernel(rows, cols, slots, pieces, *refs):
    mine_ref, other_ref, gh_ref, wt_ref, bt_ref, w_ref, table_ref = refs[:7]
    gc_ref, out_refs, whole = refs[7], refs[8:-1], refs[-1]
    px = mine_ref.shape[0]
    rep = lax.axis_index("rep")
    whole[pl.ds(pl.multiple_of(rep * px, px), px), :] = mine_ref[...]
    whole[pl.ds(pl.multiple_of((1 - rep) * px, px), px), :] = other_ref[...]
    w_half = w_ref[...]
    bias = jnp.concatenate([bt_ref[...]] * (mine_ref.shape[1] // LANES), axis=1)
    pre = jnp.dot(wt_ref[...], whole[...], preferred_element_type=F32) + bias
    grad = (gh_ref[...] * gelu_slope(pre)).astype(BF16)
    gc_ref[...] = jnp.dot(w_half, grad, preferred_element_type=F32).astype(BF16)
    send(rows, cols, slots, pieces, gc_ref, table_ref, out_refs)


def picked(rows, cols, per, piece):
    qz, qx = piece
    strip_at, sub_at = lax.axis_index("strip"), lax.axis_index("sub")
    wide = cols // per
    r0 = 0 if qz is None else facing(qz, rows, strip_at)
    tail = None if qx is None else (sub_at + qx) % 2 == 0
    half = 0 if qx is None else jnp.where(tail, (cols - H) // per, 0)
    shift = 0 if qx is None else jnp.where(tail, (cols - H) % per, 0)
    groups = [
        (r0 + r) * wide + half + h
        for r in range(rows if qz is None else H)
        for h in range(wide if qx is None else 1)
    ]
    return groups, shift


def table_kernel(rows, cols, slots, pieces, starts, counts, e_ref, m_ref, out_ref):
    per = LANES // slots
    lane = lax.broadcasted_iota(jnp.int32, (1, LANES), 1) // slots
    i = 0
    for piece, start, count in zip(pieces, starts, counts):
        groups, shift = picked(rows, cols, per, piece)
        for g in groups:
            e, m = e_ref[pl.ds(g, 1), :], m_ref[pl.ds(g, 1), :]
            here = (e >= start) & (e < start + count)
            out_ref[i * LANES : (i + 1) * LANES, :] = hot(
                jnp.where(here, (lane - shift) * slots + m, -1)
            )
            i += 1


def send(rows, cols, slots, pieces, gc_ref, table_ref, out_refs):
    per = LANES // slots
    i = 0
    for piece, ref in zip(pieces, out_refs):
        groups, _ = picked(rows, cols, per, piece)
        for at, g in enumerate(groups):
            lane = g * LANES
            lane = lane if isinstance(lane, int) else pl.multiple_of(lane, LANES)
            ref[:, at * LANES : (at + 1) * LANES] = lax.dot_general(
                gc_ref[:, pl.ds(lane, LANES)],
                table_ref[i * LANES : (i + 1) * LANES, :],
                NT,
                preferred_element_type=F32,
            ).astype(BF16)
            i += 1


def own_kernel(px, n, slots, gc_ref, hot_ref, tgt_t, sg_ref, pw, s32):
    ext_pad = tgt_t.shape[1]
    pitch = px + 1
    inv_root = 1.0 / math.sqrt(tgt_t.shape[2])
    tiles = ext_pad // LANES
    per = LANES // slots
    high = per * tiles * LANES
    for g in range(n // per):
        w = lax.dot_general(
            gc_ref[:, g * LANES : (g + 1) * LANES],
            hot_ref[g * high : (g + 1) * high, :],
            NT,
            preferred_element_type=F32,
        )
        for j in range(per):
            b = g * per + j
            for t in range(tiles):
                at = (j * tiles + t) * LANES
                pw[t, b * pitch : b * pitch + px, :] = w[:, at : at + LANES]

    def per_pixel(p):
        tp = tgt_t[p]
        sg = jnp.zeros((n, tp.shape[1]), F32)
        for t in range(tiles):
            w = pw[t, pl.ds(p, n, stride=pitch), :].astype(BF16)
            sg += jnp.dot(w, tp[t * LANES : (t + 1) * LANES, :], preferred_element_type=F32)
        s32[pl.ds(p, n, stride=pitch), :] = sg * inv_root

    loop(px, per_pixel, px)

    def narrow(i):
        sg_ref[pl.ds(pl.multiple_of(i * px, px), px), :] = s32[pl.ds(i * pitch, px), :].astype(BF16)

    loop(n, narrow, n)


def halo_kernel(px, starts, *refs):
    k = len(starts)
    src_refs, out, s32 = refs[:k], refs[k], refs[k + 1]
    pitch = px + 1
    for start, ref in zip(starts, src_refs):
        widen(s32, start, ref, px, pitch)
    last = starts[-1] + src_refs[-1].shape[0] // px
    clear(s32, last, out.shape[1], px, pitch)

    def turn(p):
        out[p] = s32[pl.ds(p, out.shape[1], stride=pitch), :].astype(BF16)

    loop(px, turn, px)


def total_kernel(px, n, slots, widths, pw_own, src_t, halo_t, *refs):
    k = len(widths)
    msg_refs, tg_ref, pw, t32 = refs[:k], refs[k], refs[k + 1], refs[k + 2]
    pitch = px + 1
    inv_root = 1.0 / math.sqrt(src_t.shape[2])
    at = 0
    for width, ref in zip(widths, msg_refs):
        for g in range(ref.shape[1] // LANES):
            block = ref[:, g * LANES : (g + 1) * LANES].astype(F32)
            for j in range(width):
                turned = block if j == 0 else pltpu.roll(block, LANES - j * slots, 1)
                pw[at * pitch : at * pitch + px, :] = turned
                at += 1
    clear(pw, at, halo_t.shape[1], px, pitch)

    def per_pixel(p):
        near = pw_own[0, pl.ds(p, n, stride=pitch), :]
        far = pw[pl.ds(p, halo_t.shape[1], stride=pitch), :]
        w = jnp.concatenate([near, far], axis=0)[:, :n].astype(BF16)
        s = jnp.concatenate([src_t[p], halo_t[p]], axis=0)
        tg = lax.dot_general(w, s, TN, preferred_element_type=F32)
        t32[pl.ds(p, n, stride=pitch), :] = tg * inv_root

    loop(px, per_pixel, px // 2)

    def narrow(i):
        tg_ref[pl.ds(pl.multiple_of(i * px, px), px), :] = t32[pl.ds(i * pitch, px), :].astype(BF16)

    loop(n, narrow, n)


VM = pl.BlockSpec(memory_space=pltpu.VMEM)
HB = pl.BlockSpec(memory_space=pltpu.HBM)


def call(kernel, outs, scratch, args, us=2.0, far=0, sems=0, limit=24, near=False):
    return pl.pallas_call(
        kernel,
        out_shape=[pltpu.VMEM(s, d) if near else jax.ShapeDtypeStruct(s, d) for s, d in outs],
        in_specs=[HB] * far + [VM] * (len(args) - far),
        out_specs=[VM] * len(outs),
        scratch_shapes=[pltpu.VMEM(s, d) for s, d in scratch]
        + ([pltpu.VMEM(x.shape, x.dtype) for x in args[:far]] if far else [])
        + ([pltpu.SemaphoreType.DMA((sems,))] if far else []),
        compiler_params=pltpu.CompilerParams(vmem_limit_bytes=limit * 2**20),
        cost_estimate=pl.CostEstimate(
            flops=0, bytes_accessed=int(us * 3 * 10**6), transcendentals=0
        ),
    )(*args)


def shards(source, target, target_ids, out_grad, w_in, b_in, w_out):
    rows, cols, px, channels = source.shape
    picks = target_ids.shape[2]
    n = rows * cols
    pitch = px + 1
    slots = 1 << (picks - 1).bit_length()
    per = LANES // slots
    groups = n // per
    assert n <= slots and cols % per == 0 and H <= per and groups * per == n
    pieces, base, ext = plan(rows, cols)
    ext_pad = -(-ext // LANES) * LANES

    shapes = [
        (rows if qz is None else H, cols if qx is None else H, px, channels) for qz, qx in pieces
    ]

    hidden = w_in.shape[1]
    outs = [(s, BF16) for s in shapes] + [
        ((px, n, channels), BF16),
        ((px, n, channels), BF16),
        ((hidden, n * slots), F32),
        ((hidden, 2 * px), BF16),
        ((px, hidden), BF16),
        ((hidden, LANES), F32),
        ((groups, LANES), jnp.int32),
        ((groups, LANES), jnp.int32),
    ]
    args = (
        source,
        target,
        jnp.swapaxes(out_grad, 1, 2),
        target_ids.reshape(n, picks),
        w_in,
        b_in.reshape(1, hidden),
        w_out,
    )
    args = tuple(pltpu.with_memory_space_constraint(a, pltpu.HBM) for a in args)
    made = call(
        partial(head_kernel, base, pieces, rows, cols, slots),
        outs,
        [((n * pitch, channels), F32)] * 2
        + [((n * (slots + 1), out_grad.shape[3]), F32), ((n, LANES), jnp.int32)],
        args,
        far=len(args),
        sems=len(args) + len(pieces),
        limit=24,
    )
    k = len(pieces)
    src_t, own_t, grad_hidden, w_t, w_half, b_t, e_ids, m_ids = made[k:]
    cut_t = pl.pallas_call(
        partial(cut_kernel, pieces, rows, cols),
        name="cut",
        out_shape=[jax.ShapeDtypeStruct(s, BF16) for s in shapes],
        in_specs=[HB],
        out_specs=[VM] * k,
        scratch_shapes=[pltpu.SemaphoreType.DMA((k,))],
        compiler_params=pltpu.CompilerParams(vmem_limit_bytes=4 * 2**20),
    )(args[1])

    def halo_of(slabs):
        got = []
        for x, (qz, qx) in zip(slabs, pieces):
            got.append(swap(x, qz, qx).reshape(-1, channels))
        return got

    tgt_halo = halo_of(cut_t)
    src_halo = halo_of(made[:k])
    starts = [base[q] for q in pieces]
    counts = [h.shape[0] // px for h in tgt_halo]
    costs, tgt_t, hots = call(
        partial(corr_kernel, px, n, ext, starts, slots),
        [
            ((px, n * slots), BF16),
            ((px, ext_pad, channels), BF16),
            ((n * ext_pad, LANES), BF16),
        ],
        [
            (((ext_pad - n) * pitch, channels), F32),
            ((ext_pad // LANES, n * pitch, LANES), F32),
        ],
        (own_t, src_t, e_ids, *tgt_halo),
        us=3,
    )
    reps = lax.axis_size("rep")
    other = lax.ppermute(costs, "rep", [(i, reps - 1 - i) for i in range(reps)])
    lanes = [
        (rows if qz is None else H) * (cols // per if qx is None else 1) * LANES
        for qz, qx in pieces
    ]
    (tables,) = call(
        partial(table_kernel, rows, cols, slots, pieces, starts, counts),
        [((sum(lanes), LANES), BF16)],
        [],
        (e_ids, m_ids),
        us=0.5,
    )
    gc, *sent = call(
        partial(decoder_kernel, rows, cols, slots, pieces),
        [((px, n * slots), BF16)] + [((px, w), BF16) for w in lanes],
        [((2 * px, n * slots), BF16)],
        (costs, other, grad_hidden, w_t, b_t, w_half, tables),
        us=3,
    )
    got = []
    for x, (qz, qx) in zip(sent, pieces):
        got.append(swap(x, qz, qx))
    sg, pw_own = call(
        partial(own_kernel, px, n, slots),
        [((n * px, channels), BF16), ((ext_pad // LANES, n * pitch, LANES), F32)],
        [((n * pitch, channels), F32)],
        (gc, hots, tgt_t),
        us=4,
    )
    halo_pad = -(-(ext - n) // 16) * 16
    (halo_t,) = call(
        partial(halo_kernel, px, [s - n for s in starts]),
        [((px, halo_pad, channels), BF16)],
        [((halo_pad * pitch, channels), F32)],
        tuple(src_halo),
        us=1,
    )
    (tg,) = call(
        partial(total_kernel, px, n, slots, [per if qx is None else H for _, qx in pieces]),
        [((n * px, channels), BF16)],
        [((halo_pad * pitch, LANES), F32), ((n * pitch, channels), F32)],
        (pw_own, src_t, halo_t, *got),
        us=3,
    )
    return sg.reshape(source.shape), tg.reshape(source.shape)


def solution(mesh):
    cells = P(("groups", "strip"), "sub", "rep", None)
    placed = (
        cells,
        cells,
        P(("groups", "strip"), "sub", None),
        P(("groups", "strip"), "sub", None, None),
        P(),
        P(),
        P(),
    )

    return jax.shard_map(
        shards, mesh=mesh, in_specs=placed, out_specs=(cells, cells), check_vma=False
    )
```
